32 devices in a mesh: aux: 4 (over x, core), orb: 8 (over z, y).
Axes of the slice: x: 2, y: 2, z: 4, core: 2. Of those that a mesh axis runs over, the one named last changes fastest.
Arguments:
- raw_ints: bfloat16 [4, 8, 1024, 1536], P(None, 'orb', 'aux'), may hold values from -0.625 to 0.625
- fit_inverse: bfloat16 [32, 1024, 1024], P(('aux', 'orb')), may hold values from -0.1875 to 0.1875
- pair_orbs: int32 [512, 2], P(('aux', 'orb')), may hold values from 0 to 7, all different within a row; in each aligned block of 16 rows (0 to 15, 16 to 31, ...) at most 8 rows name the same one
- pno_coef: bfloat16 [512, 2, 32, 1536], P(('aux', 'orb')), may hold values from -0.15625 to 0.15625
- pno_energy: float32 [512, 2, 32], P(('aux', 'orb')), may hold values from 0.3 to 6
- occ_energy: float32 [32], replicated, may hold values from -1.5 to -0.3
- fit_offset: int32 [32], replicated, may hold values from 0 to 255
Outputs:
- amplitude: float32 [512, 1024], P(('aux', 'orb'))
- energy: float32 [512], P(('aux', 'orb'))
The draws below stay inside these ranges and needn't reach their ends.
Inputs may be any that keep to these rules, and one draw needn't show every extreme that they name: `pair_orbs`: each entry is an orbital's index within the pair's region; the two entries of a row differ; among the rows of one device no orbital is named more than 8 times.
All inputs are finite; a program needn't handle non-finite values.
Results may differ from the reference program's by a relative error of at most 0.0057.
Values may be sent and summed in bfloat16 or wider, within the bound.
No kernel may reach another device: no remote copies, remote signals or barrier semaphores. Data moves between devices by JAX's collectives and lax.ppermute only.
A program may use at most 64 MiB of HBM per device.

```python
import math
import jax
import jax.numpy as jnp
import numpy as np
from jax import lax

FIT = 1024
DOM = 1536
NPNO = 32
PAIR_DEV = 16
NREG = 4
NPER = 8
NORB = 32
NPAIR = 512
CAP = 8


def place_ends(drawn, rng, least, top_value):
    extent = drawn.shape
    place = [jax.random.randint(jax.random.fold_in(rng, axis), (), 0, extent[axis]) for axis in range(len(extent))]
    drawn = drawn.at[tuple(place)].set(least)
    longest = extent.index(max(extent))
    place[longest] = (place[longest] + 1) % extent[longest]
    return drawn.at[tuple(place)].set(top_value)


def block_scale(rng, dims, shards, smallest, largest):
    def one(axis_at, blocks):
        draws = jax.random.uniform(jax.random.fold_in(jax.random.fold_in(rng, 6), axis_at), (blocks,), jnp.float32, smallest / len(shards), largest / len(shards))
        return jnp.repeat(jnp.exp(draws), dims[axis_at] // blocks).reshape((-1,) + (1,) * (len(dims) - axis_at - 1))

    level = one(*shards[0])
    for cut in shards[1:]:
        level = level * one(*cut)
    return level


def deal_out(rng, own, number, rows, number_of, top, reach, skew):
    sequence = jax.random.permutation(rng, number_of)
    packed, usual = shares(number_of, rows * top, reach, skew, True), shares(number_of, rows * top, reach, skew, False)
    places = jnp.arange(number_of)

    def named(tallies, rotation):
        used = int((tallies > 0).sum())
        fixed = max(1, used // 4)
        passed = fixed + (places - fixed + rotation * (used - fixed)) % max(1, number_of - fixed)
        return jnp.zeros((number_of,), jnp.int32).at[sequence[jnp.where(places < fixed, places, passed)]].set(jnp.asarray(tallies, jnp.int32))

    tallies = jnp.where(number % 4 == 0, named(packed, number // 4), named(usual, number - number // 4 - 1))
    mixed = jax.random.permutation(jax.random.fold_in(own, 3), number_of)
    giver, taker = mixed[0:number_of // 2 * 2:2], mixed[1:number_of // 2 * 2:2]
    room = jnp.minimum(tallies[giver] - 1, reach - tallies[taker]) // 2
    room = jnp.where((giver == sequence[0]) | (taker == sequence[0]) | (tallies[taker] == 0), 0, jnp.maximum(room, 0))
    passed = jax.random.randint(jax.random.fold_in(own, 4), (number_of // 2,), 0, 1 << 20) % (room + 1)
    tallies = tallies.at[giver].add(-passed).at[taker].add(passed)
    items = jnp.searchsorted(jnp.cumsum(tallies), jnp.arange(rows * top), side="right").astype(jnp.int32)
    grid = items.reshape(top, rows).T
    grid = grid[jax.random.permutation(jax.random.fold_in(own, 1), rows)]
    rotation = jax.random.randint(jax.random.fold_in(own, 2), (rows, 1), 0, top)
    return jnp.take_along_axis(grid, (jnp.arange(top)[None, :] + rotation) % top, axis=1)


def shares(number_of, total, limit, slope, full):
    weights = [(1 << 20) // math.isqrt(rank ** slope) + 1 for rank in range(1, number_of + 1)]
    largest = limit if full else min(limit, max(-(-total // number_of), total * weights[0] // sum(weights)))
    least = 1 if total - largest >= number_of - 1 else 0
    given, spare = [largest] + [least] * (number_of - 1), total - largest - least * (number_of - 1)
    while spare > 0:
        candidates = [i for i in range(1, number_of) if given[i] < largest] or [i for i in range(1, number_of) if given[i] < limit]
        mass, left = sum([weights[i] for i in candidates]), spare
        for i in candidates:
            more = min(limit - given[i], max(1, left * weights[i] // mass), spare)
            given[i] = given[i] + more
            spare = spare - more
    return np.array(given)


def scatter_about(key, dims, scale, bound, cuts=(), kind=jnp.bfloat16):
    array = scale * jax.random.normal(key, dims, jnp.float32)
    if cuts:
        array = array * block_scale(key, dims, cuts, -0.22, 0.18)
    return jnp.clip(array, -bound, bound).astype(kind)


def setup_inputs(seed: int = 0) -> dict:
    arg_keys = jax.random.split(jax.random.key(seed), 8)
    raw_ints = scatter_about(arg_keys[0], (NREG, NPER, FIT, DOM), 0.1, 0.625, ((1, 8), (2, 4)))
    fit_inverse = scatter_about(arg_keys[1], (NORB, FIT, FIT), FIT ** -0.5, 0.1875, ((0, 32),))
    pair_orbs_keys = jax.random.split(jax.random.fold_in(arg_keys[2], 1), NPAIR // PAIR_DEV)
    pair_orbs_turns = jax.random.permutation(jax.random.fold_in(arg_keys[2], 3), NPAIR // PAIR_DEV)
    pair_orbs = jax.vmap(lambda own, number: deal_out(jax.random.fold_in(arg_keys[2], 2), own, number, PAIR_DEV, NPER, 2, CAP, 2))(pair_orbs_keys, pair_orbs_turns).reshape((NPAIR, 2))
    pno_coef = scatter_about(arg_keys[3], (NPAIR, 2, NPNO, DOM), DOM ** -0.5, 0.15625, ((0, 32),))
    pno_energy = jnp.clip(jnp.exp(math.log(6.0) - 2.9957322 * jax.random.uniform(arg_keys[4], (NPAIR, 2, NPNO), jnp.float32) ** block_scale(arg_keys[4], (NPAIR, 2, NPNO), ((0, 32),), -0.2, 0.2)), 0.3, 6.0)
    occ_energy = jnp.clip(jax.random.uniform(arg_keys[5], (NORB,), jnp.float32, -1.5, -0.3), -1.5, -0.3)
    fit_offset = place_ends(jax.random.randint(arg_keys[6], (NORB,), 0, FIT // 4), jax.random.fold_in(arg_keys[6], 1), 0, (FIT // 4) - 1).astype(jnp.int32)
    return {"raw_ints": raw_ints, "fit_inverse": fit_inverse, "pair_orbs": pair_orbs, "pno_coef": pno_coef, "pno_energy": pno_energy, "occ_energy": occ_energy, "fit_offset": fit_offset}


def fit_block(operands):
    inverse, raw_block = operands
    return jnp.dot(inverse, raw_block, preferred_element_type=jnp.float32).astype(jnp.bfloat16)


def reference(raw_ints, fit_inverse, pair_orbs, pno_coef, pno_energy, occ_energy, fit_offset):
    blocks = raw_ints.reshape(NORB, FIT, DOM)
    fitted = lax.map(fit_block, (fit_inverse, blocks))
    region = jnp.arange(NPAIR, dtype=jnp.int32) // (PAIR_DEV * NPER)
    global_orb = (region[:, None] * NPER + pair_orbs).astype(jnp.int32)
    margin = FIT // 4
    contract = (((1,), (1,)), ((), ()))

    def one_pair(operands):
        orbitals, coef_pair, levels = operands
        first_side = lax.dot_general(coef_pair[0], fitted[orbitals[0]], contract, preferred_element_type=jnp.float32).astype(jnp.bfloat16)
        second = lax.dot_general(coef_pair[1], fitted[orbitals[1]], contract, preferred_element_type=jnp.float32).astype(jnp.bfloat16)
        shift_rows = (fit_offset[orbitals[0]] - fit_offset[orbitals[1]]).astype(jnp.int32)
        padded = jnp.pad(second, ((0, 0), (margin, margin)))
        aligned = lax.dynamic_slice_in_dim(padded, (margin + shift_rows).astype(jnp.int32), FIT, 1)
        coupling = lax.dot_general(first_side, aligned, contract, preferred_element_type=jnp.float32)
        denominator = levels[0][:, None] + levels[1][None, :] - occ_energy[orbitals[0]] - occ_energy[orbitals[1]]
        amplitude = -coupling / denominator
        energy = jnp.sum(coupling * (2.0 * amplitude - amplitude.T))
        return amplitude.reshape(NPNO * NPNO), energy

    amplitude, energy = lax.map(one_pair, (global_orb, pno_coef, pno_energy))
    return amplitude, energy
```

```python
import functools

import jax
import jax.numpy as jnp
from jax import lax
from jax.experimental import pallas as pl
from jax.experimental.pallas import tpu as pltpu
from jax.sharding import PartitionSpec as P

CHUNKS = 4


def pack_kernel(group, capacity, orbs, place, coef, *refs):
    outs, (position, held, count, holder, load_sem, store_sem) = refs[:-6], refs[-6:]
    side_count = held.shape[0]
    load = pltpu.make_async_copy(coef, held, load_sem)
    load.start()
    orb_count = 2 * group

    def clear(i, carry):
        holder[i] = 0
        return carry

    def clear_count(i, carry):
        count[i] = 0
        return carry

    lax.fori_loop(0, orb_count * capacity, clear, 0)
    lax.fori_loop(0, orb_count, clear_count, 0)

    def assign(s, carry):
        orb = orbs[s]
        at = count[orb]
        holder[orb * capacity + at] = s
        position[s] = at
        count[orb] = at + 1
        return carry

    lax.fori_loop(0, side_count, assign, 0)
    load.wait()
    me = place[1]
    for mask in range(group):
        for kind in range(2):
            orb = me ^ (mask + kind * group)

            def send(k, carry, orb=orb, out=outs[2 * mask + kind]):
                s = holder[orb * capacity + k]
                pltpu.make_async_copy(held.at[s], out.at[k], store_sem.at[2 * mask + kind]).start()
                return carry

            lax.fori_loop(0, capacity, send, 0)
    for at, out in enumerate(outs):
        pltpu.make_async_copy(held.at[pl.ds(0, capacity)], out, store_sem.at[at]).wait()


def pack(orbs, place, coef, group, capacity):
    side_count, pno_count, dom_count = coef.shape
    smem = pl.BlockSpec(memory_space=pltpu.SMEM)
    anywhere = pl.BlockSpec(memory_space=pl.ANY)
    block = jax.ShapeDtypeStruct((capacity, pno_count, dom_count), coef.dtype)
    return pl.pallas_call(
        functools.partial(pack_kernel, group, capacity),
        out_shape=(block,) * (2 * group) + (jax.ShapeDtypeStruct((side_count,), jnp.int32),),
        in_specs=[smem, smem, anywhere],
        out_specs=(anywhere,) * (2 * group) + (smem,),
        scratch_shapes=[
            pltpu.VMEM(coef.shape, coef.dtype),
            pltpu.SMEM((2 * group,), jnp.int32),
            pltpu.SMEM((2 * group * capacity,), jnp.int32),
            pltpu.SemaphoreType.DMA,
            pltpu.SemaphoreType.DMA((2 * group,)),
        ],
        cost_estimate=pl.CostEstimate(
            flops=0, transcendentals=0, bytes_accessed=6 * side_count * pno_count * dom_count
        ),
        name="pack",
    )(orbs, place, coef)


def couple_kernel(group, chunks, orbs, position, place, offset, *refs):
    near, far = refs[:group], refs[group : group + group * chunks]
    coupling, sides, sem = refs[group + group * chunks :]
    side_count, _, fit_rows = sides.shape
    wide = fit_rows // chunks
    me = place[1]

    def fetch(s, carry):
        orb, at = orbs[s], position[s]
        differs = orb ^ me
        for mask in range(group):

            @pl.when(differs == mask)
            def _(mask=mask):
                pltpu.make_async_copy(near[mask].at[at], sides.at[s], sem.at[s]).start()

            @pl.when(differs == mask + group)
            def _(mask=mask):
                for c in range(chunks):
                    pltpu.make_async_copy(
                        far[mask * chunks + c].at[at],
                        sides.at[s, :, pl.ds(c * wide, wide)],
                        sem.at[s],
                    ).start()

        return carry

    lax.fori_loop(0, side_count, fetch, 0)
    first_orb = place[0] * (2 * group)

    def one_pair(n, carry):
        for k in range(2):
            pltpu.make_async_copy(sides.at[2 * n + k], sides.at[2 * n + k], sem.at[2 * n + k]).wait()
        shift = offset[first_orb + orbs[2 * n]] - offset[first_orb + orbs[2 * n + 1]]
        second = sides[2 * n + 1].astype(jnp.float32)
        turned = pltpu.roll(second, lax.rem(fit_rows - shift, fit_rows), 1)
        at = lax.broadcasted_iota(jnp.int32, turned.shape, 1) + shift
        aligned = jnp.where((at >= 0) & (at < fit_rows), turned, 0.0).astype(sides.dtype)
        coupling[n] = lax.dot_general(
            sides[2 * n], aligned, (((1,), (1,)), ((), ())), preferred_element_type=jnp.float32
        )
        return carry

    lax.fori_loop(0, side_count // 2, one_pair, 0, unroll=2)


def couple(orbs, position, place, offset, near, far, chunks):
    group = len(near)
    side_count = orbs.shape[0]
    _, pno_count, fit_rows = near[0].shape
    smem = pl.BlockSpec(memory_space=pltpu.SMEM)
    anywhere = pl.BlockSpec(memory_space=pl.ANY)
    return pl.pallas_call(
        functools.partial(couple_kernel, group, chunks),
        out_shape=jax.ShapeDtypeStruct((side_count // 2, pno_count, pno_count), jnp.float32),
        in_specs=[smem] * 4 + [anywhere] * (len(near) + len(far)),
        out_specs=pl.BlockSpec(memory_space=pltpu.VMEM),
        scratch_shapes=[
            pltpu.VMEM((side_count, pno_count, fit_rows), near[0].dtype),
            pltpu.SemaphoreType.DMA((side_count,)),
        ],
        name="couple",
    )(orbs, position, place, offset, *near, *far)


def project(blocks, rows):
    count, pno_count, dom_count = blocks.shape
    flat = lax.dot_general(
        blocks.reshape(count * pno_count, dom_count),
        rows,
        (((1,), (1,)), ((), ())),
        preferred_element_type=jnp.float32,
    )
    return flat.astype(jnp.bfloat16).reshape(count, pno_count, rows.shape[0])


def on_device(raw_ints, fit_inverse, pair_orbs, pno_coef, pno_energy, occ_energy, fit_offset):
    orb_count = lax.axis_size("orb")
    region = lax.axis_index("aux")
    group = orb_count // 2
    pair_count = pair_orbs.shape[0]
    pno_count, dom_count = pno_coef.shape[2:]
    side_count = 2 * pair_count
    capacity = max(2, 4 * pair_count // orb_count)

    def across(array, mask):
        return lax.ppermute(array, "orb", [(i, i ^ mask) for i in range(orb_count)])

    orbs = pair_orbs.reshape(side_count)
    place = jnp.stack([region, lax.axis_index("orb")]).astype(jnp.int32)
    gathered = lax.all_to_all(raw_ints, "aux", split_axis=0, concat_axis=2, tiled=True)[0, 0]
    *blocks, position = pack(
        orbs, place, pno_coef.reshape(side_count, pno_count, dom_count), group, capacity
    )
    near_blocks = [blocks[0]] + [across(blocks[2 * m], m) for m in range(1, group)]
    far_blocks = [blocks[1]] + [across(blocks[2 * m + 1], m) for m in range(1, group)]
    fitted = jnp.dot(fit_inverse[0], gathered, preferred_element_type=jnp.float32).astype(
        jnp.bfloat16
    )
    wide = fitted.shape[0] // CHUNKS
    mirrored = [across(fitted[c * wide : (c + 1) * wide], group) for c in range(CHUNKS)]
    near = [project(block, fitted) for block in near_blocks]
    near = [near[0]] + [across(near[m], m) for m in range(1, group)]
    far = [[None] * CHUNKS for _ in range(group)]
    for c in range(CHUNKS):
        for m in range(group):
            part = project(far_blocks[m], mirrored[c])
            far[m][c] = part if m == 0 else across(part, m)
    coupling = couple(
        orbs, position, place, fit_offset, near, [part for row in far for part in row], CHUNKS
    )
    orb_total = occ_energy.shape[0]
    global_orb = region * orb_count + pair_orbs
    selector = global_orb[:, :, None] == jnp.arange(orb_total, dtype=jnp.int32)[None, None, :]
    occupied = jnp.sum(jnp.where(selector, occ_energy[None, None, :], 0.0), axis=2)
    denominator = (
        pno_energy[:, 0, :, None]
        + pno_energy[:, 1, None, :]
        - occupied[:, 0, None, None]
        - occupied[:, 1, None, None]
    )
    amplitude = -coupling / denominator
    energy = jnp.sum(coupling * (2.0 * amplitude - jnp.swapaxes(amplitude, 1, 2)), axis=(1, 2))
    return (amplitude.reshape(pair_count, pno_count * pno_count), energy)


def solution(mesh):
    return jax.shard_map(
        on_device,
        mesh=mesh,
        in_specs=(
            P(None, "orb", "aux", None),
            P(("aux", "orb"), None, None),
            P(("aux", "orb"), None),
            P(("aux", "orb"), None, None, None),
            P(("aux", "orb"), None, None),
            P(),
            P(),
        ),
        out_specs=(P(("aux", "orb"), None), P(("aux", "orb"))),
        check_vma=False,
    )
```

```python
import functools

import jax
import jax.numpy as jnp
from jax import lax
from jax.experimental import pallas as pl
from jax.experimental.pallas import tpu as pltpu
from jax.sharding import PartitionSpec as P

LAST = 128
SMEM = pl.BlockSpec(memory_space=pltpu.SMEM)
VMEM = pl.BlockSpec(memory_space=pltpu.VMEM)
ANY = pl.BlockSpec(memory_space=pl.ANY)


def copy(source, target, sem):
    return pltpu.make_async_copy(source, target, sem)


def pack_kernel(group, capacity, orbs, place, coef, *refs):
    outs, (held, count, holder, load_sem, store_sem) = refs[:-5], refs[-5:]
    load = copy(coef, held, load_sem)
    load.start()

    def clear(i, carry):
        holder[i] = 0
        return carry

    def clear_count(i, carry):
        count[i] = 0
        return carry

    def assign(s, carry):
        orb = orbs[s]
        at = count[orb]
        holder[orb * capacity + at] = s
        count[orb] = at + 1
        return carry

    lax.fori_loop(0, 2 * group * capacity, clear, 0)
    lax.fori_loop(0, 2 * group, clear_count, 0)
    lax.fori_loop(0, held.shape[0], assign, 0)
    load.wait()
    for mask, out in enumerate(outs):
        for kind in range(2):
            orb = place[1] ^ (mask + kind * group)

            def send(k, carry, orb=orb, kind=kind, out=out, sem=store_sem.at[mask]):
                copy(held.at[holder[orb * capacity + k]], out.at[kind * capacity + k], sem).start()
                return carry

            lax.fori_loop(0, capacity, send, 0)
    for mask, out in enumerate(outs):
        copy(held.at[pl.ds(0, 2 * capacity)], out, store_sem.at[mask]).wait()


def pack(orbs, place, coef, group, capacity):
    side_count, pno_count, dom_count = coef.shape
    block = jax.ShapeDtypeStruct((2 * capacity, pno_count, dom_count), coef.dtype)
    return pl.pallas_call(
        functools.partial(pack_kernel, group, capacity),
        out_shape=(block,) * group,
        in_specs=[SMEM, SMEM, ANY],
        out_specs=(ANY,) * group,
        scratch_shapes=[
            pltpu.VMEM(coef.shape, coef.dtype),
            pltpu.SMEM((2 * group,), jnp.int32),
            pltpu.SMEM((2 * group * capacity,), jnp.int32),
            pltpu.SemaphoreType.DMA,
            pltpu.SemaphoreType.DMA((group,)),
        ],
        cost_estimate=pl.CostEstimate(
            flops=0, transcendentals=0, bytes_accessed=6 * side_count * pno_count * dom_count
        ),
        name="pack",
    )(orbs, place, coef)


def project_kernel(group, capacity, kind, pieces, *refs):
    inner = group // 2
    blocks, parts = refs[:group], refs[group : group + len(pieces)]
    outs, (left, right, left_sem, right_sem) = refs[group + len(pieces) : -4], refs[-4:]
    for mask in range(group):
        base = ((mask % inner) * 2 + mask // inner) * capacity
        copy(
            blocks[mask].at[pl.ds(kind * capacity, capacity)],
            left.at[pl.ds(base, capacity)],
            left_sem,
        ).start()
    for part, (row, column, width) in zip(parts, pieces):
        copy(
            part.at[pl.ds(row, right.shape[0])], right.at[:, pl.ds(column, width)], right_sem
        ).start()
    copy(left, left, left_sem).wait()
    copy(right, right, right_sem).wait()
    _, pno_count, dom_count = left.shape
    row_count = right.shape[0]
    step = row_count if row_count <= 512 else 256

    def tile(t, carry):
        at = pl.multiple_of(t * step, step)
        rows = right[pl.ds(at, step), :]
        for i, out in enumerate(outs):
            lines = left[2 * capacity * i : 2 * capacity * (i + 1)]
            product = lax.dot_general(
                lines.reshape(2 * capacity * pno_count, dom_count),
                rows,
                (((1,), (1,)), ((), ())),
                preferred_element_type=jnp.float32,
            )
            out[:, :, pl.ds(at, step)] = product.astype(out.dtype).reshape(
                2 * capacity, pno_count, step
            )
        return carry

    if row_count == step:
        tile(0, 0)
    else:
        lax.fori_loop(0, row_count // step, tile, 0)


def project(blocks, kind, parts, pieces, row_count, name):
    group = len(blocks)
    slots, pno_count, dom_count = blocks[0].shape
    capacity = slots // 2
    out = jax.ShapeDtypeStruct((slots, pno_count, row_count), blocks[0].dtype)
    return pl.pallas_call(
        functools.partial(project_kernel, group, capacity, kind, tuple(pieces)),
        out_shape=(out,) * (group // 2),
        in_specs=[ANY] * (group + len(parts)),
        out_specs=(VMEM,) * (group // 2),
        scratch_shapes=[
            pltpu.VMEM((group * capacity, pno_count, dom_count), blocks[0].dtype),
            pltpu.VMEM((row_count, dom_count), blocks[0].dtype),
            pltpu.SemaphoreType.DMA,
            pltpu.SemaphoreType.DMA,
        ],
        cost_estimate=pl.CostEstimate(
            flops=2 * group * capacity * pno_count * dom_count * row_count,
            transcendentals=0,
            bytes_accessed=2 * group * capacity * pno_count * dom_count,
        ),
        name=name,
    )(*blocks, *parts)


def fetch(near, far, spans, low, width, group, differs, slot, target, sem):
    inner = group // 2
    for i in range(inner):
        line = (differs & (inner - 1)) == i

        @pl.when(line & ((differs & group) == 0))
        def _(i=i):
            copy(near[i].at[slot, :, pl.ds(low, width)], target, sem).start()

        @pl.when(line & ((differs & group) != 0))
        def _(i=i):
            for c, (start, size) in enumerate(spans):
                copy(
                    far[c * inner + i].at[slot], target.at[:, pl.ds(start - low, size)], sem
                ).start()


def forward_kernel(group, capacity, spans, orbs, position, place, *refs):
    inner = group // 2
    near, far, out, sem = refs[:inner], refs[inner:-2], refs[-2], refs[-1]
    low, width = spans[0][0], sum(size for _, size in spans)
    pair_count = out.shape[0]

    def look(n):
        first = orbs[1, 2 * n] ^ place[1]
        second = orbs[1, 2 * n + 1] ^ place[1]
        take_first = (first & inner) == 0
        return first, second, take_first, take_first != ((second & inner) == 0)

    def start(n, carry):
        first, second, take_first, mixed = look(n)

        @pl.when(mixed)
        def _():
            slot = capacity + jnp.where(take_first, position[1, 2 * n], position[1, 2 * n + 1])
            differs = jnp.where(take_first, first, second)
            fetch(near, far, spans, low, width, group, differs, slot, out.at[n], sem.at[n])

        return carry

    def finish(n, carry):
        @pl.when(look(n)[3])
        def _():
            copy(out.at[n], out.at[n], sem.at[n]).wait()

        return carry

    lax.fori_loop(0, pair_count, start, 0)
    lax.fori_loop(0, pair_count, finish, 0)


def forward(orbs, position, place, near, far, spans, group, name):
    slots, pno_count, _ = near[0].shape
    pair_count = orbs.shape[1] // 2
    return pl.pallas_call(
        functools.partial(forward_kernel, group, slots // 2, spans),
        out_shape=jax.ShapeDtypeStruct(
            (pair_count, pno_count, sum(size for _, size in spans)), near[0].dtype
        ),
        in_specs=[SMEM] * 3 + [ANY] * (len(near) + len(far)),
        out_specs=VMEM,
        scratch_shapes=[pltpu.SemaphoreType.DMA((pair_count,))],
        name=name,
    )(orbs, position, place, *near, *far)


def couple_kernel(group, capacity, spans, mixing, orbs, position, place, offset, before, *refs):
    inner = group // 2
    near = refs[:inner]
    far = refs[inner : inner + inner * len(spans)]
    others = refs[inner + inner * len(spans) : -3]
    coupling, sides, sem = refs[-3:]
    low, width = spans[0][0], sum(size for _, size in spans)
    homes, pair_count = coupling.shape[:2]
    first_orb = place[0] * (2 * group)

    def look(h, n):
        first = orbs[h, 2 * n] ^ place[1]
        second = orbs[h, 2 * n + 1] ^ place[1]
        here_first, here_second = (first & inner) == 0, (second & inner) == 0
        wanted = (here_first != here_second) if mixing else (here_first & here_second)
        return (first, second), (here_first, here_second), wanted

    for h in range(homes):

        def start(n, carry, h=h):
            differs, here, wanted = look(h, n)
            for k in range(2):
                s = 2 * n + k
                target, at = sides.at[h, s], sem.at[h, s]

                @pl.when(wanted & here[k])
                def _(k=k, s=s, target=target, at=at):
                    slot = h * capacity + position[h, s]
                    fetch(near, far, spans, low, width, group, differs[k], slot, target, at)

                if mixing:

                    @pl.when(wanted & jnp.logical_not(here[k]))
                    def _(target=target, at=at):
                        for other, (begin, size) in zip(others, spans):
                            copy(other.at[n], target.at[:, pl.ds(begin - low, size)], at).start()

            return carry

        lax.fori_loop(0, pair_count, start, 0)

    for h in range(homes):

        def one_pair(n, carry, h=h):
            _, _, wanted = look(h, n)

            @pl.when(wanted)
            def _():
                for k in range(2):
                    s = 2 * n + k
                    copy(sides.at[h, s], sides.at[h, s], sem.at[h, s]).wait()
                first = offset[first_orb + orbs[h, 2 * n]]
                second = offset[first_orb + orbs[h, 2 * n + 1]]
                lane = lax.broadcasted_iota(jnp.int32, (1, width), 1) + low
                apart = (lane < first) != (lane < second)
                keep = jnp.where(apart, 0.0, 1.0).astype(sides.dtype)
                product = lax.dot_general(
                    sides[h, 2 * n],
                    sides[h, 2 * n + 1] * keep,
                    (((1,), (1,)), ((), ())),
                    preferred_element_type=jnp.float32,
                )
                coupling[h, n] = product if low == 0 else product + before[h, n]

            @pl.when(jnp.logical_not(wanted))
            def _():
                coupling[h, n] = jnp.zeros(coupling.shape[2:], coupling.dtype)

            return carry

        lax.fori_loop(0, pair_count, one_pair, 0)


def couple(orbs, position, place, offset, before, near, far, others, spans, group, name):
    slots, pno_count, _ = near[0].shape
    homes = 1 if others else 2
    side_count = orbs.shape[1]
    width = sum(size for _, size in spans)
    if before is None:
        before = jnp.zeros((1, 8, 128), jnp.float32)
    return pl.pallas_call(
        functools.partial(couple_kernel, group, slots // 2, spans, bool(others)),
        out_shape=jax.ShapeDtypeStruct((homes, side_count // 2, pno_count, pno_count), jnp.float32),
        in_specs=[SMEM] * 4 + [VMEM] + [ANY] * (len(near) + len(far) + len(others)),
        out_specs=VMEM,
        scratch_shapes=[
            pltpu.VMEM((homes, side_count, pno_count, width), near[0].dtype),
            pltpu.SemaphoreType.DMA((homes, side_count)),
        ],
        name=name,
    )(orbs, position, place, offset, before, *near, *far, *others)


def slots_of(orbs):
    sequence = jnp.arange(orbs.shape[1], dtype=jnp.int32)
    same = orbs[:, :, None] == orbs[:, None, :]
    earlier = sequence[None, None, :] < sequence[None, :, None]
    return jnp.sum(jnp.where(same & earlier, 1, 0), axis=2).astype(jnp.int32)


def chunk_spans(fit_rows):
    sizes, start = [], 0
    body = (fit_rows - LAST) // 128
    for c in range(3):
        sizes.append(128 * (body // 3 + (1 if c < body % 3 else 0)))
    spans = []
    for size in sizes + [LAST]:
        spans.append((start, size))
        start += size
    return spans


def on_device(raw_ints, fit_inverse, pair_orbs, pno_coef, pno_energy, occ_energy, fit_offset):
    orb_count = lax.axis_size("orb")
    region = lax.axis_index("aux")
    group = orb_count // 2
    inner = group // 2
    pair_count = pair_orbs.shape[0]
    pno_count, dom_count = pno_coef.shape[2:]
    side_count = 2 * pair_count
    capacity = max(2, 4 * pair_count // orb_count)
    fit_rows = fit_inverse.shape[1]

    def across(array, mask):
        return lax.ppermute(array, "orb", [(i, i ^ mask) for i in range(orb_count)])

    own_orbs = pair_orbs.reshape(side_count)
    place = jnp.stack([region, lax.axis_index("orb")]).astype(jnp.int32)
    half = dom_count // 2
    raw_parts = [
        lax.all_to_all(
            raw_ints[:, :, :, k * half : (k + 1) * half],
            "aux",
            split_axis=0,
            concat_axis=2,
            tiled=True,
        )[0, 0]
        for k in range(2)
    ]
    blocks = pack(
        own_orbs, place, pno_coef.reshape(side_count, pno_count, dom_count), group, capacity
    )
    blocks = [blocks[0]] + [across(blocks[m], m) for m in range(1, group)]
    orbs = jnp.stack([own_orbs, across(own_orbs, inner)])
    position = slots_of(orbs)
    own_offset = fit_offset[region * orb_count + lax.axis_index("orb")]
    turned = jnp.roll(fit_inverse[0], own_offset, axis=0)
    fitted = [
        jnp.dot(turned, part, preferred_element_type=jnp.float32).astype(jnp.bfloat16)
        for part in raw_parts
    ]
    spans = chunk_spans(fit_rows)
    mirrored_head = across(fitted[0], group)
    mirrored = [across(fitted[1][start : start + size], group) for start, size in spans]

    def hop(outs):
        return [outs[0]] + [across(outs[i], i) for i in range(1, inner)]

    near = hop(
        project(blocks, 0, fitted, [(0, 0, half), (0, half, half)], fit_rows, "project_near")
    )
    far, others = [], []
    for c, span in enumerate(spans):
        parts = project(
            blocks,
            1,
            [mirrored_head, mirrored[c]],
            [(span[0], 0, half), (0, half, half)],
            span[1],
            f"project_far_{c}",
        )
        far.append(hop(parts))
        others.append(
            across(
                forward(orbs, position, place, near, far[c], (span,), group, f"forward_{c}"), inner
            )
        )

    def sum_over(which, before, mixing, name):
        return couple(
            orbs,
            position,
            place,
            fit_offset,
            before,
            near,
            [part for c in which for part in far[c]],
            [others[c] for c in which] if mixing else [],
            tuple(spans[c] for c in which),
            group,
            name,
        )

    body, tail = range(len(spans) - 1), [len(spans) - 1]
    here = sum_over(tail, sum_over(body, None, False, "here_body"), False, "here_tail")
    mixed = sum_over(tail, sum_over(body, None, True, "mixed_body"), True, "mixed_tail")
    coupling = here[0] + across(here[1], inner) + mixed[0]
    orb_total = occ_energy.shape[0]
    global_orb = region * orb_count + pair_orbs
    selector = global_orb[:, :, None] == jnp.arange(orb_total, dtype=jnp.int32)[None, None, :]
    occupied = jnp.sum(jnp.where(selector, occ_energy[None, None, :], 0.0), axis=2)
    denominator = (
        pno_energy[:, 0, :, None]
        + pno_energy[:, 1, None, :]
        - occupied[:, 0, None, None]
        - occupied[:, 1, None, None]
    )
    amplitude = -coupling / denominator
    energy = jnp.sum(coupling * (2.0 * amplitude - jnp.swapaxes(amplitude, 1, 2)), axis=(1, 2))
    return (amplitude.reshape(pair_count, pno_count * pno_count), energy)


def solution(mesh):
    return jax.shard_map(
        on_device,
        mesh=mesh,
        in_specs=(
            P(None, "orb", "aux", None),
            P(("aux", "orb"), None, None),
            P(("aux", "orb"), None),
            P(("aux", "orb"), None, None, None),
            P(("aux", "orb"), None, None),
            P(),
            P(),
        ),
        out_specs=(P(("aux", "orb"), None), P(("aux", "orb"))),
        check_vma=False,
    )
```

```python
import functools

import jax
import jax.numpy as jnp
from jax import lax
from jax.experimental import pallas as pl
from jax.experimental.pallas import tpu as pltpu
from jax.sharding import PartitionSpec as P

LAST = 128
SMEM = pl.BlockSpec(memory_space=pltpu.SMEM)
VMEM = pl.BlockSpec(memory_space=pltpu.VMEM)
ANY = pl.BlockSpec(memory_space=pl.ANY)


def copy(source, target, sem):
    return pltpu.make_async_copy(source, target, sem)


def pack_kernel(group, capacity, orbs, place, coef, *refs):
    outs, (held, count, holder, load_sem, store_sem) = refs[:-5], refs[-5:]
    load = copy(coef, held, load_sem)
    load.start()

    def clear(i, carry):
        holder[i] = 0
        return carry

    def clear_count(i, carry):
        count[i] = 0
        return carry

    def assign(s, carry):
        orb = orbs[s]
        at = count[orb]
        holder[orb * capacity + at] = s
        count[orb] = at + 1
        return carry

    lax.fori_loop(0, 2 * group * capacity, clear, 0)
    lax.fori_loop(0, 2 * group, clear_count, 0)
    lax.fori_loop(0, held.shape[0], assign, 0)
    load.wait()
    for mask, out in enumerate(outs):
        for kind in range(2):
            orb = place[1] ^ (mask + kind * group)

            def send(k, carry, orb=orb, kind=kind, out=out, sem=store_sem.at[mask]):
                copy(held.at[holder[orb * capacity + k]], out.at[kind * capacity + k], sem).start()
                return carry

            lax.fori_loop(0, capacity, send, 0)
    for mask, out in enumerate(outs):
        copy(held.at[pl.ds(0, 2 * capacity)], out, store_sem.at[mask]).wait()


def pack(orbs, place, coef, group, capacity):
    side_count, pno_count, dom_count = coef.shape
    block = jax.ShapeDtypeStruct((2 * capacity, pno_count, dom_count), coef.dtype)
    return pl.pallas_call(
        functools.partial(pack_kernel, group, capacity),
        out_shape=(block,) * group,
        in_specs=[SMEM, SMEM, ANY],
        out_specs=(ANY,) * group,
        scratch_shapes=[
            pltpu.VMEM(coef.shape, coef.dtype),
            pltpu.SMEM((2 * group,), jnp.int32),
            pltpu.SMEM((2 * group * capacity,), jnp.int32),
            pltpu.SemaphoreType.DMA,
            pltpu.SemaphoreType.DMA((group,)),
        ],
        cost_estimate=pl.CostEstimate(
            flops=0, transcendentals=0, bytes_accessed=6 * side_count * pno_count * dom_count
        ),
        name="pack",
    )(orbs, place, coef)


def project_kernel(group, capacity, kind, pieces, *refs):
    inner = group // 2
    count = group + len(pieces)
    blocks, parts = refs[:group], refs[group:count]
    outs, (left, right, made, left_sem, right_sem, out_sem) = refs[-6 - inner : -6], refs[-6:]
    row_count = right.shape[0]
    _, pno_count, dom_count = left.shape
    lines = 2 * capacity
    for part, (row, column, width) in zip(parts, pieces):
        copy(
            part.at[pl.ds(row, row_count)], right.at[:, pl.ds(column, width)], right_sem
        ).start()
    for i in range(inner):
        for j in range(2):
            copy(
                blocks[i + j * inner].at[pl.ds(kind * capacity, capacity)],
                left.at[pl.ds(i * lines + j * capacity, capacity)],
                left_sem.at[i],
            ).start()
    copy(right, right, right_sem).wait()
    step = row_count if row_count <= 512 else 256
    for i in range(inner):
        mine = left.at[pl.ds(i * lines, lines)]
        copy(mine, mine, left_sem.at[i]).wait()

        def tile(t, carry, i=i, mine=mine):
            at = t * step if isinstance(t, int) else pl.multiple_of(t * step, step)
            product = lax.dot_general(
                mine[...].reshape(lines * pno_count, dom_count),
                right[pl.ds(at, step), :],
                (((1,), (1,)), ((), ())),
                preferred_element_type=jnp.float32,
            )
            made[i, :, :, pl.ds(at, step)] = product.astype(made.dtype).reshape(
                lines, pno_count, step
            )
            return carry

        if row_count == step:
            tile(0, 0)
        else:
            lax.fori_loop(0, row_count // step, tile, 0)
        copy(made.at[i], outs[i], out_sem).start()
    for i in range(inner):
        copy(made.at[i], outs[i], out_sem).wait()


def project(blocks, kind, parts, pieces, row_count, tokens):
    group = len(blocks)
    inner = group // 2
    slots, pno_count, dom_count = blocks[0].shape
    capacity = slots // 2
    dtype = blocks[0].dtype
    out = jax.ShapeDtypeStruct((slots, pno_count, row_count), dtype)
    return pl.pallas_call(
        functools.partial(project_kernel, group, capacity, kind, tuple(pieces)),
        out_shape=(out,) * inner,
        in_specs=[ANY] * (group + len(parts) + len(tokens)),
        out_specs=(ANY,) * inner,
        scratch_shapes=[
            pltpu.VMEM((group * capacity, pno_count, dom_count), dtype),
            pltpu.VMEM((row_count, dom_count), dtype),
            pltpu.VMEM((inner, slots, pno_count, row_count), dtype),
            pltpu.SemaphoreType.DMA((inner,)),
            pltpu.SemaphoreType.DMA,
            pltpu.SemaphoreType.DMA,
        ],
        compiler_params=pltpu.CompilerParams(vmem_limit_bytes=24 << 20),
        cost_estimate=pl.CostEstimate(
            flops=2 * group * capacity * pno_count * dom_count * row_count,
            transcendentals=0,
            bytes_accessed=2 * group * capacity * pno_count * dom_count,
        ),
    )(*blocks, *parts, *tokens)


def gather_sides(near, far, spans, slots, held, sem):
    inner = len(near)
    low, width = spans[0][0], sum(size for _, size in spans)
    for i in range(inner):
        copy(
            near[i].at[pl.ds(0, slots), :, pl.ds(low, width)],
            held.at[pl.ds(i * slots, slots)],
            sem,
        ).start()
        for c, (begin, size) in enumerate(spans):
            copy(
                far[c * inner + i].at[pl.ds(0, slots)],
                held.at[pl.ds((inner + i) * slots, slots), :, pl.ds(begin - low, size)],
                sem,
            ).start()


def overlap(first, second, limits, low):
    if low < limits[2]:
        lane = lax.broadcasted_iota(jnp.int32, (1, second.shape[1]), 1) + low
        apart = (lane < limits[0]) != (lane < limits[1])
        second = second * jnp.where(apart, 0.0, 1.0).astype(second.dtype)
    return lax.dot_general(
        first, second, (((1,), (1,)), ((), ())), preferred_element_type=jnp.float32
    )


def relay_kernel(inner, spans, margin, rows, offsets, before, *refs):
    near, far = refs[:inner], refs[inner : 2 * inner]
    sent, coupling, held, sem = refs[-4:]
    low = spans[0][0]
    pair_count = sent.shape[0]
    gather_sides(near, far, spans, near[0].shape[0], held, sem)
    copy(held, held, sem).wait()

    def choose(n, carry):
        sent[n] = held[jnp.maximum(jnp.maximum(rows[1, 2 * n], rows[1, 2 * n + 1]), 0)]
        return carry

    lax.fori_loop(0, pair_count, choose, 0, unroll=4)
    for h in range(2):

        def one_pair(n, carry, h=h):
            first, second = rows[h, 2 * n], rows[h, 2 * n + 1]
            product = overlap(
                held[jnp.maximum(first, 0)],
                held[jnp.maximum(second, 0)],
                (offsets[h, 2 * n], offsets[h, 2 * n + 1], margin),
                low,
            )
            product = jnp.where((first >= 0) & (second >= 0), product, 0.0)
            coupling[h, n] = product if low == 0 else product + before[h, n]
            return carry

        lax.fori_loop(0, pair_count, one_pair, 0, unroll=4)


def relay(rows, offsets, before, near, far, span, margin, tokens):
    inner = len(near)
    slots, pno_count, _ = near[0].shape
    pair_count = rows.shape[1] // 2
    return pl.pallas_call(
        functools.partial(relay_kernel, inner, (span,), margin),
        out_shape=(
            jax.ShapeDtypeStruct((pair_count, pno_count, span[1]), near[0].dtype),
            jax.ShapeDtypeStruct((2, pair_count, pno_count, pno_count), jnp.float32),
        ),
        in_specs=[SMEM, SMEM, VMEM] + [ANY] * (len(near) + len(far) + len(tokens)),
        out_specs=(VMEM, VMEM),
        scratch_shapes=[
            pltpu.VMEM((2 * inner * slots, pno_count, span[1]), near[0].dtype),
            pltpu.SemaphoreType.DMA,
        ],
        compiler_params=pltpu.CompilerParams(vmem_limit_bytes=24 << 20),
    )(rows, offsets, before, *near, *far, *tokens)


def mixed_pairs(inner, spans, margin, rows, offsets, near, far, others, held, sem, write):
    low = spans[0][0]
    slots = near[0].shape[0] // 2
    pair_count = others[0].shape[0]
    at = 2 * inner * slots
    gather_sides(near, far, spans, slots, held, sem)
    for other, (begin, size) in zip(others, spans):
        copy(
            other, held.at[pl.ds(at, pair_count), :, pl.ds(begin - low, size)], sem
        ).start()
    copy(held, held, sem).wait()

    def one_pair(n, carry):
        first, second = rows[0, 2 * n], rows[0, 2 * n + 1]
        product = overlap(
            held[jnp.where(first >= 0, first, at + n)],
            held[jnp.where(second >= 0, second, at + n)],
            (offsets[0, 2 * n], offsets[0, 2 * n + 1], margin),
            low,
        )
        write(n, jnp.where((first >= 0) != (second >= 0), product, 0.0))
        return carry

    lax.fori_loop(0, pair_count, one_pair, 0, unroll=4)


def mixed_kernel(inner, spans, margin, rows, offsets, *refs):
    near, refs = refs[:inner], refs[inner:]
    far, refs = refs[: inner * len(spans)], refs[inner * len(spans) :]
    others = refs[: len(spans)]
    coupling, held, sem = refs[-3:]

    def write(n, product):
        coupling[n] = product

    mixed_pairs(inner, spans, margin, rows, offsets, near, far, others, held, sem, write)


def finish_kernel(inner, spans, margin, rows, offsets, here, there, before, denominator, *refs):
    near, refs = refs[:inner], refs[inner:]
    far, refs = refs[: inner * len(spans)], refs[inner * len(spans) :]
    others = refs[: len(spans)]
    amplitude, energy, coupling, held, sem = refs[-5:]

    def write(n, product):
        coupling[n] = product

    mixed_pairs(inner, spans, margin, rows, offsets, near, far, others, held, sem, write)
    total = coupling[...] + before[...] + here[0] + there[...]
    result = -total / denominator[...]
    amplitude[...] = result
    parts = total * (2.0 * result - jnp.swapaxes(result, 1, 2))
    energy[...] = jnp.sum(jnp.sum(parts, axis=1), axis=1, keepdims=True)


def mixed(rows, offsets, near, far, others, spans, margin, tokens, finals):
    inner = len(near)
    slots, pno_count, _ = near[0].shape
    pair_count = rows.shape[1] // 2
    width = sum(size for _, size in spans)
    square = jax.ShapeDtypeStruct((pair_count, pno_count, pno_count), jnp.float32)
    line = jax.ShapeDtypeStruct((pair_count, 1), jnp.float32)
    scratch = [
        pltpu.VMEM((inner * slots + pair_count, pno_count, width), near[0].dtype),
        pltpu.SemaphoreType.DMA,
    ]
    if finals:
        scratch = [pltpu.VMEM(square.shape, jnp.float32)] + scratch
    return pl.pallas_call(
        functools.partial(
            finish_kernel if finals else mixed_kernel, inner, tuple(spans), margin
        ),
        out_shape=(square, line) if finals else square,
        in_specs=[SMEM] * 2
        + [VMEM] * len(finals)
        + [ANY] * (len(near) + len(far) + len(others) + len(tokens)),
        out_specs=(VMEM, VMEM) if finals else VMEM,
        scratch_shapes=scratch,
        compiler_params=pltpu.CompilerParams(vmem_limit_bytes=24 << 20),
    )(rows, offsets, *finals, *near, *far, *others, *tokens)


def slots_of(orbs):
    sequence = jnp.arange(orbs.shape[1], dtype=jnp.int32)
    same = orbs[:, :, None] == orbs[:, None, :]
    earlier = sequence[None, None, :] < sequence[None, :, None]
    return jnp.sum(jnp.where(same & earlier, 1, 0), axis=2).astype(jnp.int32)


def chunk_spans(fit_rows):
    sizes, start = [], 0
    body = (fit_rows - LAST) // 128
    for c in range(3):
        sizes.append(128 * (body // 3 + (1 if c < body % 3 else 0)))
    spans = []
    for size in sizes + [LAST]:
        spans.append((start, size))
        start += size
    return spans


def on_device(raw_ints, fit_inverse, pair_orbs, pno_coef, pno_energy, occ_energy, fit_offset):
    orb_count = lax.axis_size("orb")
    region, me = lax.axis_index("aux"), lax.axis_index("orb")
    group = orb_count // 2
    inner = group // 2
    pair_count = pair_orbs.shape[0]
    pno_count, dom_count = pno_coef.shape[2:]
    side_count = 2 * pair_count
    capacity = max(2, 4 * pair_count // orb_count)
    fit_rows = fit_inverse.shape[1]
    margin = fit_rows // 4

    def across(array, mask):
        return lax.ppermute(array, "orb", [(i, i ^ mask) for i in range(orb_count)])

    own_orbs = pair_orbs.reshape(side_count)
    place = jnp.stack([region, me]).astype(jnp.int32)
    half = dom_count // 2
    raw_parts = []
    for k in range(2):
        part = lax.all_to_all(
            raw_ints[:, :, :, k * half : (k + 1) * half],
            "aux",
            split_axis=0,
            concat_axis=2,
            tiled=True,
        )
        raw_parts.append(part[0, 0])
    packed = pack(
        own_orbs, place, pno_coef.reshape(side_count, pno_count, dom_count), group, capacity
    )
    blocks = [packed[0]]
    for m in range(1, group):
        blocks.append(across(packed[m], m))
    own_offset = fit_offset[region * orb_count + me]
    turned = lax.optimization_barrier(jnp.roll(fit_inverse[0], own_offset, axis=0))
    orbs = jnp.stack([own_orbs, across(own_orbs, inner)])
    differs = orbs ^ me
    line = jnp.where((differs & group) != 0, inner, 0) + (differs & (inner - 1))
    home = jnp.arange(2, dtype=jnp.int32)[:, None]
    position = slots_of(orbs)
    there = (differs & inner) != 0
    rows = jnp.where(there, -1, line * 2 * capacity + home * capacity + position)
    rows_home = jnp.where(there, -1, line * capacity + position)
    orb_total = occ_energy.shape[0]
    global_orb = region * orb_count + orbs
    selector = global_orb[:, :, None] == jnp.arange(orb_total, dtype=jnp.int32)[None, None, :]
    offsets = jnp.sum(jnp.where(selector, fit_offset[None, None, :], 0), axis=2)
    occupied = jnp.sum(jnp.where(selector[0], occ_energy[None, :], 0.0), axis=1)
    occupied = occupied.reshape(pair_count, 2)
    denominator = (
        pno_energy[:, 0, :, None]
        + pno_energy[:, 1, None, :]
        - occupied[:, 0, None, None]
        - occupied[:, 1, None, None]
    )
    spans = chunk_spans(fit_rows)
    fitted, mirrored = [], []
    for k in range(2):
        fitted.append(
            jnp.dot(turned, raw_parts[k], preferred_element_type=jnp.float32).astype(jnp.bfloat16)
        )
        if k == 0:
            mirrored.append(across(fitted[0], group))
        else:
            for begin, size in spans:
                mirrored.append(across(fitted[1][begin : begin + size], group))

    def hop(outs):
        return [outs[0]] + [across(outs[i], i) for i in range(1, inner)]

    near = project(blocks, 0, fitted, [(0, 0, half), (0, half, half)], fit_rows, [])
    near = hop(near)
    far, others, tokens = [], [], []
    here = jnp.zeros((8, 128), jnp.float32)
    body = None
    for c, span in enumerate(spans):
        final = c == len(spans) - 1
        parts = project(
            blocks,
            1,
            [mirrored[0], mirrored[1 + c]],
            [(span[0], 0, half), (0, half, half)],
            span[1],
            tokens,
        )
        if final:
            body = mixed(
                rows_home,
                offsets,
                near,
                far[0] + far[1],
                others[:2],
                spans[:2],
                margin,
                [parts[0]],
                [],
            )
        far.append(hop(parts))
        sent, here = relay(rows, offsets, here, near, far[c], span, margin, [body] if final else [])
        tokens = [here]
        others.append(across(sent, inner))
    amplitude, energy = mixed(
        rows_home,
        offsets,
        near,
        far[2] + far[3],
        others[2:],
        spans[2:],
        margin,
        [],
        [here, across(here[1], inner), body, denominator],
    )
    return (amplitude.reshape(pair_count, pno_count * pno_count), energy.reshape(pair_count))


def solution(mesh):
    return jax.shard_map(
        on_device,
        mesh=mesh,
        in_specs=(
            P(None, "orb", "aux", None),
            P(("aux", "orb"), None, None),
            P(("aux", "orb"), None),
            P(("aux", "orb"), None, None, None),
            P(("aux", "orb"), None, None),
            P(),
            P(),
        ),
        out_specs=(P(("aux", "orb"), None), P(("aux", "orb"))),
        check_vma=False,
    )
```

```python
import functools

import jax
import jax.numpy as jnp
from jax import lax
from jax.experimental import pallas as pl
from jax.experimental.pallas import tpu as pltpu
from jax.sharding import PartitionSpec as P

SMEM = pl.BlockSpec(memory_space=pltpu.SMEM)
VMEM = pl.BlockSpec(memory_space=pltpu.VMEM)
ANY = pl.BlockSpec(memory_space=pl.ANY)


def copy(source, target, sem):
    return pltpu.make_async_copy(source, target, sem)


def pack_kernel(group, capacity, orbs, place, coef, *refs):
    outs, (held, count, holder, load_sem, store_sem) = refs[:-5], refs[-5:]
    load = copy(coef, held, load_sem)
    load.start()

    def clear(i, carry):
        holder[i] = 0
        return carry

    def clear_count(i, carry):
        count[i] = 0
        return carry

    def assign(s, carry):
        orb = orbs[s]
        at = count[orb]
        holder[orb * capacity + at] = s
        count[orb] = at + 1
        return carry

    lax.fori_loop(0, 2 * group * capacity, clear, 0)
    lax.fori_loop(0, 2 * group, clear_count, 0)
    lax.fori_loop(0, held.shape[0], assign, 0)
    load.wait()
    for mask, out in enumerate(outs):
        for kind in range(2):
            orb = place[1] ^ (mask + kind * group)

            def send(k, carry, orb=orb, kind=kind, out=out, sem=store_sem.at[mask]):
                copy(held.at[holder[orb * capacity + k]], out.at[kind * capacity + k], sem).start()
                return carry

            lax.fori_loop(0, capacity, send, 0)
    for mask, out in enumerate(outs):
        copy(held.at[pl.ds(0, 2 * capacity)], out, store_sem.at[mask]).wait()


def pack(orbs, place, coef, group, capacity):
    side_count, pno_count, dom_count = coef.shape
    block = jax.ShapeDtypeStruct((2 * capacity, pno_count, dom_count), coef.dtype)
    return pl.pallas_call(
        functools.partial(pack_kernel, group, capacity),
        out_shape=(block,) * group,
        in_specs=[SMEM, SMEM, ANY],
        out_specs=(ANY,) * group,
        scratch_shapes=[
            pltpu.VMEM(coef.shape, coef.dtype),
            pltpu.SMEM((2 * group,), jnp.int32),
            pltpu.SMEM((2 * group * capacity,), jnp.int32),
            pltpu.SemaphoreType.DMA,
            pltpu.SemaphoreType.DMA((group,)),
        ],
        cost_estimate=pl.CostEstimate(
            flops=0, transcendentals=0, bytes_accessed=6 * side_count * pno_count * dom_count
        ),
        name="pack",
    )(orbs, place, coef)


def project_kernel(group, capacity, kind, pieces, *refs):
    inner = group // 2
    count = group + len(pieces)
    blocks, parts = refs[:group], refs[group:count]
    outs, (left, right, made, left_sem, right_sem, out_sem) = refs[-6 - inner : -6], refs[-6:]
    row_count = right.shape[0]
    _, pno_count, dom_count = left.shape
    lines = 2 * capacity
    for part, (row, column, width) in zip(parts, pieces):
        copy(
            part.at[pl.ds(row, row_count)], right.at[:, pl.ds(column, width)], right_sem
        ).start()
    for i in range(inner):
        for j in range(2):
            copy(
                blocks[i + j * inner].at[pl.ds(kind * capacity, capacity)],
                left.at[pl.ds(i * lines + j * capacity, capacity)],
                left_sem.at[i],
            ).start()
    copy(right, right, right_sem).wait()
    step = row_count if row_count <= 512 else 256
    for i in range(inner):
        mine = left.at[pl.ds(i * lines, lines)]
        copy(mine, mine, left_sem.at[i]).wait()

        def tile(t, carry, i=i, mine=mine):
            at = t * step if isinstance(t, int) else pl.multiple_of(t * step, step)
            product = lax.dot_general(
                mine[...].reshape(lines * pno_count, dom_count),
                right[pl.ds(at, step), :],
                (((1,), (1,)), ((), ())),
                preferred_element_type=jnp.float32,
            )
            made[i, :, :, pl.ds(at, step)] = product.astype(made.dtype).reshape(
                lines, pno_count, step
            )
            return carry

        if row_count == step:
            tile(0, 0)
        else:
            lax.fori_loop(0, row_count // step, tile, 0)
        copy(made.at[i], outs[i], out_sem).start()
    for i in range(inner):
        copy(made.at[i], outs[i], out_sem).wait()


def project(blocks, kind, parts, pieces, row_count, tokens):
    group = len(blocks)
    inner = group // 2
    slots, pno_count, dom_count = blocks[0].shape
    capacity = slots // 2
    dtype = blocks[0].dtype
    out = jax.ShapeDtypeStruct((slots, pno_count, row_count), dtype)
    return pl.pallas_call(
        functools.partial(project_kernel, group, capacity, kind, tuple(pieces)),
        out_shape=(out,) * inner,
        in_specs=[ANY] * (group + len(parts) + len(tokens)),
        out_specs=(ANY,) * inner,
        scratch_shapes=[
            pltpu.VMEM((group * capacity, pno_count, dom_count), dtype),
            pltpu.VMEM((row_count, dom_count), dtype),
            pltpu.VMEM((inner, slots, pno_count, row_count), dtype),
            pltpu.SemaphoreType.DMA((inner,)),
            pltpu.SemaphoreType.DMA,
            pltpu.SemaphoreType.DMA,
        ],
        compiler_params=pltpu.CompilerParams(vmem_limit_bytes=24 << 20),
        cost_estimate=pl.CostEstimate(
            flops=2 * group * capacity * pno_count * dom_count * row_count,
            transcendentals=0,
            bytes_accessed=2 * group * capacity * pno_count * dom_count,
        ),
    )(*blocks, *parts, *tokens)


def gather_sides(near, far, spans, slots, held, sem):
    inner = len(near)
    low, width = spans[0][0], sum(size for _, size in spans)
    for i in range(inner):
        copy(
            near[i].at[pl.ds(0, slots), :, pl.ds(low, width)],
            held.at[pl.ds(i * slots, slots)],
            sem,
        ).start()
        for c, (begin, size) in enumerate(spans):
            copy(
                far[c * inner + i].at[pl.ds(0, slots)],
                held.at[pl.ds((inner + i) * slots, slots), :, pl.ds(begin - low, size)],
                sem,
            ).start()


def overlap(first, second, limits, low):
    if low < limits[2]:
        lane = lax.broadcasted_iota(jnp.int32, (1, second.shape[1]), 1) + low
        apart = (lane < limits[0]) != (lane < limits[1])
        second = second * jnp.where(apart, 0.0, 1.0).astype(second.dtype)
    return lax.dot_general(
        first, second, (((1,), (1,)), ((), ())), preferred_element_type=jnp.float32
    )


def relay_kernel(inner, spans, margin, rows, offsets, before, *refs):
    near, far = refs[:inner], refs[inner : 2 * inner]
    sent, coupling, held, sem = refs[-4:]
    low = spans[0][0]
    pair_count = sent.shape[0]
    gather_sides(near, far, spans, near[0].shape[0], held, sem)
    copy(held, held, sem).wait()

    def choose(n, carry):
        sent[n] = held[jnp.maximum(jnp.maximum(rows[1, 2 * n], rows[1, 2 * n + 1]), 0)]
        return carry

    lax.fori_loop(0, pair_count, choose, 0, unroll=4)
    for h in range(2):

        def one_pair(n, carry, h=h):
            first, second = rows[h, 2 * n], rows[h, 2 * n + 1]
            product = overlap(
                held[jnp.maximum(first, 0)],
                held[jnp.maximum(second, 0)],
                (offsets[h, 2 * n], offsets[h, 2 * n + 1], margin),
                low,
            )
            product = jnp.where((first >= 0) & (second >= 0), product, 0.0)
            coupling[h, n] = product if low == 0 else product + before[h, n]
            return carry

        lax.fori_loop(0, pair_count, one_pair, 0, unroll=4)


def relay(rows, offsets, before, near, far, span, margin, tokens):
    inner = len(near)
    slots, pno_count, _ = near[0].shape
    pair_count = rows.shape[1] // 2
    return pl.pallas_call(
        functools.partial(relay_kernel, inner, (span,), margin),
        out_shape=(
            jax.ShapeDtypeStruct((pair_count, pno_count, span[1]), near[0].dtype),
            jax.ShapeDtypeStruct((2, pair_count, pno_count, pno_count), jnp.float32),
        ),
        in_specs=[SMEM, SMEM, VMEM] + [ANY] * (len(near) + len(far) + len(tokens)),
        out_specs=(VMEM, VMEM),
        scratch_shapes=[
            pltpu.VMEM((2 * inner * slots, pno_count, span[1]), near[0].dtype),
            pltpu.SemaphoreType.DMA,
        ],
        compiler_params=pltpu.CompilerParams(vmem_limit_bytes=24 << 20),
    )(rows, offsets, before, *near, *far, *tokens)


def mixed_pairs(inner, spans, margin, rows, offsets, near, far, others, held, sem, write):
    low = spans[0][0]
    slots = near[0].shape[0] // 2
    pair_count = others[0].shape[0]
    at = 2 * inner * slots
    gather_sides(near, far, spans, slots, held, sem)
    for other, (begin, size) in zip(others, spans):
        copy(
            other, held.at[pl.ds(at, pair_count), :, pl.ds(begin - low, size)], sem
        ).start()
    copy(held, held, sem).wait()

    def one_pair(n, carry):
        first, second = rows[0, 2 * n], rows[0, 2 * n + 1]
        product = overlap(
            held[jnp.where(first >= 0, first, at + n)],
            held[jnp.where(second >= 0, second, at + n)],
            (offsets[0, 2 * n], offsets[0, 2 * n + 1], margin),
            low,
        )
        write(n, jnp.where((first >= 0) != (second >= 0), product, 0.0))
        return carry

    lax.fori_loop(0, pair_count, one_pair, 0, unroll=4)


def mixed_kernel(inner, spans, margin, rows, offsets, *refs):
    near, refs = refs[:inner], refs[inner:]
    far, refs = refs[: inner * len(spans)], refs[inner * len(spans) :]
    others = refs[: len(spans)]
    coupling, held, sem = refs[-3:]

    def write(n, product):
        coupling[n] = product

    mixed_pairs(inner, spans, margin, rows, offsets, near, far, others, held, sem, write)


def finish_kernel(inner, spans, margin, rows, offsets, here, there, before, denominator, *refs):
    near, refs = refs[:inner], refs[inner:]
    far, refs = refs[: inner * len(spans)], refs[inner * len(spans) :]
    others = refs[: len(spans)]
    amplitude, energy, coupling, held, sem = refs[-5:]

    def write(n, product):
        coupling[n] = product

    mixed_pairs(inner, spans, margin, rows, offsets, near, far, others, held, sem, write)
    total = coupling[...] + before[...] + here[0] + there[...]
    result = -total / denominator[...]
    amplitude[...] = result
    parts = total * (2.0 * result - jnp.swapaxes(result, 1, 2))
    energy[...] = jnp.sum(jnp.sum(parts, axis=1), axis=1, keepdims=True)


def mixed(rows, offsets, near, far, others, spans, margin, tokens, finals):
    inner = len(near)
    slots, pno_count, _ = near[0].shape
    pair_count = rows.shape[1] // 2
    width = sum(size for _, size in spans)
    square = jax.ShapeDtypeStruct((pair_count, pno_count, pno_count), jnp.float32)
    line = jax.ShapeDtypeStruct((pair_count, 1), jnp.float32)
    scratch = [
        pltpu.VMEM((inner * slots + pair_count, pno_count, width), near[0].dtype),
        pltpu.SemaphoreType.DMA,
    ]
    if finals:
        scratch = [pltpu.VMEM(square.shape, jnp.float32)] + scratch
    return pl.pallas_call(
        functools.partial(
            finish_kernel if finals else mixed_kernel, inner, tuple(spans), margin
        ),
        out_shape=(square, line) if finals else square,
        in_specs=[SMEM] * 2
        + [VMEM] * len(finals)
        + [ANY] * (len(near) + len(far) + len(others) + len(tokens)),
        out_specs=(VMEM, VMEM) if finals else VMEM,
        scratch_shapes=scratch,
        compiler_params=pltpu.CompilerParams(vmem_limit_bytes=24 << 20),
    )(rows, offsets, *finals, *near, *far, *others, *tokens)


def slots_of(orbs):
    sequence = jnp.arange(orbs.shape[1], dtype=jnp.int32)
    same = orbs[:, :, None] == orbs[:, None, :]
    earlier = sequence[None, None, :] < sequence[None, :, None]
    return jnp.sum(jnp.where(same & earlier, 1, 0), axis=2).astype(jnp.int32)


def chunk_spans(fit_rows):
    sizes = (fit_rows // 2, 3 * fit_rows // 8, fit_rows // 8)
    return [(sum(sizes[:c]), size) for c, size in enumerate(sizes)]


def on_device(raw_ints, fit_inverse, pair_orbs, pno_coef, pno_energy, occ_energy, fit_offset):
    orb_count = lax.axis_size("orb")
    region, me = lax.axis_index("aux"), lax.axis_index("orb")
    group = orb_count // 2
    inner = group // 2
    pair_count = pair_orbs.shape[0]
    pno_count, dom_count = pno_coef.shape[2:]
    side_count = 2 * pair_count
    capacity = max(2, 4 * pair_count // orb_count)
    fit_rows = fit_inverse.shape[1]
    margin = fit_rows // 4

    def across(array, mask):
        return lax.ppermute(array, "orb", [(i, i ^ mask) for i in range(orb_count)])

    own_orbs = pair_orbs.reshape(side_count)
    mate_orbs = across(own_orbs, inner)
    place = jnp.stack([region, me]).astype(jnp.int32)
    half = dom_count // 2

    def exchange(array, k):
        part = lax.all_to_all(
            array[:, :, :, k * half : (k + 1) * half],
            "aux",
            split_axis=0,
            concat_axis=2,
            tiled=True,
        )
        return part[0, 0]

    raw_parts = [exchange(raw_ints, 0)]
    packed = pack(
        own_orbs, place, pno_coef.reshape(side_count, pno_count, dom_count), group, capacity
    )
    later, packed = lax.optimization_barrier((raw_ints, packed))
    raw_parts.append(exchange(later, 1))
    blocks = [packed[0]]
    for m in range(1, group):
        blocks.append(across(packed[m], m))
    own_offset = fit_offset[region * orb_count + me]
    turned = lax.optimization_barrier(jnp.roll(fit_inverse[0], own_offset, axis=0))
    orbs = jnp.stack([own_orbs, mate_orbs])
    differs = orbs ^ me
    line = jnp.where((differs & group) != 0, inner, 0) + (differs & (inner - 1))
    home = jnp.arange(2, dtype=jnp.int32)[:, None]
    position = slots_of(orbs)
    there = (differs & inner) != 0
    rows = jnp.where(there, -1, line * 2 * capacity + home * capacity + position)
    rows_home = jnp.where(there, -1, line * capacity + position)
    orb_total = occ_energy.shape[0]
    global_orb = region * orb_count + orbs
    selector = global_orb[:, :, None] == jnp.arange(orb_total, dtype=jnp.int32)[None, None, :]
    offsets = jnp.sum(jnp.where(selector, fit_offset[None, None, :], 0), axis=2)
    occupied = jnp.sum(jnp.where(selector[0], occ_energy[None, :], 0.0), axis=1)
    occupied = occupied.reshape(pair_count, 2)
    denominator = (
        pno_energy[:, 0, :, None]
        + pno_energy[:, 1, None, :]
        - occupied[:, 0, None, None]
        - occupied[:, 1, None, None]
    )
    spans = chunk_spans(fit_rows)
    fitted, mirrored = [], []
    for k in range(2):
        fitted.append(
            jnp.dot(turned, raw_parts[k], preferred_element_type=jnp.float32).astype(jnp.bfloat16)
        )
        if k == 0:
            mirrored.append(across(fitted[0], group))
        else:
            for begin, size in spans:
                mirrored.append(across(fitted[1][begin : begin + size], group))

    def hop(outs):
        return [outs[0]] + [across(outs[i], i) for i in range(1, inner)]

    def project_far(c, tokens):
        begin, size = spans[c]
        parts = project(
            blocks,
            1,
            [mirrored[0], mirrored[1 + c]],
            [(begin, 0, half), (0, half, half)],
            size,
            tokens,
        )
        return hop(parts)

    def pass_on(c, before, tokens):
        sent, here = relay(rows, offsets, before, near, far[c], spans[c], margin, tokens)
        return across(sent, inner), here

    near = project(
        blocks,
        0,
        fitted,
        [(0, 0, half), (0, half, half)],
        fit_rows,
        [denominator, rows, rows_home, offsets],
    )
    near = hop(near)
    far, others = [None] * 3, [None] * 3
    far[0] = project_far(0, [])
    others[0], here = pass_on(0, jnp.zeros((8, 128), jnp.float32), [])
    far[1] = project_far(1, [here])
    far[2] = project_far(2, [far[1][0]])
    others[1], here = pass_on(1, here, [far[2][0]])
    others[2], here = pass_on(2, here, [])
    there = across(here[1], inner)
    body = mixed(
        rows_home, offsets, near, far[0] + far[1], others[:2], spans[:2], margin, [here], []
    )
    amplitude, energy = mixed(
        rows_home,
        offsets,
        near,
        far[2],
        others[2:],
        spans[2:],
        margin,
        [],
        [here, there, body, denominator],
    )
    return (amplitude.reshape(pair_count, pno_count * pno_count), energy.reshape(pair_count))


def solution(mesh):
    return jax.shard_map(
        on_device,
        mesh=mesh,
        in_specs=(
            P(None, "orb", "aux", None),
            P(("aux", "orb"), None, None),
            P(("aux", "orb"), None),
            P(("aux", "orb"), None, None, None),
            P(("aux", "orb"), None, None),
            P(),
            P(),
        ),
        out_specs=(P(("aux", "orb"), None), P(("aux", "orb"))),
        check_vma=False,
    )
```

```python
import functools

import jax
import jax.numpy as jnp
from jax import lax
from jax.experimental import pallas as pl
from jax.experimental.pallas import tpu as pltpu
from jax.sharding import PartitionSpec as P

SMEM = pl.BlockSpec(memory_space=pltpu.SMEM)
VMEM = pl.BlockSpec(memory_space=pltpu.VMEM)
ANY = pl.BlockSpec(memory_space=pl.ANY)


def copy(source, target, sem):
    return pltpu.make_async_copy(source, target, sem)


def pack_kernel(group, capacity, orbs, place, coef, *refs):
    outs, (held, count, holder, load_sem, store_sem) = refs[:-5], refs[-5:]
    load = copy(coef, held, load_sem)
    load.start()

    def clear(i, carry):
        holder[i] = 0
        return carry

    def clear_count(i, carry):
        count[i] = 0
        return carry

    def assign(s, carry):
        orb = orbs[s]
        at = count[orb]
        holder[orb * capacity + at] = s
        count[orb] = at + 1
        return carry

    lax.fori_loop(0, 2 * group * capacity, clear, 0)
    lax.fori_loop(0, 2 * group, clear_count, 0)
    lax.fori_loop(0, held.shape[0], assign, 0)
    load.wait()
    for mask, out in enumerate(outs):
        for kind in range(2):
            orb = place[1] ^ mask ^ (kind * (group + group // 2))

            def send(k, carry, orb=orb, kind=kind, out=out, sem=store_sem.at[mask]):
                copy(held.at[holder[orb * capacity + k]], out.at[kind * capacity + k], sem).start()
                return carry

            lax.fori_loop(0, capacity, send, 0)
    for mask, out in enumerate(outs):
        copy(held.at[pl.ds(0, 2 * capacity)], out, store_sem.at[mask]).wait()


def pack(orbs, place, coef, group, capacity):
    side_count, pno_count, dom_count = coef.shape
    block = jax.ShapeDtypeStruct((2 * capacity, pno_count, dom_count), coef.dtype)
    return pl.pallas_call(
        functools.partial(pack_kernel, group, capacity),
        out_shape=(block,) * group,
        in_specs=[SMEM, SMEM, ANY],
        out_specs=(ANY,) * group,
        scratch_shapes=[
            pltpu.VMEM(coef.shape, coef.dtype),
            pltpu.SMEM((2 * group,), jnp.int32),
            pltpu.SMEM((2 * group * capacity,), jnp.int32),
            pltpu.SemaphoreType.DMA,
            pltpu.SemaphoreType.DMA((group,)),
        ],
        cost_estimate=pl.CostEstimate(
            flops=0, transcendentals=0, bytes_accessed=6 * side_count * pno_count * dom_count
        ),
        name="pack",
    )(orbs, place, coef)


def project_kernel(group, capacity, kind, pieces, place, *refs):
    inner = group // 2
    blocks, parts = refs[:group], refs[group : group + len(pieces)]
    outs, (left, right, made, left_sem, right_sem, out_sem) = refs[-6 - inner : -6], refs[-6:]
    row_count = right.shape[0]
    _, pno_count, dom_count = left.shape
    lines = 2 * capacity
    plane = place[1] // inner
    at_end = (plane == 0) | (plane == 3)
    for part, (row, column, width, end) in zip(parts, pieces):

        @pl.when(at_end == end if kind else plane >= 0)
        def _(part=part, row=row, column=column, width=width):
            copy(
                part.at[pl.ds(row, row_count)], right.at[:, pl.ds(column, width)], right_sem
            ).start()

    for i in range(inner):
        for j in range(2):
            copy(
                blocks[i + j * inner].at[pl.ds(kind * capacity, capacity)],
                left.at[pl.ds(i * lines + j * capacity, capacity)],
                left_sem.at[i],
            ).start()
    copy(right, right, right_sem).wait()
    step = row_count if row_count <= 512 else 256
    for i in range(inner):
        mine = left.at[pl.ds(i * lines, lines)]
        copy(mine, mine, left_sem.at[i]).wait()

        def tile(t, carry, i=i, mine=mine):
            at = t * step if isinstance(t, int) else pl.multiple_of(t * step, step)
            product = lax.dot_general(
                mine[...].reshape(lines * pno_count, dom_count),
                right[pl.ds(at, step), :],
                (((1,), (1,)), ((), ())),
                preferred_element_type=jnp.float32,
            )
            made[i, :, :, pl.ds(at, step)] = product.astype(made.dtype).reshape(
                lines, pno_count, step
            )
            return carry

        if row_count == step:
            tile(0, 0)
        else:
            lax.fori_loop(0, row_count // step, tile, 0)
        copy(made.at[i], outs[i], out_sem).start()
    for i in range(inner):
        copy(made.at[i], outs[i], out_sem).wait()


def project(place, blocks, kind, parts, pieces, row_count, tokens):
    group = len(blocks)
    inner = group // 2
    slots, pno_count, dom_count = blocks[0].shape
    capacity = slots // 2
    dtype = blocks[0].dtype
    out = jax.ShapeDtypeStruct((slots, pno_count, row_count), dtype)
    return pl.pallas_call(
        functools.partial(project_kernel, group, capacity, kind, tuple(pieces)),
        out_shape=(out,) * inner,
        in_specs=[SMEM] + [ANY] * (group + len(parts) + len(tokens)),
        out_specs=(ANY,) * inner,
        scratch_shapes=[
            pltpu.VMEM((group * capacity, pno_count, dom_count), dtype),
            pltpu.VMEM((row_count, dom_count), dtype),
            pltpu.VMEM((inner, slots, pno_count, row_count), dtype),
            pltpu.SemaphoreType.DMA((inner,)),
            pltpu.SemaphoreType.DMA,
            pltpu.SemaphoreType.DMA,
        ],
        compiler_params=pltpu.CompilerParams(vmem_limit_bytes=24 << 20),
        cost_estimate=pl.CostEstimate(
            flops=2 * group * capacity * pno_count * dom_count * row_count,
            transcendentals=0,
            bytes_accessed=2 * group * capacity * pno_count * dom_count,
        ),
    )(place, *blocks, *parts, *tokens)


def gather_sides(near, far, spans, slots, held, sem):
    inner = len(near)
    low, width = spans[0][0], sum(size for _, size in spans)
    for i in range(inner):
        copy(
            near[i].at[pl.ds(0, slots), :, pl.ds(low, width)],
            held.at[pl.ds(i * slots, slots)],
            sem,
        ).start()
        for c, (begin, size) in enumerate(spans):
            copy(
                far[c * inner + i].at[pl.ds(0, slots)],
                held.at[pl.ds((inner + i) * slots, slots), :, pl.ds(begin - low, size)],
                sem,
            ).start()


def overlap(first, second, limits, low):
    if low < limits[2]:
        lane = lax.broadcasted_iota(jnp.int32, (1, second.shape[1]), 1) + low
        apart = (lane < limits[0]) != (lane < limits[1])
        second = second * jnp.where(apart, 0.0, 1.0).astype(second.dtype)
    return lax.dot_general(
        first, second, (((1,), (1,)), ((), ())), preferred_element_type=jnp.float32
    )


def relay_kernel(inner, spans, margin, rows, offsets, before, *refs):
    near, far = refs[:inner], refs[inner : 2 * inner]
    sent, coupling, held, sem = refs[-4:]
    low = spans[0][0]
    pair_count = sent.shape[0]
    gather_sides(near, far, spans, near[0].shape[0], held, sem)
    copy(held, held, sem).wait()

    def choose(n, carry):
        sent[n] = held[jnp.maximum(jnp.maximum(rows[1, 2 * n], rows[1, 2 * n + 1]), 0)]
        return carry

    lax.fori_loop(0, pair_count, choose, 0, unroll=4)
    for h in range(2):

        def one_pair(n, carry, h=h):
            first, second = rows[h, 2 * n], rows[h, 2 * n + 1]
            product = overlap(
                held[jnp.maximum(first, 0)],
                held[jnp.maximum(second, 0)],
                (offsets[h, 2 * n], offsets[h, 2 * n + 1], margin),
                low,
            )
            product = jnp.where((first >= 0) & (second >= 0), product, 0.0)
            coupling[h, n] = product if low == 0 else product + before[h, n]
            return carry

        lax.fori_loop(0, pair_count, one_pair, 0, unroll=4)


def relay(rows, offsets, before, near, far, span, margin, tokens):
    inner = len(near)
    slots, pno_count, _ = near[0].shape
    pair_count = rows.shape[1] // 2
    return pl.pallas_call(
        functools.partial(relay_kernel, inner, (span,), margin),
        out_shape=(
            jax.ShapeDtypeStruct((pair_count, pno_count, span[1]), near[0].dtype),
            jax.ShapeDtypeStruct((2, pair_count, pno_count, pno_count), jnp.float32),
        ),
        in_specs=[SMEM, SMEM, VMEM] + [ANY] * (len(near) + len(far) + len(tokens)),
        out_specs=(VMEM, VMEM),
        scratch_shapes=[
            pltpu.VMEM((2 * inner * slots, pno_count, span[1]), near[0].dtype),
            pltpu.SemaphoreType.DMA,
        ],
        compiler_params=pltpu.CompilerParams(vmem_limit_bytes=24 << 20),
    )(rows, offsets, before, *near, *far, *tokens)


def mixed_pairs(inner, spans, margin, rows, offsets, near, far, others, held, sem, write):
    low = spans[0][0]
    slots = near[0].shape[0] // 2
    pair_count = others[0].shape[0]
    at = 2 * inner * slots
    gather_sides(near, far, spans, slots, held, sem)
    for other, (begin, size) in zip(others, spans):
        copy(
            other, held.at[pl.ds(at, pair_count), :, pl.ds(begin - low, size)], sem
        ).start()
    copy(held, held, sem).wait()

    def one_pair(n, carry):
        first, second = rows[0, 2 * n], rows[0, 2 * n + 1]
        product = overlap(
            held[jnp.where(first >= 0, first, at + n)],
            held[jnp.where(second >= 0, second, at + n)],
            (offsets[0, 2 * n], offsets[0, 2 * n + 1], margin),
            low,
        )
        write(n, jnp.where((first >= 0) != (second >= 0), product, 0.0))
        return carry

    lax.fori_loop(0, pair_count, one_pair, 0, unroll=4)


def mixed_kernel(inner, spans, margin, rows, offsets, *refs):
    near, refs = refs[:inner], refs[inner:]
    far, refs = refs[: inner * len(spans)], refs[inner * len(spans) :]
    others = refs[: len(spans)]
    coupling, held, sem = refs[-3:]

    def write(n, product):
        coupling[n] = product

    mixed_pairs(inner, spans, margin, rows, offsets, near, far, others, held, sem, write)


def finish_kernel(inner, spans, margin, rows, offsets, here, there, before, denominator, *refs):
    near, refs = refs[:inner], refs[inner:]
    far, refs = refs[: inner * len(spans)], refs[inner * len(spans) :]
    others = refs[: len(spans)]
    amplitude, energy, coupling, held, sem = refs[-5:]

    def write(n, product):
        coupling[n] = product

    mixed_pairs(inner, spans, margin, rows, offsets, near, far, others, held, sem, write)
    total = coupling[...] + before[...] + here[0] + there[...]
    result = -total / denominator[...]
    amplitude[...] = result
    parts = total * (2.0 * result - jnp.swapaxes(result, 1, 2))
    energy[...] = jnp.sum(jnp.sum(parts, axis=1), axis=1, keepdims=True)


def mixed(rows, offsets, near, far, others, spans, margin, tokens, finals):
    inner = len(near)
    slots, pno_count, _ = near[0].shape
    pair_count = rows.shape[1] // 2
    width = sum(size for _, size in spans)
    square = jax.ShapeDtypeStruct((pair_count, pno_count, pno_count), jnp.float32)
    line = jax.ShapeDtypeStruct((pair_count, 1), jnp.float32)
    scratch = [
        pltpu.VMEM((inner * slots + pair_count, pno_count, width), near[0].dtype),
        pltpu.SemaphoreType.DMA,
    ]
    if finals:
        scratch = [pltpu.VMEM(square.shape, jnp.float32)] + scratch
    return pl.pallas_call(
        functools.partial(
            finish_kernel if finals else mixed_kernel, inner, tuple(spans), margin
        ),
        out_shape=(square, line) if finals else square,
        in_specs=[SMEM] * 2
        + [VMEM] * len(finals)
        + [ANY] * (len(near) + len(far) + len(others) + len(tokens)),
        out_specs=(VMEM, VMEM) if finals else VMEM,
        scratch_shapes=scratch,
        compiler_params=pltpu.CompilerParams(vmem_limit_bytes=24 << 20),
    )(rows, offsets, *finals, *near, *far, *others, *tokens)


def slots_of(orbs):
    sequence = jnp.arange(orbs.shape[1], dtype=jnp.int32)
    same = orbs[:, :, None] == orbs[:, None, :]
    earlier = sequence[None, None, :] < sequence[None, :, None]
    return jnp.sum(jnp.where(same & earlier, 1, 0), axis=2).astype(jnp.int32)


def chunk_spans(fit_rows):
    sizes = (fit_rows // 2, 3 * fit_rows // 8, fit_rows // 8)
    return [(sum(sizes[:c]), size) for c, size in enumerate(sizes)]


def on_device(raw_ints, fit_inverse, pair_orbs, pno_coef, pno_energy, occ_energy, fit_offset):
    orb_count = lax.axis_size("orb")
    region, me = lax.axis_index("aux"), lax.axis_index("orb")
    group = orb_count // 2
    inner = group // 2
    pair_count = pair_orbs.shape[0]
    pno_count, dom_count = pno_coef.shape[2:]
    side_count = 2 * pair_count
    capacity = max(2, 4 * pair_count // orb_count)
    fit_rows = fit_inverse.shape[1]
    margin = fit_rows // 4

    def across(array, mask):
        return lax.ppermute(array, "orb", [(i, i ^ mask) for i in range(orb_count)])

    own_orbs = pair_orbs.reshape(side_count)
    mate_orbs = across(own_orbs, inner)
    place = jnp.stack([region, me]).astype(jnp.int32)
    half = dom_count // 2

    def exchange(array, k):
        part = lax.all_to_all(
            array[:, :, :, k * half : (k + 1) * half],
            "aux",
            split_axis=0,
            concat_axis=2,
            tiled=True,
        )
        return part[0, 0]

    raw_parts = [exchange(raw_ints, 0)]
    packed = pack(
        own_orbs, place, pno_coef.reshape(side_count, pno_count, dom_count), group, capacity
    )
    later, packed = lax.optimization_barrier((raw_ints, packed))
    raw_parts.append(exchange(later, 1))
    blocks = [packed[0]]
    for m in range(1, group):
        blocks.append(across(packed[m], m))
    own_offset = fit_offset[region * orb_count + me]
    turned = lax.optimization_barrier(jnp.roll(fit_inverse[0], own_offset, axis=0))
    orbs = jnp.stack([own_orbs, mate_orbs])
    differs = orbs ^ me
    other_half = (differs & group) != 0
    line = jnp.where(other_half, inner, 0) + (differs & (inner - 1))
    home = jnp.arange(2, dtype=jnp.int32)[:, None]
    position = slots_of(orbs)
    there = ((differs & inner) != 0) != other_half
    rows = jnp.where(there, -1, line * 2 * capacity + home * capacity + position)
    rows_home = jnp.where(there, -1, line * capacity + position)
    orb_total = occ_energy.shape[0]
    global_orb = region * orb_count + orbs
    selector = global_orb[:, :, None] == jnp.arange(orb_total, dtype=jnp.int32)[None, None, :]
    offsets = jnp.sum(jnp.where(selector, fit_offset[None, None, :], 0), axis=2)
    occupied = jnp.sum(jnp.where(selector[0], occ_energy[None, :], 0.0), axis=1)
    occupied = occupied.reshape(pair_count, 2)
    denominator = (
        pno_energy[:, 0, :, None]
        + pno_energy[:, 1, None, :]
        - occupied[:, 0, None, None]
        - occupied[:, 1, None, None]
    )
    spans = chunk_spans(fit_rows)
    reverse = group + inner
    ends = [(i, i ^ reverse) for i in range(orb_count) if i // inner in (0, 3)]
    middles = [(i, i ^ reverse) for i in range(orb_count) if i // inner in (1, 2)]
    fitted, mirrored = [], []
    for k in range(2):
        fitted.append(
            jnp.dot(turned, raw_parts[k], preferred_element_type=jnp.float32).astype(jnp.bfloat16)
        )
        mirrored.append(lax.ppermute(fitted[k], "orb", middles))
    for begin, size in spans:
        chunk = jnp.concatenate([part[begin : begin + size] for part in fitted], axis=1)
        mirrored.append(lax.ppermute(chunk, "orb", ends))

    def hop(outs):
        return [outs[0]] + [across(outs[i], i) for i in range(1, inner)]

    def project_far(c, tokens):
        begin, size = spans[c]
        parts = project(
            place,
            blocks,
            1,
            [mirrored[0], mirrored[1], mirrored[2 + c]],
            [(begin, 0, half, False), (begin, half, half, False), (0, 0, dom_count, True)],
            size,
            tokens,
        )
        return hop(parts)

    def pass_on(c, before, tokens):
        sent, here = relay(rows, offsets, before, near, far[c], spans[c], margin, tokens)
        return across(sent, inner), here

    near = project(
        place,
        blocks,
        0,
        fitted,
        [(0, 0, half, False), (0, half, half, False)],
        fit_rows,
        [denominator],
    )
    near = hop(near)
    far, others = [None] * 3, [None] * 3
    far[0] = project_far(0, [rows, rows_home, offsets])
    others[0], here = pass_on(0, jnp.zeros((8, 128), jnp.float32), [])
    far[1] = project_far(1, [here])
    far[2] = project_far(2, [far[1][0]])
    others[1], here = pass_on(1, here, [far[2][0]])
    others[2], here = pass_on(2, here, [])
    there = across(here[1], inner)
    body = mixed(
        rows_home, offsets, near, far[0] + far[1], others[:2], spans[:2], margin, [here], []
    )
    amplitude, energy = mixed(
        rows_home,
        offsets,
        near,
        far[2],
        others[2:],
        spans[2:],
        margin,
        [],
        [here, there, body, denominator],
    )
    return (amplitude.reshape(pair_count, pno_count * pno_count), energy.reshape(pair_count))


def solution(mesh):
    return jax.shard_map(
        on_device,
        mesh=mesh,
        in_specs=(
            P(None, "orb", "aux", None),
            P(("aux", "orb"), None, None),
            P(("aux", "orb"), None),
            P(("aux", "orb"), None, None, None),
            P(("aux", "orb"), None, None),
            P(),
            P(),
        ),
        out_specs=(P(("aux", "orb"), None), P(("aux", "orb"))),
        check_vma=False,
    )
```

```python
import functools

import jax
import jax.numpy as jnp
from jax import lax
from jax.experimental import pallas as pl
from jax.experimental.pallas import tpu as pltpu
from jax.sharding import PartitionSpec as P

SMEM = pl.BlockSpec(memory_space=pltpu.SMEM)
VMEM = pl.BlockSpec(memory_space=pltpu.VMEM)
ANY = pl.BlockSpec(memory_space=pl.ANY)


def copy(source, target, sem):
    return pltpu.make_async_copy(source, target, sem)


def pack_kernel(group, capacity, orbs, place, coef, *refs):
    outs, (held, count, holder, load_sem, store_sem) = refs[:-5], refs[-5:]
    load = copy(coef, held, load_sem)
    load.start()

    def clear(i, carry):
        holder[i] = 0
        return carry

    def clear_count(i, carry):
        count[i] = 0
        return carry

    def assign(s, carry):
        orb = orbs[s]
        at = count[orb]
        holder[orb * capacity + at] = s
        count[orb] = at + 1
        return carry

    lax.fori_loop(0, 2 * group * capacity, clear, 0)
    lax.fori_loop(0, 2 * group, clear_count, 0)
    lax.fori_loop(0, held.shape[0], assign, 0)
    load.wait()
    for mask, out in enumerate(outs):
        for kind in range(2):
            orb = place[1] ^ mask ^ (kind * (group + group // 2))

            def send(k, carry, orb=orb, kind=kind, out=out, sem=store_sem.at[mask]):
                copy(held.at[holder[orb * capacity + k]], out.at[kind * capacity + k], sem).start()
                return carry

            lax.fori_loop(0, capacity, send, 0)
    for mask, out in enumerate(outs):
        copy(held.at[pl.ds(0, 2 * capacity)], out, store_sem.at[mask]).wait()


def pack(orbs, place, coef, group, capacity):
    side_count, pno_count, dom_count = coef.shape
    block = jax.ShapeDtypeStruct((2 * capacity, pno_count, dom_count), coef.dtype)
    return pl.pallas_call(
        functools.partial(pack_kernel, group, capacity),
        out_shape=(block,) * group,
        in_specs=[SMEM, SMEM, ANY],
        out_specs=(ANY,) * group,
        scratch_shapes=[
            pltpu.VMEM(coef.shape, coef.dtype),
            pltpu.SMEM((2 * group,), jnp.int32),
            pltpu.SMEM((2 * group * capacity,), jnp.int32),
            pltpu.SemaphoreType.DMA,
            pltpu.SemaphoreType.DMA((group,)),
        ],
        cost_estimate=pl.CostEstimate(
            flops=0, transcendentals=0, bytes_accessed=6 * side_count * pno_count * dom_count
        ),
        name="pack",
    )(orbs, place, coef)


def project_kernel(group, capacity, kind, pieces, place, *refs):
    inner = group // 2
    blocks, parts = refs[:group], refs[group : group + len(pieces)]
    outs, (left, right, made, left_sem, right_sem, out_sem) = refs[-6 - inner : -6], refs[-6:]
    row_count = right.shape[0]
    _, pno_count, dom_count = left.shape
    lines = 2 * capacity
    plane = place[1] // inner
    at_end = (plane == 0) | (plane == 3)
    for part, (row, column, width, end) in zip(parts, pieces):

        @pl.when(at_end == end if kind else plane >= 0)
        def _(part=part, row=row, column=column, width=width):
            copy(
                part.at[pl.ds(row, row_count)], right.at[:, pl.ds(column, width)], right_sem
            ).start()

    for i in range(inner):
        for j in range(2):
            copy(
                blocks[i + j * inner].at[pl.ds(kind * capacity, capacity)],
                left.at[pl.ds(i * lines + j * capacity, capacity)],
                left_sem.at[i],
            ).start()
    copy(right, right, right_sem).wait()
    step = row_count if row_count <= 512 else 256
    for i in range(inner):
        mine = left.at[pl.ds(i * lines, lines)]
        copy(mine, mine, left_sem.at[i]).wait()

        def tile(t, carry, i=i, mine=mine):
            at = t * step if isinstance(t, int) else pl.multiple_of(t * step, step)
            product = lax.dot_general(
                mine[...].reshape(lines * pno_count, dom_count),
                right[pl.ds(at, step), :],
                (((1,), (1,)), ((), ())),
                preferred_element_type=jnp.float32,
            )
            made[i, :, :, pl.ds(at, step)] = product.astype(made.dtype).reshape(
                lines, pno_count, step
            )
            return carry

        if row_count == step:
            tile(0, 0)
        else:
            lax.fori_loop(0, row_count // step, tile, 0)
        copy(made.at[i], outs[i], out_sem).start()
    for i in range(inner):
        copy(made.at[i], outs[i], out_sem).wait()


def project(place, blocks, kind, parts, pieces, row_count, tokens):
    group = len(blocks)
    inner = group // 2
    slots, pno_count, dom_count = blocks[0].shape
    capacity = slots // 2
    dtype = blocks[0].dtype
    out = jax.ShapeDtypeStruct((slots, pno_count, row_count), dtype)
    return pl.pallas_call(
        functools.partial(project_kernel, group, capacity, kind, tuple(pieces)),
        out_shape=(out,) * inner,
        in_specs=[SMEM] + [ANY] * (group + len(parts) + len(tokens)),
        out_specs=(ANY,) * inner,
        scratch_shapes=[
            pltpu.VMEM((group * capacity, pno_count, dom_count), dtype),
            pltpu.VMEM((row_count, dom_count), dtype),
            pltpu.VMEM((inner, slots, pno_count, row_count), dtype),
            pltpu.SemaphoreType.DMA((inner,)),
            pltpu.SemaphoreType.DMA,
            pltpu.SemaphoreType.DMA,
        ],
        compiler_params=pltpu.CompilerParams(vmem_limit_bytes=24 << 20),
        cost_estimate=pl.CostEstimate(
            flops=2 * group * capacity * pno_count * dom_count * row_count,
            transcendentals=0,
            bytes_accessed=2 * group * capacity * pno_count * dom_count,
        ),
    )(place, *blocks, *parts, *tokens)


def gather_sides(near, far, spans, slots, held, sem):
    inner = len(near)
    low, width = spans[0][0], sum(size for _, size in spans)
    for i in range(inner):
        copy(
            near[i].at[pl.ds(0, slots), :, pl.ds(low, width)],
            held.at[pl.ds(i * slots, slots)],
            sem,
        ).start()
        for c, (begin, size) in enumerate(spans):
            copy(
                far[c * inner + i].at[pl.ds(0, slots)],
                held.at[pl.ds((inner + i) * slots, slots), :, pl.ds(begin - low, size)],
                sem,
            ).start()


def overlap(first, second, limits, low):
    if low < limits[2]:
        lane = lax.broadcasted_iota(jnp.int32, (1, second.shape[1]), 1) + low
        apart = (lane < limits[0]) != (lane < limits[1])
        second = second * jnp.where(apart, 0.0, 1.0).astype(second.dtype)
    return lax.dot_general(
        first, second, (((1,), (1,)), ((), ())), preferred_element_type=jnp.float32
    )


def relay_kernel(inner, spans, margin, rows, offsets, before, *refs):
    near, far = refs[:inner], refs[inner : 2 * inner]
    sent, coupling, held, sem = refs[-4:]
    low = spans[0][0]
    pair_count = sent.shape[0]
    gather_sides(near, far, spans, near[0].shape[0], held, sem)
    copy(held, held, sem).wait()

    def choose(n, carry):
        sent[n] = held[jnp.maximum(jnp.maximum(rows[1, 2 * n], rows[1, 2 * n + 1]), 0)]
        return carry

    lax.fori_loop(0, pair_count, choose, 0, unroll=4)
    for h in range(2):

        def one_pair(n, carry, h=h):
            first, second = rows[h, 2 * n], rows[h, 2 * n + 1]
            product = overlap(
                held[jnp.maximum(first, 0)],
                held[jnp.maximum(second, 0)],
                (offsets[h, 2 * n], offsets[h, 2 * n + 1], margin),
                low,
            )
            product = jnp.where((first >= 0) & (second >= 0), product, 0.0)
            coupling[h, n] = product if low == 0 else product + before[h, n]
            return carry

        lax.fori_loop(0, pair_count, one_pair, 0, unroll=4)


def relay(rows, offsets, before, near, far, span, margin, tokens):
    inner = len(near)
    slots, pno_count, _ = near[0].shape
    pair_count = rows.shape[1] // 2
    return pl.pallas_call(
        functools.partial(relay_kernel, inner, (span,), margin),
        out_shape=(
            jax.ShapeDtypeStruct((pair_count, pno_count, span[1]), near[0].dtype),
            jax.ShapeDtypeStruct((2, pair_count, pno_count, pno_count), jnp.float32),
        ),
        in_specs=[SMEM, SMEM, VMEM] + [ANY] * (len(near) + len(far) + len(tokens)),
        out_specs=(VMEM, VMEM),
        scratch_shapes=[
            pltpu.VMEM((2 * inner * slots, pno_count, span[1]), near[0].dtype),
            pltpu.SemaphoreType.DMA,
        ],
        compiler_params=pltpu.CompilerParams(vmem_limit_bytes=24 << 20),
    )(rows, offsets, before, *near, *far, *tokens)


def mixed_pairs(inner, spans, margin, rows, offsets, near, far, others, held, sem, write):
    low = spans[0][0]
    slots = near[0].shape[0] // 2
    pair_count = others[0].shape[0]
    at = 2 * inner * slots
    gather_sides(near, far, spans, slots, held, sem)
    for other, (begin, size) in zip(others, spans):
        copy(
            other, held.at[pl.ds(at, pair_count), :, pl.ds(begin - low, size)], sem
        ).start()
    copy(held, held, sem).wait()

    def one_pair(n, carry):
        first, second = rows[0, 2 * n], rows[0, 2 * n + 1]
        product = overlap(
            held[jnp.where(first >= 0, first, at + n)],
            held[jnp.where(second >= 0, second, at + n)],
            (offsets[0, 2 * n], offsets[0, 2 * n + 1], margin),
            low,
        )
        write(n, jnp.where((first >= 0) != (second >= 0), product, 0.0))
        return carry

    lax.fori_loop(0, pair_count, one_pair, 0, unroll=4)


def mixed_kernel(inner, spans, margin, rows, offsets, *refs):
    near, refs = refs[:inner], refs[inner:]
    far, refs = refs[: inner * len(spans)], refs[inner * len(spans) :]
    others = refs[: len(spans)]
    coupling, held, sem = refs[-3:]

    def write(n, product):
        coupling[n] = product

    mixed_pairs(inner, spans, margin, rows, offsets, near, far, others, held, sem, write)


def finish_kernel(inner, spans, margin, rows, offsets, here, there, before, denominator, *refs):
    near, refs = refs[:inner], refs[inner:]
    far, refs = refs[: inner * len(spans)], refs[inner * len(spans) :]
    others = refs[: len(spans)]
    amplitude, energy, coupling, held, sem = refs[-5:]

    def write(n, product):
        coupling[n] = product

    mixed_pairs(inner, spans, margin, rows, offsets, near, far, others, held, sem, write)
    total = coupling[...] + before[...] + here[0] + there[...]
    result = -total / denominator[...]
    amplitude[...] = result
    parts = total * (2.0 * result - jnp.swapaxes(result, 1, 2))
    energy[...] = jnp.sum(jnp.sum(parts, axis=1), axis=1, keepdims=True)


def mixed(rows, offsets, near, far, others, spans, margin, tokens, finals):
    inner = len(near)
    slots, pno_count, _ = near[0].shape
    pair_count = rows.shape[1] // 2
    width = sum(size for _, size in spans)
    square = jax.ShapeDtypeStruct((pair_count, pno_count, pno_count), jnp.float32)
    line = jax.ShapeDtypeStruct((pair_count, 1), jnp.float32)
    scratch = [
        pltpu.VMEM((inner * slots + pair_count, pno_count, width), near[0].dtype),
        pltpu.SemaphoreType.DMA,
    ]
    if finals:
        scratch = [pltpu.VMEM(square.shape, jnp.float32)] + scratch
    return pl.pallas_call(
        functools.partial(
            finish_kernel if finals else mixed_kernel, inner, tuple(spans), margin
        ),
        out_shape=(square, line) if finals else square,
        in_specs=[SMEM] * 2
        + [VMEM] * len(finals)
        + [ANY] * (len(near) + len(far) + len(others) + len(tokens)),
        out_specs=(VMEM, VMEM) if finals else VMEM,
        scratch_shapes=scratch,
        compiler_params=pltpu.CompilerParams(vmem_limit_bytes=24 << 20),
    )(rows, offsets, *finals, *near, *far, *others, *tokens)


def slots_of(orbs):
    sequence = jnp.arange(orbs.shape[1], dtype=jnp.int32)
    same = orbs[:, :, None] == orbs[:, None, :]
    earlier = sequence[None, None, :] < sequence[None, :, None]
    return jnp.sum(jnp.where(same & earlier, 1, 0), axis=2).astype(jnp.int32)


def chunk_spans(fit_rows):
    sizes = (fit_rows // 2, 3 * fit_rows // 8, fit_rows // 8)
    return [(sum(sizes[:c]), size) for c, size in enumerate(sizes)]


def on_device(raw_ints, fit_inverse, pair_orbs, pno_coef, pno_energy, occ_energy, fit_offset):
    orb_count = lax.axis_size("orb")
    region, me = lax.axis_index("aux"), lax.axis_index("orb")
    group = orb_count // 2
    inner = group // 2
    pair_count = pair_orbs.shape[0]
    pno_count, dom_count = pno_coef.shape[2:]
    side_count = 2 * pair_count
    capacity = max(2, 4 * pair_count // orb_count)
    fit_rows = fit_inverse.shape[1]
    margin = fit_rows // 4

    def across(array, mask):
        return lax.ppermute(array, "orb", [(i, i ^ mask) for i in range(orb_count)])

    own_orbs = pair_orbs.reshape(side_count)
    place = jnp.stack([region, me]).astype(jnp.int32)
    half = dom_count // 2

    def exchange(array, k):
        part = lax.all_to_all(
            array[:, :, :, k * half : (k + 1) * half],
            "aux",
            split_axis=0,
            concat_axis=2,
            tiled=True,
        )
        return part[0, 0]

    raw_parts = [exchange(raw_ints, 0)]
    packed = pack(
        own_orbs, place, pno_coef.reshape(side_count, pno_count, dom_count), group, capacity
    )
    blocks = [packed[0]]
    for m in range(1, group):
        blocks.append(across(packed[m], m))
    own_offset = fit_offset[region * orb_count + me]
    turned = jnp.roll(fit_inverse[0], own_offset, axis=0)
    mate_orbs = across(own_orbs, inner)
    orb_total = occ_energy.shape[0]

    def pick(values, chosen):
        selector = (region * orb_count + chosen)[:, None] == jnp.arange(orb_total, dtype=jnp.int32)
        return jnp.sum(jnp.where(selector, values[None, :], 0), axis=1)

    occupied = pick(occ_energy, own_orbs).reshape(pair_count, 2)
    denominator = (
        pno_energy[:, 0, :, None]
        + pno_energy[:, 1, None, :]
        - occupied[:, 0, None, None]
        - occupied[:, 1, None, None]
    )
    spans = chunk_spans(fit_rows)
    reverse = group + inner
    ends = [(i, i ^ reverse) for i in range(orb_count) if i // inner in (0, 3)]
    middles = [(i, i ^ reverse) for i in range(orb_count) if i // inner in (1, 2)]
    fitted, mirrored = [], []
    for k in range(2):
        fitted.append(
            jnp.dot(turned, raw_parts[k], preferred_element_type=jnp.float32).astype(jnp.bfloat16)
        )
        mirrored.append(lax.ppermute(fitted[k], "orb", middles))
        if k == 0:
            later, fitted[0] = lax.optimization_barrier((raw_ints, fitted[0]))
            raw_parts.append(exchange(later, 1))
    for begin, size in spans:
        chunk = jnp.concatenate([part[begin : begin + size] for part in fitted], axis=1)
        mirrored.append(lax.ppermute(chunk, "orb", ends))

    def hop(outs):
        return [outs[0]] + [across(outs[i], i) for i in range(1, inner)]

    def project_far(c, tokens):
        begin, size = spans[c]
        parts = project(
            place,
            blocks,
            1,
            [mirrored[0], mirrored[1], mirrored[2 + c]],
            [(begin, 0, half, False), (begin, half, half, False), (0, 0, dom_count, True)],
            size,
            tokens,
        )
        return hop(parts)

    def pass_on(c, before, tokens):
        sent, here = relay(rows, offsets, before, near, far[c], spans[c], margin, tokens)
        return across(sent, inner), here

    near = project(
        place,
        blocks,
        0,
        fitted,
        [(0, 0, half, False), (0, half, half, False)],
        fit_rows,
        [denominator],
    )
    mate_orbs, *near = lax.optimization_barrier((mate_orbs, *near))
    near = hop(near)
    orbs = jnp.stack([own_orbs, mate_orbs])
    differs = orbs ^ me
    other_half = (differs & group) != 0
    line = jnp.where(other_half, inner, 0) + (differs & (inner - 1))
    home = jnp.arange(2, dtype=jnp.int32)[:, None]
    position = slots_of(orbs)
    there = ((differs & inner) != 0) != other_half
    rows = jnp.where(there, -1, line * 2 * capacity + home * capacity + position)
    rows_home = jnp.where(there, -1, line * capacity + position)
    offsets = pick(fit_offset, orbs.reshape(2 * side_count)).reshape(2, side_count)
    far, others = [None] * 3, [None] * 3
    far[0] = project_far(0, [rows, rows_home, offsets])
    others[0], here = pass_on(0, jnp.zeros((8, 128), jnp.float32), [])
    far[1] = project_far(1, [here])
    far[2] = project_far(2, [far[1][0]])
    others[1], here = pass_on(1, here, [far[2][0]])
    others[2], here = pass_on(2, here, [])
    there = across(here[1], inner)
    body = mixed(
        rows_home, offsets, near, far[0] + far[1], others[:2], spans[:2], margin, [here], []
    )
    amplitude, energy = mixed(
        rows_home,
        offsets,
        near,
        far[2],
        others[2:],
        spans[2:],
        margin,
        [],
        [here, there, body, denominator],
    )
    return (amplitude.reshape(pair_count, pno_count * pno_count), energy.reshape(pair_count))


def solution(mesh):
    return jax.shard_map(
        on_device,
        mesh=mesh,
        in_specs=(
            P(None, "orb", "aux", None),
            P(("aux", "orb"), None, None),
            P(("aux", "orb"), None),
            P(("aux", "orb"), None, None, None),
            P(("aux", "orb"), None, None),
            P(),
            P(),
        ),
        out_specs=(P(("aux", "orb"), None), P(("aux", "orb"))),
        check_vma=False,
    )
```

```python
import functools

import jax
import jax.numpy as jnp
from jax import lax
from jax.experimental import pallas as pl
from jax.experimental.pallas import tpu as pltpu
from jax.sharding import PartitionSpec as P

SMEM = pl.BlockSpec(memory_space=pltpu.SMEM)
VMEM = pl.BlockSpec(memory_space=pltpu.VMEM)
ANY = pl.BlockSpec(memory_space=pl.ANY)


def copy(source, target, sem):
    return pltpu.make_async_copy(source, target, sem)


def pack_kernel(group, capacity, orbs, place, coef, *refs):
    outs, (held, count, holder, load_sem, store_sem) = refs[:-5], refs[-5:]
    load = copy(coef, held, load_sem)
    load.start()

    def clear(i, carry):
        holder[i] = 0
        return carry

    def clear_count(i, carry):
        count[i] = 0
        return carry

    def assign(s, carry):
        orb = orbs[s]
        at = count[orb]
        holder[orb * capacity + at] = s
        count[orb] = at + 1
        return carry

    lax.fori_loop(0, 2 * group * capacity, clear, 0)
    lax.fori_loop(0, 2 * group, clear_count, 0)
    lax.fori_loop(0, held.shape[0], assign, 0)
    load.wait()
    for mask, out in enumerate(outs):
        for kind in range(2):
            orb = place[1] ^ mask ^ (kind * (group + group // 2))

            def send(k, carry, orb=orb, kind=kind, out=out, sem=store_sem.at[mask]):
                copy(held.at[holder[orb * capacity + k]], out.at[kind * capacity + k], sem).start()
                return carry

            lax.fori_loop(0, capacity, send, 0)
    for mask, out in enumerate(outs):
        copy(held.at[pl.ds(0, 2 * capacity)], out, store_sem.at[mask]).wait()


def pack(orbs, place, coef, group, capacity):
    side_count, pno_count, dom_count = coef.shape
    block = jax.ShapeDtypeStruct((2 * capacity, pno_count, dom_count), coef.dtype)
    return pl.pallas_call(
        functools.partial(pack_kernel, group, capacity),
        out_shape=(block,) * group,
        in_specs=[SMEM, SMEM, ANY],
        out_specs=(ANY,) * group,
        scratch_shapes=[
            pltpu.VMEM(coef.shape, coef.dtype),
            pltpu.SMEM((2 * group,), jnp.int32),
            pltpu.SMEM((2 * group * capacity,), jnp.int32),
            pltpu.SemaphoreType.DMA,
            pltpu.SemaphoreType.DMA((group,)),
        ],
        cost_estimate=pl.CostEstimate(
            flops=0, transcendentals=0, bytes_accessed=6 * side_count * pno_count * dom_count
        ),
        name="pack",
    )(orbs, place, coef)


def project_kernel(group, capacity, kind, pieces, place, *refs):
    inner = group // 2
    blocks, parts = refs[:group], refs[group : group + len(pieces)]
    outs, (left, right, made, left_sem, right_sem, out_sem) = refs[-6 - inner : -6], refs[-6:]
    row_count = right.shape[0]
    _, pno_count, dom_count = left.shape
    lines = 2 * capacity
    plane = place[1] // inner
    at_end = (plane == 0) | (plane == 3)
    for part, (row, column, width, end) in zip(parts, pieces):

        @pl.when((plane >= 0) if end is None else (at_end == end))
        def _(part=part, row=row, column=column, width=width):
            copy(
                part.at[pl.ds(row, row_count)], right.at[:, pl.ds(column, width)], right_sem
            ).start()

    for i in range(inner):
        for j in range(2):
            copy(
                blocks[i + j * inner].at[pl.ds(kind * capacity, capacity)],
                left.at[pl.ds(i * lines + j * capacity, capacity)],
                left_sem.at[i],
            ).start()
    copy(right, right, right_sem).wait()
    step = row_count if row_count <= 512 else 256
    for i in range(inner):
        mine = left.at[pl.ds(i * lines, lines)]
        copy(mine, mine, left_sem.at[i]).wait()

        def tile(t, carry, i=i, mine=mine):
            at = t * step if isinstance(t, int) else pl.multiple_of(t * step, step)
            product = lax.dot_general(
                mine[...].reshape(lines * pno_count, dom_count),
                right[pl.ds(at, step), :],
                (((1,), (1,)), ((), ())),
                preferred_element_type=jnp.float32,
            )
            made[i, :, :, pl.ds(at, step)] = product.astype(made.dtype).reshape(
                lines, pno_count, step
            )
            return carry

        if row_count == step:
            tile(0, 0)
        else:
            lax.fori_loop(0, row_count // step, tile, 0)
        copy(made.at[i], outs[i], out_sem).start()
    for i in range(inner):
        copy(made.at[i], outs[i], out_sem).wait()


def project(place, blocks, kind, parts, pieces, row_count, tokens):
    group = len(blocks)
    inner = group // 2
    slots, pno_count, dom_count = blocks[0].shape
    capacity = slots // 2
    dtype = blocks[0].dtype
    out = jax.ShapeDtypeStruct((slots, pno_count, row_count), dtype)
    return pl.pallas_call(
        functools.partial(project_kernel, group, capacity, kind, tuple(pieces)),
        out_shape=(out,) * inner,
        in_specs=[SMEM] + [ANY] * (group + len(parts) + len(tokens)),
        out_specs=(ANY,) * inner,
        scratch_shapes=[
            pltpu.VMEM((group * capacity, pno_count, dom_count), dtype),
            pltpu.VMEM((row_count, dom_count), dtype),
            pltpu.VMEM((inner, slots, pno_count, row_count), dtype),
            pltpu.SemaphoreType.DMA((inner,)),
            pltpu.SemaphoreType.DMA,
            pltpu.SemaphoreType.DMA,
        ],
        compiler_params=pltpu.CompilerParams(vmem_limit_bytes=24 << 20),
        cost_estimate=pl.CostEstimate(
            flops=2 * group * capacity * pno_count * dom_count * row_count,
            transcendentals=0,
            bytes_accessed=2 * group * capacity * pno_count * dom_count,
        ),
    )(place, *blocks, *parts, *tokens)


def gather_sides(near, far, spans, slots, held, sem):
    inner = len(near)
    low, width = spans[0][0], sum(size for _, size in spans)
    for i in range(inner):
        copy(
            near[i].at[pl.ds(0, slots), :, pl.ds(low, width)],
            held.at[pl.ds(i * slots, slots)],
            sem,
        ).start()
        for c, (begin, size) in enumerate(spans):
            copy(
                far[c * inner + i].at[pl.ds(0, slots)],
                held.at[pl.ds((inner + i) * slots, slots), :, pl.ds(begin - low, size)],
                sem,
            ).start()


def overlap(first, second, limits, low):
    if low < limits[2]:
        lane = lax.broadcasted_iota(jnp.int32, (1, second.shape[1]), 1) + low
        apart = (lane < limits[0]) != (lane < limits[1])
        second = second * jnp.where(apart, 0.0, 1.0).astype(second.dtype)
    return lax.dot_general(
        first, second, (((1,), (1,)), ((), ())), preferred_element_type=jnp.float32
    )


def relay_kernel(inner, spans, margin, rows, offsets, before, *refs):
    near, far = refs[:inner], refs[inner : 2 * inner]
    sent, coupling, held, sem = refs[-4:]
    low = spans[0][0]
    pair_count = sent.shape[0]
    gather_sides(near, far, spans, near[0].shape[0], held, sem)
    copy(held, held, sem).wait()

    def choose(n, carry):
        sent[n] = held[jnp.maximum(jnp.maximum(rows[1, 2 * n], rows[1, 2 * n + 1]), 0)]
        return carry

    lax.fori_loop(0, pair_count, choose, 0, unroll=4)
    for h in range(2):

        def one_pair(n, carry, h=h):
            first, second = rows[h, 2 * n], rows[h, 2 * n + 1]
            product = overlap(
                held[jnp.maximum(first, 0)],
                held[jnp.maximum(second, 0)],
                (offsets[h, 2 * n], offsets[h, 2 * n + 1], margin),
                low,
            )
            product = jnp.where((first >= 0) & (second >= 0), product, 0.0)
            coupling[h, n] = product if low == 0 else product + before[h, n]
            return carry

        lax.fori_loop(0, pair_count, one_pair, 0, unroll=4)


def relay(rows, offsets, before, near, far, span, margin, tokens):
    inner = len(near)
    slots, pno_count, _ = near[0].shape
    pair_count = rows.shape[1] // 2
    return pl.pallas_call(
        functools.partial(relay_kernel, inner, (span,), margin),
        out_shape=(
            jax.ShapeDtypeStruct((pair_count, pno_count, span[1]), near[0].dtype),
            jax.ShapeDtypeStruct((2, pair_count, pno_count, pno_count), jnp.float32),
        ),
        in_specs=[SMEM, SMEM, VMEM] + [ANY] * (len(near) + len(far) + len(tokens)),
        out_specs=(VMEM, VMEM),
        scratch_shapes=[
            pltpu.VMEM((2 * inner * slots, pno_count, span[1]), near[0].dtype),
            pltpu.SemaphoreType.DMA,
        ],
        compiler_params=pltpu.CompilerParams(vmem_limit_bytes=24 << 20),
    )(rows, offsets, before, *near, *far, *tokens)


def mixed_pairs(inner, spans, margin, rows, offsets, near, far, others, held, sem, write):
    low = spans[0][0]
    slots = near[0].shape[0] // 2
    pair_count = others[0].shape[0]
    at = 2 * inner * slots
    gather_sides(near, far, spans, slots, held, sem)
    for other, (begin, size) in zip(others, spans):
        copy(
            other, held.at[pl.ds(at, pair_count), :, pl.ds(begin - low, size)], sem
        ).start()
    copy(held, held, sem).wait()

    def one_pair(n, carry):
        first, second = rows[0, 2 * n], rows[0, 2 * n + 1]
        product = overlap(
            held[jnp.where(first >= 0, first, at + n)],
            held[jnp.where(second >= 0, second, at + n)],
            (offsets[0, 2 * n], offsets[0, 2 * n + 1], margin),
            low,
        )
        write(n, jnp.where((first >= 0) != (second >= 0), product, 0.0))
        return carry

    lax.fori_loop(0, pair_count, one_pair, 0, unroll=4)


def mixed_kernel(inner, spans, margin, rows, offsets, *refs):
    near, refs = refs[:inner], refs[inner:]
    far, refs = refs[: inner * len(spans)], refs[inner * len(spans) :]
    others = refs[: len(spans)]
    coupling, held, sem = refs[-3:]

    def write(n, product):
        coupling[n] = product

    mixed_pairs(inner, spans, margin, rows, offsets, near, far, others, held, sem, write)


def finish_kernel(inner, spans, margin, rows, offsets, here, there, before, denominator, *refs):
    near, refs = refs[:inner], refs[inner:]
    far, refs = refs[: inner * len(spans)], refs[inner * len(spans) :]
    others = refs[: len(spans)]
    amplitude, energy, coupling, held, sem = refs[-5:]

    def write(n, product):
        coupling[n] = product

    mixed_pairs(inner, spans, margin, rows, offsets, near, far, others, held, sem, write)
    total = coupling[...] + before[...] + here[0] + there[...]
    result = -total / denominator[...]
    amplitude[...] = result
    parts = total * (2.0 * result - jnp.swapaxes(result, 1, 2))
    energy[...] = jnp.sum(jnp.sum(parts, axis=1), axis=1, keepdims=True)


def mixed(rows, offsets, near, far, others, spans, margin, tokens, finals):
    inner = len(near)
    slots, pno_count, _ = near[0].shape
    pair_count = rows.shape[1] // 2
    width = sum(size for _, size in spans)
    square = jax.ShapeDtypeStruct((pair_count, pno_count, pno_count), jnp.float32)
    line = jax.ShapeDtypeStruct((pair_count, 1), jnp.float32)
    scratch = [
        pltpu.VMEM((inner * slots + pair_count, pno_count, width), near[0].dtype),
        pltpu.SemaphoreType.DMA,
    ]
    if finals:
        scratch = [pltpu.VMEM(square.shape, jnp.float32)] + scratch
    return pl.pallas_call(
        functools.partial(
            finish_kernel if finals else mixed_kernel, inner, tuple(spans), margin
        ),
        out_shape=(square, line) if finals else square,
        in_specs=[SMEM] * 2
        + [VMEM] * len(finals)
        + [ANY] * (len(near) + len(far) + len(others) + len(tokens)),
        out_specs=(VMEM, VMEM) if finals else VMEM,
        scratch_shapes=scratch,
        compiler_params=pltpu.CompilerParams(vmem_limit_bytes=24 << 20),
    )(rows, offsets, *finals, *near, *far, *others, *tokens)


def slots_of(orbs):
    sequence = jnp.arange(orbs.shape[1], dtype=jnp.int32)
    same = orbs[:, :, None] == orbs[:, None, :]
    earlier = sequence[None, None, :] < sequence[None, :, None]
    return jnp.sum(jnp.where(same & earlier, 1, 0), axis=2).astype(jnp.int32)


def chunk_spans(fit_rows):
    sizes = (fit_rows // 2, 3 * fit_rows // 8, fit_rows // 8)
    return [(sum(sizes[:c]), size) for c, size in enumerate(sizes)]


def on_device(raw_ints, fit_inverse, pair_orbs, pno_coef, pno_energy, occ_energy, fit_offset):
    orb_count = lax.axis_size("orb")
    region, me = lax.axis_index("aux"), lax.axis_index("orb")
    group = orb_count // 2
    inner = group // 2
    pair_count = pair_orbs.shape[0]
    pno_count, dom_count = pno_coef.shape[2:]
    side_count = 2 * pair_count
    capacity = max(2, 4 * pair_count // orb_count)
    fit_rows = fit_inverse.shape[1]
    margin = fit_rows // 4

    def across(array, mask):
        return lax.ppermute(array, "orb", [(i, i ^ mask) for i in range(orb_count)])

    own_orbs = pair_orbs.reshape(side_count)
    place = jnp.stack([region, me]).astype(jnp.int32)
    half = dom_count // 2

    def exchange(array, k):
        part = lax.all_to_all(
            array[:, :, :, k * half : (k + 1) * half],
            "aux",
            split_axis=0,
            concat_axis=2,
            tiled=True,
        )
        return part[0, 0]

    raw_parts = [exchange(raw_ints, 0)]
    packed = pack(
        own_orbs, place, pno_coef.reshape(side_count, pno_count, dom_count), group, capacity
    )
    blocks = [packed[0]]
    for m in range(1, group):
        blocks.append(across(packed[m], m))
    own_offset = fit_offset[region * orb_count + me]
    turned = jnp.roll(fit_inverse[0], own_offset, axis=0)
    mate_orbs = across(own_orbs, inner)
    orb_total = occ_energy.shape[0]

    def pick(values, chosen):
        selector = (region * orb_count + chosen)[:, None] == jnp.arange(orb_total, dtype=jnp.int32)
        return jnp.sum(jnp.where(selector, values[None, :], 0), axis=1)

    occupied = pick(occ_energy, own_orbs).reshape(pair_count, 2)
    denominator = (
        pno_energy[:, 0, :, None]
        + pno_energy[:, 1, None, :]
        - occupied[:, 0, None, None]
        - occupied[:, 1, None, None]
    )
    spans = chunk_spans(fit_rows)
    reverse = group + inner
    ends = [(i, i ^ reverse) for i in range(orb_count) if i // inner in (0, 3)]
    middles = [(i, i ^ reverse) for i in range(orb_count) if i // inner in (1, 2)]
    fitted = []
    for k in range(2):
        fitted.append(
            jnp.dot(turned, raw_parts[k], preferred_element_type=jnp.float32).astype(jnp.bfloat16)
        )
        if k == 0:
            from_middle = lax.ppermute(fitted[0], "orb", middles)
            from_end = lax.ppermute(fitted[0], "orb", ends)
            later, fitted[0] = lax.optimization_barrier((raw_ints, fitted[0]))
            raw_parts.append(exchange(later, 1))
    mirrored = []
    for begin, size in spans:
        mirrored.append(across(fitted[1][begin : begin + size], reverse))

    def hop(outs):
        return [outs[0]] + [across(outs[i], i) for i in range(1, inner)]

    def project_far(c, tokens):
        begin, size = spans[c]
        parts = project(
            place,
            blocks,
            1,
            [from_middle, from_end, mirrored[c]],
            [(begin, 0, half, False), (begin, 0, half, True), (0, half, half, None)],
            size,
            tokens,
        )
        return hop(parts)

    def pass_on(c, before, tokens):
        sent, here = relay(rows, offsets, before, near, far[c], spans[c], margin, tokens)
        return across(sent, inner), here

    near = project(
        place,
        blocks,
        0,
        fitted,
        [(0, 0, half, None), (0, half, half, None)],
        fit_rows,
        [denominator],
    )
    mate_orbs, *near = lax.optimization_barrier((mate_orbs, *near))
    near = hop(near)
    orbs = jnp.stack([own_orbs, mate_orbs])
    differs = orbs ^ me
    other_half = (differs & group) != 0
    line = jnp.where(other_half, inner, 0) + (differs & (inner - 1))
    home = jnp.arange(2, dtype=jnp.int32)[:, None]
    position = slots_of(orbs)
    there = ((differs & inner) != 0) != other_half
    rows = jnp.where(there, -1, line * 2 * capacity + home * capacity + position)
    rows_home = jnp.where(there, -1, line * capacity + position)
    offsets = pick(fit_offset, orbs.reshape(2 * side_count)).reshape(2, side_count)
    far, others = [None] * 3, [None] * 3
    far[0] = project_far(0, [rows, rows_home, offsets])
    others[0], here = pass_on(0, jnp.zeros((8, 128), jnp.float32), [])
    far[1] = project_far(1, [here])
    far[2] = project_far(2, [far[1][0]])
    others[1], here = pass_on(1, here, [far[2][0]])
    others[2], here = pass_on(2, here, [])
    there = across(here[1], inner)
    body = mixed(
        rows_home, offsets, near, far[0] + far[1], others[:2], spans[:2], margin, [here], []
    )
    amplitude, energy = mixed(
        rows_home,
        offsets,
        near,
        far[2],
        others[2:],
        spans[2:],
        margin,
        [],
        [here, there, body, denominator],
    )
    return (amplitude.reshape(pair_count, pno_count * pno_count), energy.reshape(pair_count))


def solution(mesh):
    return jax.shard_map(
        on_device,
        mesh=mesh,
        in_specs=(
            P(None, "orb", "aux", None),
            P(("aux", "orb"), None, None),
            P(("aux", "orb"), None),
            P(("aux", "orb"), None, None, None),
            P(("aux", "orb"), None, None),
            P(),
            P(),
        ),
        out_specs=(P(("aux", "orb"), None), P(("aux", "orb"))),
        check_vma=False,
    )
```

```python
import functools

import jax
import jax.numpy as jnp
from jax import lax
from jax.experimental import pallas as pl
from jax.experimental.pallas import tpu as pltpu
from jax.sharding import PartitionSpec as P

SMEM = pl.BlockSpec(memory_space=pltpu.SMEM)
VMEM = pl.BlockSpec(memory_space=pltpu.VMEM)
ANY = pl.BlockSpec(memory_space=pl.ANY)


def copy(source, target, sem):
    return pltpu.make_async_copy(source, target, sem)


def pack_kernel(group, capacity, orbs, place, coef, *refs):
    outs, (held, count, holder, load_sem, store_sem) = refs[:-5], refs[-5:]
    load = copy(coef, held, load_sem)
    load.start()

    def clear(i, carry):
        holder[i] = 0
        return carry

    def clear_count(i, carry):
        count[i] = 0
        return carry

    def assign(s, carry):
        orb = orbs[s]
        at = count[orb]
        holder[orb * capacity + at] = s
        count[orb] = at + 1
        return carry

    lax.fori_loop(0, 2 * group * capacity, clear, 0)
    lax.fori_loop(0, 2 * group, clear_count, 0)
    lax.fori_loop(0, held.shape[0], assign, 0)
    load.wait()
    for mask, out in enumerate(outs):
        for kind in range(2):
            orb = place[1] ^ mask ^ (kind * (group + group // 2))

            def send(k, carry, orb=orb, kind=kind, out=out, sem=store_sem.at[mask]):
                copy(held.at[holder[orb * capacity + k]], out.at[kind * capacity + k], sem).start()
                return carry

            lax.fori_loop(0, capacity, send, 0)
    for mask, out in enumerate(outs):
        copy(held.at[pl.ds(0, 2 * capacity)], out, store_sem.at[mask]).wait()


def pack(orbs, place, coef, group, capacity):
    side_count, pno_count, dom_count = coef.shape
    block = jax.ShapeDtypeStruct((2 * capacity, pno_count, dom_count), coef.dtype)
    return pl.pallas_call(
        functools.partial(pack_kernel, group, capacity),
        out_shape=(block,) * group,
        in_specs=[SMEM, SMEM, ANY],
        out_specs=(ANY,) * group,
        scratch_shapes=[
            pltpu.VMEM(coef.shape, coef.dtype),
            pltpu.SMEM((2 * group,), jnp.int32),
            pltpu.SMEM((2 * group * capacity,), jnp.int32),
            pltpu.SemaphoreType.DMA,
            pltpu.SemaphoreType.DMA((group,)),
        ],
        cost_estimate=pl.CostEstimate(
            flops=0, transcendentals=0, bytes_accessed=6 * side_count * pno_count * dom_count
        ),
        name="pack",
    )(orbs, place, coef)


def project_kernel(group, capacity, kind, low, place, *refs):
    inner = group // 2
    blocks, heads = refs[:group], refs[group : -1 - inner]
    tail, outs = refs[-1 - inner], refs[-inner:]
    row_count, half = tail.shape
    pno_count = outs[0].shape[1]
    step = row_count if row_count <= 640 else 256
    plane = place[1] // inner
    at_end = (plane == 0) | (plane == 3)

    def tile(t, carry):
        at = t * step if isinstance(t, int) else pl.multiple_of(t * step, step)
        head = heads[0][pl.ds(low + at, step), :]
        if len(heads) > 1:
            head = jnp.where(at_end, heads[1][pl.ds(low + at, step), :], head)
        rest = tail[pl.ds(at, step), :]
        for i in range(inner):
            for j in range(2):
                lines = blocks[i + j * inner][kind * capacity : (kind + 1) * capacity]
                lines = lines.reshape(capacity * pno_count, 2 * half)
                product = lax.dot_general(
                    lines[:, :half],
                    head,
                    (((1,), (1,)), ((), ())),
                    preferred_element_type=jnp.float32,
                ) + lax.dot_general(
                    lines[:, half:],
                    rest,
                    (((1,), (1,)), ((), ())),
                    preferred_element_type=jnp.float32,
                )
                outs[i][j * capacity : (j + 1) * capacity, :, pl.ds(at, step)] = product.astype(
                    outs[i].dtype
                ).reshape(capacity, pno_count, step)
        return carry

    if row_count == step:
        tile(0, 0)
    else:
        lax.fori_loop(0, row_count // step, tile, 0)


def project(place, blocks, kind, heads, tail, low, tokens):
    group = len(blocks)
    inner = group // 2
    slots, pno_count, dom_count = blocks[0].shape
    capacity = slots // 2
    row_count = tail.shape[0]

    def kernel(*refs):
        used = 1 + group + len(heads) + 1
        project_kernel(group, capacity, kind, low, *refs[:used], *refs[-inner:])

    return pl.pallas_call(
        kernel,
        out_shape=(jax.ShapeDtypeStruct((slots, pno_count, row_count), blocks[0].dtype),) * inner,
        in_specs=[SMEM] + [VMEM] * (group + len(heads) + 1) + [ANY] * len(tokens),
        out_specs=(VMEM,) * inner,
        compiler_params=pltpu.CompilerParams(vmem_limit_bytes=24 << 20),
        cost_estimate=pl.CostEstimate(
            flops=2 * group * capacity * pno_count * dom_count * row_count,
            transcendentals=0,
            bytes_accessed=2 * group * capacity * pno_count * dom_count,
        ),
    )(place, *blocks, *heads, tail, *tokens)


def gather_sides(near, far, spans, slots, held, sem):
    inner = len(near)
    low, width = spans[0][0], sum(size for _, size in spans)
    for i in range(inner):
        copy(
            near[i].at[pl.ds(0, slots), :, pl.ds(low, width)],
            held.at[pl.ds(i * slots, slots)],
            sem,
        ).start()
        for c, (begin, size) in enumerate(spans):
            copy(
                far[c * inner + i].at[pl.ds(0, slots)],
                held.at[pl.ds((inner + i) * slots, slots), :, pl.ds(begin - low, size)],
                sem,
            ).start()


def overlap(first, second, limits, low):
    if low < limits[2]:
        lane = lax.broadcasted_iota(jnp.int32, (1, second.shape[1]), 1) + low
        apart = (lane < limits[0]) != (lane < limits[1])
        second = second * jnp.where(apart, 0.0, 1.0).astype(second.dtype)
    return lax.dot_general(
        first, second, (((1,), (1,)), ((), ())), preferred_element_type=jnp.float32
    )


def relay_kernel(inner, spans, margin, rows, offsets, before, *refs):
    near, far = refs[:inner], refs[inner : 2 * inner]
    sent, coupling, held, sem = refs[-4:]
    low = spans[0][0]
    pair_count = sent.shape[0]
    gather_sides(near, far, spans, near[0].shape[0], held, sem)
    copy(held, held, sem).wait()

    def choose(n, carry):
        sent[n] = held[jnp.maximum(jnp.maximum(rows[1, 2 * n], rows[1, 2 * n + 1]), 0)]
        return carry

    lax.fori_loop(0, pair_count, choose, 0, unroll=4)
    for h in range(2):

        def one_pair(n, carry, h=h):
            first, second = rows[h, 2 * n], rows[h, 2 * n + 1]
            product = overlap(
                held[jnp.maximum(first, 0)],
                held[jnp.maximum(second, 0)],
                (offsets[h, 2 * n], offsets[h, 2 * n + 1], margin),
                low,
            )
            product = jnp.where((first >= 0) & (second >= 0), product, 0.0)
            coupling[h, n] = product if low == 0 else product + before[h, n]
            return carry

        lax.fori_loop(0, pair_count, one_pair, 0, unroll=4)


def relay(rows, offsets, before, near, far, span, margin, tokens):
    inner = len(near)
    slots, pno_count, _ = near[0].shape
    pair_count = rows.shape[1] // 2
    return pl.pallas_call(
        functools.partial(relay_kernel, inner, (span,), margin),
        out_shape=(
            jax.ShapeDtypeStruct((pair_count, pno_count, span[1]), near[0].dtype),
            jax.ShapeDtypeStruct((2, pair_count, pno_count, pno_count), jnp.float32),
        ),
        in_specs=[SMEM, SMEM, VMEM] + [ANY] * (len(near) + len(far) + len(tokens)),
        out_specs=(VMEM, VMEM),
        scratch_shapes=[
            pltpu.VMEM((2 * inner * slots, pno_count, span[1]), near[0].dtype),
            pltpu.SemaphoreType.DMA,
        ],
        compiler_params=pltpu.CompilerParams(vmem_limit_bytes=24 << 20),
    )(rows, offsets, before, *near, *far, *tokens)


def mixed_pairs(inner, spans, margin, rows, offsets, near, far, others, held, sem, write):
    low = spans[0][0]
    slots = near[0].shape[0] // 2
    pair_count = others[0].shape[0]
    at = 2 * inner * slots
    gather_sides(near, far, spans, slots, held, sem)
    for other, (begin, size) in zip(others, spans):
        copy(
            other, held.at[pl.ds(at, pair_count), :, pl.ds(begin - low, size)], sem
        ).start()
    copy(held, held, sem).wait()

    def one_pair(n, carry):
        first, second = rows[0, 2 * n], rows[0, 2 * n + 1]
        product = overlap(
            held[jnp.where(first >= 0, first, at + n)],
            held[jnp.where(second >= 0, second, at + n)],
            (offsets[0, 2 * n], offsets[0, 2 * n + 1], margin),
            low,
        )
        write(n, jnp.where((first >= 0) != (second >= 0), product, 0.0))
        return carry

    lax.fori_loop(0, pair_count, one_pair, 0, unroll=4)


def mixed_kernel(inner, spans, margin, rows, offsets, *refs):
    near, refs = refs[:inner], refs[inner:]
    far, refs = refs[: inner * len(spans)], refs[inner * len(spans) :]
    others = refs[: len(spans)]
    coupling, held, sem = refs[-3:]

    def write(n, product):
        coupling[n] = product

    mixed_pairs(inner, spans, margin, rows, offsets, near, far, others, held, sem, write)


def finish_kernel(inner, spans, margin, rows, offsets, here, there, before, denominator, *refs):
    near, refs = refs[:inner], refs[inner:]
    far, refs = refs[: inner * len(spans)], refs[inner * len(spans) :]
    others = refs[: len(spans)]
    amplitude, energy, coupling, held, sem = refs[-5:]

    def write(n, product):
        coupling[n] = product

    mixed_pairs(inner, spans, margin, rows, offsets, near, far, others, held, sem, write)
    total = coupling[...] + before[...] + here[0] + there[...]
    result = -total / denominator[...]
    amplitude[...] = result
    parts = total * (2.0 * result - jnp.swapaxes(result, 1, 2))
    energy[...] = jnp.sum(jnp.sum(parts, axis=1), axis=1, keepdims=True)


def mixed(rows, offsets, near, far, others, spans, margin, tokens, finals):
    inner = len(near)
    slots, pno_count, _ = near[0].shape
    pair_count = rows.shape[1] // 2
    width = sum(size for _, size in spans)
    square = jax.ShapeDtypeStruct((pair_count, pno_count, pno_count), jnp.float32)
    line = jax.ShapeDtypeStruct((pair_count, 1), jnp.float32)
    scratch = [
        pltpu.VMEM((inner * slots + pair_count, pno_count, width), near[0].dtype),
        pltpu.SemaphoreType.DMA,
    ]
    if finals:
        scratch = [pltpu.VMEM(square.shape, jnp.float32)] + scratch
    return pl.pallas_call(
        functools.partial(
            finish_kernel if finals else mixed_kernel, inner, tuple(spans), margin
        ),
        out_shape=(square, line) if finals else square,
        in_specs=[SMEM] * 2
        + [VMEM] * len(finals)
        + [ANY] * (len(near) + len(far) + len(others) + len(tokens)),
        out_specs=(VMEM, VMEM) if finals else VMEM,
        scratch_shapes=scratch,
        compiler_params=pltpu.CompilerParams(vmem_limit_bytes=24 << 20),
    )(rows, offsets, *finals, *near, *far, *others, *tokens)


def slots_of(orbs):
    sequence = jnp.arange(orbs.shape[1], dtype=jnp.int32)
    same = orbs[:, :, None] == orbs[:, None, :]
    earlier = sequence[None, None, :] < sequence[None, :, None]
    return jnp.sum(jnp.where(same & earlier, 1, 0), axis=2).astype(jnp.int32)


def chunk_spans(fit_rows):
    sizes = (5 * fit_rows // 8, fit_rows // 4, fit_rows // 8)
    return [(sum(sizes[:c]), size) for c, size in enumerate(sizes)]


def on_device(raw_ints, fit_inverse, pair_orbs, pno_coef, pno_energy, occ_energy, fit_offset):
    orb_count = lax.axis_size("orb")
    region, me = lax.axis_index("aux"), lax.axis_index("orb")
    group = orb_count // 2
    inner = group // 2
    pair_count = pair_orbs.shape[0]
    pno_count, dom_count = pno_coef.shape[2:]
    side_count = 2 * pair_count
    capacity = max(2, 4 * pair_count // orb_count)
    fit_rows = fit_inverse.shape[1]
    margin = fit_rows // 4

    def across(array, mask):
        return lax.ppermute(array, "orb", [(i, i ^ mask) for i in range(orb_count)])

    own_orbs = pair_orbs.reshape(side_count)
    place = jnp.stack([region, me]).astype(jnp.int32)
    half = dom_count // 2

    def exchange(array, k):
        part = lax.all_to_all(
            array[:, :, :, k * half : (k + 1) * half],
            "aux",
            split_axis=0,
            concat_axis=2,
            tiled=True,
        )
        return part[0, 0]

    raw_parts = [exchange(raw_ints, 0)]
    packed = pack(
        own_orbs, place, pno_coef.reshape(side_count, pno_count, dom_count), group, capacity
    )
    blocks = [packed[0]]
    for m in range(1, group):
        blocks.append(across(packed[m], m))
    own_offset = fit_offset[region * orb_count + me]
    turned = jnp.roll(fit_inverse[0], own_offset, axis=0)
    mate_orbs = across(own_orbs, inner)
    orb_total = occ_energy.shape[0]

    def pick(values, chosen):
        selector = (region * orb_count + chosen)[:, None] == jnp.arange(orb_total, dtype=jnp.int32)
        return jnp.sum(jnp.where(selector, values[None, :], 0), axis=1)

    occupied = pick(occ_energy, own_orbs).reshape(pair_count, 2)
    denominator = (
        pno_energy[:, 0, :, None]
        + pno_energy[:, 1, None, :]
        - occupied[:, 0, None, None]
        - occupied[:, 1, None, None]
    )
    spans = chunk_spans(fit_rows)
    reverse = group + inner
    ends = [(i, i ^ reverse) for i in range(orb_count) if i // inner in (0, 3)]
    middles = [(i, i ^ reverse) for i in range(orb_count) if i // inner in (1, 2)]
    fitted = []
    for k in range(2):
        fitted.append(
            jnp.dot(turned, raw_parts[k], preferred_element_type=jnp.float32).astype(jnp.bfloat16)
        )
        if k == 0:
            from_middle = lax.ppermute(fitted[0], "orb", middles)
            from_end = lax.ppermute(fitted[0], "orb", ends)
            later, fitted[0] = lax.optimization_barrier((raw_ints, fitted[0]))
            raw_parts.append(exchange(later, 1))
    mirrored = []
    for begin, size in spans:
        mirrored.append(across(fitted[1][begin : begin + size], reverse))

    def hop(outs):
        return [outs[0]] + [across(outs[i], i) for i in range(1, inner)]

    def project_far(c, tokens):
        parts = project(place, blocks, 1, [from_middle, from_end], mirrored[c], spans[c][0], tokens)
        return hop(parts)

    def pass_on(c, before, tokens):
        sent, here = relay(rows, offsets, before, near, far[c], spans[c], margin, tokens)
        return across(sent, inner), here

    near = project(place, blocks, 0, fitted[:1], fitted[1], 0, [denominator])
    near = hop(near)
    far, others = [None] * 3, [None] * 3
    far[0] = project_far(0, [])
    far[1] = project_far(1, [far[0][0]])
    mate_orbs, far[1][0] = lax.optimization_barrier((mate_orbs, far[1][0]))
    orbs = jnp.stack([own_orbs, mate_orbs])
    differs = orbs ^ me
    other_half = (differs & group) != 0
    line = jnp.where(other_half, inner, 0) + (differs & (inner - 1))
    home = jnp.arange(2, dtype=jnp.int32)[:, None]
    position = slots_of(orbs)
    there = ((differs & inner) != 0) != other_half
    rows = jnp.where(there, -1, line * 2 * capacity + home * capacity + position)
    rows_home = jnp.where(there, -1, line * capacity + position)
    offsets = pick(fit_offset, orbs.reshape(2 * side_count)).reshape(2, side_count)
    others[0], here = pass_on(0, jnp.zeros((8, 128), jnp.float32), [far[1][0]])
    far[2] = project_far(2, [here])
    others[1], here = pass_on(1, here, [far[2][0]])
    others[2], here = pass_on(2, here, [])
    there = across(here[1], inner)
    body = mixed(
        rows_home, offsets, near, far[0] + far[1], others[:2], spans[:2], margin, [here], []
    )
    amplitude, energy = mixed(
        rows_home,
        offsets,
        near,
        far[2],
        others[2:],
        spans[2:],
        margin,
        [],
        [here, there, body, denominator],
    )
    return (amplitude.reshape(pair_count, pno_count * pno_count), energy.reshape(pair_count))


def solution(mesh):
    return jax.shard_map(
        on_device,
        mesh=mesh,
        in_specs=(
            P(None, "orb", "aux", None),
            P(("aux", "orb"), None, None),
            P(("aux", "orb"), None),
            P(("aux", "orb"), None, None, None),
            P(("aux", "orb"), None, None),
            P(),
            P(),
        ),
        out_specs=(P(("aux", "orb"), None), P(("aux", "orb"))),
        check_vma=False,
    )
```

```python
import functools

import jax
import jax.numpy as jnp
from jax import lax
from jax.experimental import pallas as pl
from jax.experimental.pallas import tpu as pltpu
from jax.sharding import PartitionSpec as P

SMEM = pl.BlockSpec(memory_space=pltpu.SMEM)
VMEM = pl.BlockSpec(memory_space=pltpu.VMEM)
ANY = pl.BlockSpec(memory_space=pl.ANY)


def copy(source, target, sem):
    return pltpu.make_async_copy(source, target, sem)


def pack_kernel(group, capacity, orbs, place, coef, *refs):
    outs, (held, count, holder, load_sem, store_sem) = refs[:-5], refs[-5:]
    load = copy(coef, held, load_sem)
    load.start()

    def clear(i, carry):
        holder[i] = 0
        return carry

    def clear_count(i, carry):
        count[i] = 0
        return carry

    def assign(s, carry):
        orb = orbs[s]
        at = count[orb]
        holder[orb * capacity + at] = s
        count[orb] = at + 1
        return carry

    lax.fori_loop(0, 2 * group * capacity, clear, 0)
    lax.fori_loop(0, 2 * group, clear_count, 0)
    lax.fori_loop(0, held.shape[0], assign, 0)
    load.wait()
    for mask, out in enumerate(outs):
        for kind in range(2):
            orb = place[1] ^ mask ^ (kind * (group + group // 2))

            def send(k, carry, orb=orb, kind=kind, out=out, sem=store_sem.at[mask]):
                copy(held.at[holder[orb * capacity + k]], out.at[kind * capacity + k], sem).start()
                return carry

            lax.fori_loop(0, capacity, send, 0)
    for mask, out in enumerate(outs):
        copy(held.at[pl.ds(0, 2 * capacity)], out, store_sem.at[mask]).wait()


def pack(orbs, place, coef, group, capacity):
    side_count, pno_count, dom_count = coef.shape
    block = jax.ShapeDtypeStruct((2 * capacity, pno_count, dom_count), coef.dtype)
    return pl.pallas_call(
        functools.partial(pack_kernel, group, capacity),
        out_shape=(block,) * group,
        in_specs=[SMEM, SMEM, ANY],
        out_specs=(ANY,) * group,
        scratch_shapes=[
            pltpu.VMEM(coef.shape, coef.dtype),
            pltpu.SMEM((2 * group,), jnp.int32),
            pltpu.SMEM((2 * group * capacity,), jnp.int32),
            pltpu.SemaphoreType.DMA,
            pltpu.SemaphoreType.DMA((group,)),
        ],
        cost_estimate=pl.CostEstimate(
            flops=0, transcendentals=0, bytes_accessed=6 * side_count * pno_count * dom_count
        ),
        name="pack",
    )(orbs, place, coef)


def project_kernel(group, capacity, *refs):
    inner = group // 2
    blocks, parts, outs = refs[:group], refs[group : group + 2], refs[-inner:]
    row_count, half = parts[0].shape
    pno_count = outs[0].shape[1]
    step = row_count if row_count <= 640 else 256

    def tile(t, carry):
        at = t * step if isinstance(t, int) else pl.multiple_of(t * step, step)
        rows = [part[pl.ds(at, step), :] for part in parts]
        for i in range(inner):
            for j in range(2):
                lines = blocks[i + j * inner][...].reshape(capacity * pno_count, 2 * half)
                product = sum(
                    lax.dot_general(
                        lines[:, k * half : (k + 1) * half],
                        rows[k],
                        (((1,), (1,)), ((), ())),
                        preferred_element_type=jnp.float32,
                    )
                    for k in range(2)
                )
                outs[i][j * capacity : (j + 1) * capacity, :, pl.ds(at, step)] = product.astype(
                    outs[i].dtype
                ).reshape(capacity, pno_count, step)
        return carry

    if row_count == step:
        tile(0, 0)
    else:
        lax.fori_loop(0, row_count // step, tile, 0)


def project(blocks, kind, parts, tokens):
    group = len(blocks)
    inner = group // 2
    slots, pno_count, dom_count = blocks[0].shape
    capacity = slots // 2
    row_count = parts[0].shape[0]

    def kernel(*refs):
        project_kernel(group, capacity, *refs[: group + 2], *refs[-inner:])

    block = pl.BlockSpec((capacity, pno_count, dom_count), lambda i: (kind, 0, 0))
    part = pl.BlockSpec(parts[0].shape, lambda i: (0, 0))
    return pl.pallas_call(
        kernel,
        grid=(1,),
        out_shape=(jax.ShapeDtypeStruct((slots, pno_count, row_count), blocks[0].dtype),) * inner,
        in_specs=[block] * group + [part] * 2 + [ANY] * len(tokens),
        out_specs=(pl.BlockSpec((slots, pno_count, row_count), lambda i: (0, 0, 0)),) * inner,
        compiler_params=pltpu.CompilerParams(vmem_limit_bytes=32 << 20),
        cost_estimate=pl.CostEstimate(
            flops=2 * group * capacity * pno_count * dom_count * row_count,
            transcendentals=0,
            bytes_accessed=2 * group * capacity * pno_count * dom_count,
        ),
    )(*blocks, *parts, *tokens)


def gather_sides(near, far, spans, slots, held, sem):
    inner = len(near)
    low, width = spans[0][0], sum(size for _, size in spans)
    for i in range(inner):
        copy(
            near[i].at[pl.ds(0, slots), :, pl.ds(low, width)],
            held.at[pl.ds(i * slots, slots)],
            sem,
        ).start()
        for c, (begin, size) in enumerate(spans):
            copy(
                far[c * inner + i].at[pl.ds(0, slots)],
                held.at[pl.ds((inner + i) * slots, slots), :, pl.ds(begin - low, size)],
                sem,
            ).start()


def overlap(first, second, limits, low):
    if low < limits[2]:
        lane = lax.broadcasted_iota(jnp.int32, (1, second.shape[1]), 1) + low
        apart = (lane < limits[0]) != (lane < limits[1])
        second = second * jnp.where(apart, 0.0, 1.0).astype(second.dtype)
    return lax.dot_general(
        first, second, (((1,), (1,)), ((), ())), preferred_element_type=jnp.float32
    )


def relay_kernel(inner, spans, margin, rows, offsets, before, *refs):
    near, far = refs[:inner], refs[inner : 2 * inner]
    sent, coupling, held, sem = refs[-4:]
    low = spans[0][0]
    pair_count = sent.shape[0]
    gather_sides(near, far, spans, near[0].shape[0], held, sem)
    copy(held, held, sem).wait()

    def choose(n, carry):
        sent[n] = held[jnp.maximum(jnp.maximum(rows[1, 2 * n], rows[1, 2 * n + 1]), 0)]
        return carry

    lax.fori_loop(0, pair_count, choose, 0, unroll=4)
    for h in range(2):

        def one_pair(n, carry, h=h):
            first, second = rows[h, 2 * n], rows[h, 2 * n + 1]
            product = overlap(
                held[jnp.maximum(first, 0)],
                held[jnp.maximum(second, 0)],
                (offsets[h, 2 * n], offsets[h, 2 * n + 1], margin),
                low,
            )
            product = jnp.where((first >= 0) & (second >= 0), product, 0.0)
            coupling[h, n] = product if low == 0 else product + before[h, n]
            return carry

        lax.fori_loop(0, pair_count, one_pair, 0, unroll=4)


def relay(rows, offsets, before, near, far, span, margin, tokens):
    inner = len(near)
    slots, pno_count, _ = near[0].shape
    pair_count = rows.shape[1] // 2
    return pl.pallas_call(
        functools.partial(relay_kernel, inner, (span,), margin),
        out_shape=(
            jax.ShapeDtypeStruct((pair_count, pno_count, span[1]), near[0].dtype),
            jax.ShapeDtypeStruct((2, pair_count, pno_count, pno_count), jnp.float32),
        ),
        in_specs=[SMEM, SMEM, VMEM] + [ANY] * (len(near) + len(far) + len(tokens)),
        out_specs=(VMEM, VMEM),
        scratch_shapes=[
            pltpu.VMEM((2 * inner * slots, pno_count, span[1]), near[0].dtype),
            pltpu.SemaphoreType.DMA,
        ],
        compiler_params=pltpu.CompilerParams(vmem_limit_bytes=24 << 20),
    )(rows, offsets, before, *near, *far, *tokens)


def mixed_pairs(inner, spans, margin, rows, offsets, near, far, others, held, sem, write):
    low = spans[0][0]
    slots = near[0].shape[0] // 2
    pair_count = others[0].shape[0]
    at = 2 * inner * slots
    gather_sides(near, far, spans, slots, held, sem)
    for other, (begin, size) in zip(others, spans):
        copy(
            other, held.at[pl.ds(at, pair_count), :, pl.ds(begin - low, size)], sem
        ).start()
    copy(held, held, sem).wait()

    def one_pair(n, carry):
        first, second = rows[0, 2 * n], rows[0, 2 * n + 1]
        product = overlap(
            held[jnp.where(first >= 0, first, at + n)],
            held[jnp.where(second >= 0, second, at + n)],
            (offsets[0, 2 * n], offsets[0, 2 * n + 1], margin),
            low,
        )
        write(n, jnp.where((first >= 0) != (second >= 0), product, 0.0))
        return carry

    lax.fori_loop(0, pair_count, one_pair, 0, unroll=4)


def mixed_kernel(inner, spans, margin, rows, offsets, *refs):
    near, refs = refs[:inner], refs[inner:]
    far, refs = refs[: inner * len(spans)], refs[inner * len(spans) :]
    others = refs[: len(spans)]
    coupling, held, sem = refs[-3:]

    def write(n, product):
        coupling[n] = product

    mixed_pairs(inner, spans, margin, rows, offsets, near, far, others, held, sem, write)


def finish_kernel(inner, spans, margin, rows, offsets, here, there, before, denominator, *refs):
    near, refs = refs[:inner], refs[inner:]
    far, refs = refs[: inner * len(spans)], refs[inner * len(spans) :]
    others = refs[: len(spans)]
    amplitude, energy, coupling, held, sem = refs[-5:]

    def write(n, product):
        coupling[n] = product

    mixed_pairs(inner, spans, margin, rows, offsets, near, far, others, held, sem, write)
    total = coupling[...] + before[...] + here[0] + there[...]
    result = -total / denominator[...]
    amplitude[...] = result
    parts = total * (2.0 * result - jnp.swapaxes(result, 1, 2))
    energy[...] = jnp.sum(jnp.sum(parts, axis=1), axis=1, keepdims=True)


def mixed(rows, offsets, near, far, others, spans, margin, tokens, finals):
    inner = len(near)
    slots, pno_count, _ = near[0].shape
    pair_count = rows.shape[1] // 2
    width = sum(size for _, size in spans)
    square = jax.ShapeDtypeStruct((pair_count, pno_count, pno_count), jnp.float32)
    line = jax.ShapeDtypeStruct((pair_count, 1), jnp.float32)
    scratch = [
        pltpu.VMEM((inner * slots + pair_count, pno_count, width), near[0].dtype),
        pltpu.SemaphoreType.DMA,
    ]
    if finals:
        scratch = [pltpu.VMEM(square.shape, jnp.float32)] + scratch
    return pl.pallas_call(
        functools.partial(
            finish_kernel if finals else mixed_kernel, inner, tuple(spans), margin
        ),
        out_shape=(square, line) if finals else square,
        in_specs=[SMEM] * 2
        + [VMEM] * len(finals)
        + [ANY] * (len(near) + len(far) + len(others) + len(tokens)),
        out_specs=(VMEM, VMEM) if finals else VMEM,
        scratch_shapes=scratch,
        compiler_params=pltpu.CompilerParams(vmem_limit_bytes=24 << 20),
    )(rows, offsets, *finals, *near, *far, *others, *tokens)


def slots_of(orbs):
    sequence = jnp.arange(orbs.shape[1], dtype=jnp.int32)
    same = orbs[:, :, None] == orbs[:, None, :]
    earlier = sequence[None, None, :] < sequence[None, :, None]
    return jnp.sum(jnp.where(same & earlier, 1, 0), axis=2).astype(jnp.int32)


def chunk_spans(fit_rows):
    sizes = (5 * fit_rows // 8, fit_rows // 4, fit_rows // 8)
    return [(sum(sizes[:c]), size) for c, size in enumerate(sizes)]


def on_device(raw_ints, fit_inverse, pair_orbs, pno_coef, pno_energy, occ_energy, fit_offset):
    orb_count = lax.axis_size("orb")
    region, me = lax.axis_index("aux"), lax.axis_index("orb")
    group = orb_count // 2
    inner = group // 2
    pair_count = pair_orbs.shape[0]
    pno_count, dom_count = pno_coef.shape[2:]
    side_count = 2 * pair_count
    capacity = max(2, 4 * pair_count // orb_count)
    fit_rows = fit_inverse.shape[1]
    margin = fit_rows // 4

    def across(array, mask):
        return lax.ppermute(array, "orb", [(i, i ^ mask) for i in range(orb_count)])

    own_orbs = pair_orbs.reshape(side_count)
    place = jnp.stack([region, me]).astype(jnp.int32)
    half = dom_count // 2

    def exchange(array, k):
        part = lax.all_to_all(
            array[:, :, :, k * half : (k + 1) * half],
            "aux",
            split_axis=0,
            concat_axis=2,
            tiled=True,
        )
        return part[0, 0]

    raw_parts = [exchange(raw_ints, 0)]
    packed = pack(
        own_orbs, place, pno_coef.reshape(side_count, pno_count, dom_count), group, capacity
    )
    blocks = [packed[0]]
    for m in range(1, group):
        blocks.append(across(packed[m], m))
    own_offset = fit_offset[region * orb_count + me]
    turned = jnp.roll(fit_inverse[0], own_offset, axis=0)
    mate_orbs = across(own_orbs, inner)
    orb_total = occ_energy.shape[0]

    def pick(values, chosen):
        selector = (region * orb_count + chosen)[:, None] == jnp.arange(orb_total, dtype=jnp.int32)
        return jnp.sum(jnp.where(selector, values[None, :], 0), axis=1)

    occupied = pick(occ_energy, own_orbs).reshape(pair_count, 2)
    denominator = (
        pno_energy[:, 0, :, None]
        + pno_energy[:, 1, None, :]
        - occupied[:, 0, None, None]
        - occupied[:, 1, None, None]
    )
    spans = chunk_spans(fit_rows)
    reverse = group + inner
    fitted, mirrored = [], [[None] * 2 for _ in spans]

    def mirror(c, k):
        begin, size = spans[c]
        mirrored[c][k] = across(fitted[k][begin : begin + size], reverse)

    for k in range(2):
        fitted.append(
            jnp.dot(turned, raw_parts[k], preferred_element_type=jnp.float32).astype(jnp.bfloat16)
        )
        mirror(0, k)
        if k == 0:
            later, fitted[0] = lax.optimization_barrier((raw_ints, fitted[0]))
            raw_parts.append(exchange(later, 1))
        mirror(1, k)
    mirror(2, 0)
    mirror(2, 1)

    def hop(outs):
        return [outs[0]] + [across(outs[i], i) for i in range(1, inner)]

    def project_far(c, tokens):
        parts = project(blocks, 1, mirrored[c], tokens)
        return hop(parts)

    def pass_on(c, before, tokens):
        sent, here = relay(rows, offsets, before, near, far[c], spans[c], margin, tokens)
        return across(sent, inner), here

    near = project(blocks, 0, fitted, [denominator])
    near = hop(near)
    far, others = [None] * 3, [None] * 3
    far[0] = project_far(0, [])
    mate_orbs, far[0][0] = lax.optimization_barrier((mate_orbs, far[0][0]))
    orbs = jnp.stack([own_orbs, mate_orbs])
    differs = orbs ^ me
    other_half = (differs & group) != 0
    line = jnp.where(other_half, inner, 0) + (differs & (inner - 1))
    home = jnp.arange(2, dtype=jnp.int32)[:, None]
    position = slots_of(orbs)
    there = ((differs & inner) != 0) != other_half
    rows = jnp.where(there, -1, line * 2 * capacity + home * capacity + position)
    rows_home = jnp.where(there, -1, line * capacity + position)
    offsets = pick(fit_offset, orbs.reshape(2 * side_count)).reshape(2, side_count)
    others[0], here = pass_on(0, jnp.zeros((8, 128), jnp.float32), [])
    far[1] = project_far(1, [here])
    far[2] = project_far(2, [far[1][0]])
    others[1], here = pass_on(1, here, [far[2][0]])
    others[2], here = pass_on(2, here, [])
    there = across(here[1], inner)
    body = mixed(
        rows_home, offsets, near, far[0] + far[1], others[:2], spans[:2], margin, [here], []
    )
    amplitude, energy = mixed(
        rows_home,
        offsets,
        near,
        far[2],
        others[2:],
        spans[2:],
        margin,
        [],
        [here, there, body, denominator],
    )
    return (amplitude.reshape(pair_count, pno_count * pno_count), energy.reshape(pair_count))


def solution(mesh):
    return jax.shard_map(
        on_device,
        mesh=mesh,
        in_specs=(
            P(None, "orb", "aux", None),
            P(("aux", "orb"), None, None),
            P(("aux", "orb"), None),
            P(("aux", "orb"), None, None, None),
            P(("aux", "orb"), None, None),
            P(),
            P(),
        ),
        out_specs=(P(("aux", "orb"), None), P(("aux", "orb"))),
        check_vma=False,
    )
```

```python
import functools

import jax
import jax.numpy as jnp
from jax import lax
from jax.experimental import pallas as pl
from jax.experimental.pallas import tpu as pltpu
from jax.sharding import PartitionSpec as P

SMEM = pl.BlockSpec(memory_space=pltpu.SMEM)
VMEM = pl.BlockSpec(memory_space=pltpu.VMEM)
ANY = pl.BlockSpec(memory_space=pl.ANY)


def copy(source, target, sem):
    return pltpu.make_async_copy(source, target, sem)


def pack_kernel(group, capacity, orbs, place, coef, *refs):
    outs, (held, count, holder, load_sem, store_sem) = refs[:-5], refs[-5:]
    load = copy(coef, held, load_sem)
    load.start()

    def clear(i, carry):
        holder[i] = 0
        return carry

    def clear_count(i, carry):
        count[i] = 0
        return carry

    def assign(s, carry):
        orb = orbs[s]
        at = count[orb]
        holder[orb * capacity + at] = s
        count[orb] = at + 1
        return carry

    lax.fori_loop(0, 2 * group * capacity, clear, 0)
    lax.fori_loop(0, 2 * group, clear_count, 0)
    lax.fori_loop(0, held.shape[0], assign, 0)
    load.wait()
    for mask, out in enumerate(outs):
        for kind in range(2):
            orb = place[1] ^ mask ^ (kind * (group + group // 2))

            def send(k, carry, orb=orb, kind=kind, out=out, sem=store_sem.at[mask]):
                copy(held.at[holder[orb * capacity + k]], out.at[kind * capacity + k], sem).start()
                return carry

            lax.fori_loop(0, capacity, send, 0)
    for mask, out in enumerate(outs):
        copy(held.at[pl.ds(0, 2 * capacity)], out, store_sem.at[mask]).wait()


def pack(orbs, place, coef, group, capacity):
    side_count, pno_count, dom_count = coef.shape
    block = jax.ShapeDtypeStruct((2 * capacity, pno_count, dom_count), coef.dtype)
    return pl.pallas_call(
        functools.partial(pack_kernel, group, capacity),
        out_shape=(block,) * group,
        in_specs=[SMEM, SMEM, ANY],
        out_specs=(ANY,) * group,
        scratch_shapes=[
            pltpu.VMEM(coef.shape, coef.dtype),
            pltpu.SMEM((2 * group,), jnp.int32),
            pltpu.SMEM((2 * group * capacity,), jnp.int32),
            pltpu.SemaphoreType.DMA,
            pltpu.SemaphoreType.DMA((group,)),
        ],
        cost_estimate=pl.CostEstimate(
            flops=0, transcendentals=0, bytes_accessed=6 * side_count * pno_count * dom_count
        ),
        name="pack",
    )(orbs, place, coef)


def project_kernel(group, capacity, direct, *refs):
    inner = group // 2
    blocks, parts, outs = refs[:group], refs[group : group + 2], refs[group + 2 :]
    row_count, half = parts[0].shape
    pno_count = outs[0].shape[1]
    step = row_count if row_count <= 640 else 256

    def tile(t, carry):
        at = t * step if isinstance(t, int) else pl.multiple_of(t * step, step)
        rows = [part[pl.ds(at, step), :] for part in parts]
        for i in range(inner):
            for j in range(2):
                lines = blocks[i + j * inner][...].reshape(capacity * pno_count, 2 * half)
                product = sum(
                    lax.dot_general(
                        lines[:, k * half : (k + 1) * half],
                        rows[k],
                        (((1,), (1,)), ((), ())),
                        preferred_element_type=jnp.float32,
                    )
                    for k in range(2)
                )
                out, first = (outs[i + j * inner], 0) if direct else (outs[i], j * capacity)
                out[first : first + capacity, :, pl.ds(at, step)] = product.astype(
                    out.dtype
                ).reshape(capacity, pno_count, step)
        return carry

    if row_count == step:
        tile(0, 0)
    else:
        lax.fori_loop(0, row_count // step, tile, 0)


def project(blocks, kind, parts, tokens, direct):
    group = len(blocks)
    inner = group // 2
    slots, pno_count, dom_count = blocks[0].shape
    capacity = slots // 2
    row_count = parts[0].shape[0]
    count, lines = (group, capacity) if direct else (inner, slots)

    def kernel(*refs):
        project_kernel(group, capacity, direct, *refs[: group + 2], *refs[-count:])

    block = pl.BlockSpec((capacity, pno_count, dom_count), lambda i: (kind, 0, 0))
    part = pl.BlockSpec(parts[0].shape, lambda i: (0, 0))
    return pl.pallas_call(
        kernel,
        grid=(1,),
        out_shape=(jax.ShapeDtypeStruct((lines, pno_count, row_count), blocks[0].dtype),) * count,
        in_specs=[block] * group + [part] * 2 + [ANY] * len(tokens),
        out_specs=(pl.BlockSpec((lines, pno_count, row_count), lambda i: (0, 0, 0)),) * count,
        compiler_params=pltpu.CompilerParams(vmem_limit_bytes=32 << 20),
        cost_estimate=pl.CostEstimate(
            flops=2 * group * capacity * pno_count * dom_count * row_count,
            transcendentals=0,
            bytes_accessed=2 * group * capacity * pno_count * dom_count,
        ),
    )(*blocks, *parts, *tokens)


def gather_sides(near, far, spans, slots, held, sem):
    inner = len(near)
    low, width = spans[0][0], sum(size for _, size in spans)
    for i in range(inner):
        copy(
            near[i].at[pl.ds(0, slots), :, pl.ds(low, width)],
            held.at[pl.ds(i * slots, slots)],
            sem,
        ).start()
        for c, (begin, size) in enumerate(spans):
            copy(
                far[c * inner + i].at[pl.ds(0, slots)],
                held.at[pl.ds((inner + i) * slots, slots), :, pl.ds(begin - low, size)],
                sem,
            ).start()


def overlap(first, second, limits, low):
    if low < limits[2]:
        lane = lax.broadcasted_iota(jnp.int32, (1, second.shape[1]), 1) + low
        apart = (lane < limits[0]) != (lane < limits[1])
        second = second * jnp.where(apart, 0.0, 1.0).astype(second.dtype)
    return lax.dot_general(
        first, second, (((1,), (1,)), ((), ())), preferred_element_type=jnp.float32
    )


def relay_kernel(inner, spans, margin, rows, offsets, before, *refs):
    near, far = refs[:inner], refs[inner : 2 * inner]
    sent, coupling, held, sem = refs[-4:]
    low = spans[0][0]
    pair_count = sent.shape[0]
    gather_sides(near, far, spans, near[0].shape[0], held, sem)
    copy(held, held, sem).wait()

    def choose(n, carry):
        sent[n] = held[jnp.maximum(jnp.maximum(rows[1, 2 * n], rows[1, 2 * n + 1]), 0)]
        return carry

    lax.fori_loop(0, pair_count, choose, 0, unroll=4)
    for h in range(2):

        def one_pair(n, carry, h=h):
            first, second = rows[h, 2 * n], rows[h, 2 * n + 1]
            product = overlap(
                held[jnp.maximum(first, 0)],
                held[jnp.maximum(second, 0)],
                (offsets[h, 2 * n], offsets[h, 2 * n + 1], margin),
                low,
            )
            product = jnp.where((first >= 0) & (second >= 0), product, 0.0)
            coupling[h, n] = product if low == 0 else product + before[h, n]
            return carry

        lax.fori_loop(0, pair_count, one_pair, 0, unroll=4)


def relay(rows, offsets, before, near, far, span, margin, tokens):
    inner = len(near)
    slots, pno_count, _ = near[0].shape
    pair_count = rows.shape[1] // 2
    return pl.pallas_call(
        functools.partial(relay_kernel, inner, (span,), margin),
        out_shape=(
            jax.ShapeDtypeStruct((pair_count, pno_count, span[1]), near[0].dtype),
            jax.ShapeDtypeStruct((2, pair_count, pno_count, pno_count), jnp.float32),
        ),
        in_specs=[SMEM, SMEM, VMEM] + [ANY] * (len(near) + len(far) + len(tokens)),
        out_specs=(VMEM, VMEM),
        scratch_shapes=[
            pltpu.VMEM((2 * inner * slots, pno_count, span[1]), near[0].dtype),
            pltpu.SemaphoreType.DMA,
        ],
        compiler_params=pltpu.CompilerParams(vmem_limit_bytes=24 << 20),
    )(rows, offsets, before, *near, *far, *tokens)


def mixed_pairs(inner, spans, margin, rows, offsets, near, far, others, held, sem, write):
    low = spans[0][0]
    slots = near[0].shape[0] // 2
    pair_count = others[0].shape[0]
    at = 2 * inner * slots
    gather_sides(near, far, spans, slots, held, sem)
    for other, (begin, size) in zip(others, spans):
        copy(
            other, held.at[pl.ds(at, pair_count), :, pl.ds(begin - low, size)], sem
        ).start()
    copy(held, held, sem).wait()

    def one_pair(n, carry):
        first, second = rows[0, 2 * n], rows[0, 2 * n + 1]
        product = overlap(
            held[jnp.where(first >= 0, first, at + n)],
            held[jnp.where(second >= 0, second, at + n)],
            (offsets[0, 2 * n], offsets[0, 2 * n + 1], margin),
            low,
        )
        write(n, jnp.where((first >= 0) != (second >= 0), product, 0.0))
        return carry

    lax.fori_loop(0, pair_count, one_pair, 0, unroll=4)


def mixed_kernel(inner, spans, margin, rows, offsets, *refs):
    near, refs = refs[:inner], refs[inner:]
    far, refs = refs[: inner * len(spans)], refs[inner * len(spans) :]
    others = refs[: len(spans)]
    coupling, held, sem = refs[-3:]

    def write(n, product):
        coupling[n] = product

    mixed_pairs(inner, spans, margin, rows, offsets, near, far, others, held, sem, write)


def finish_kernel(group, sizes, rows, here, there, before, denominator, *refs):
    inner = group // 2
    near, straight, far = refs[:inner], refs[inner:group], refs[group : group + group * len(sizes)]
    amplitude, energy, coupling, held, sem = refs[-5:]
    capacity, _, width = straight[0].shape
    low = near[0].shape[2] - width
    for m in range(group):
        source = straight[m - inner]
        if m < inner:
            source = near[m].at[pl.ds(0, capacity), :, pl.ds(low, width)]
        copy(source, held.at[pl.ds(m * capacity, capacity)], sem).start()
        at = 0
        for c, size in enumerate(sizes):
            copy(
                far[c * group + m],
                held.at[pl.ds((group + m) * capacity, capacity), :, pl.ds(at, size)],
                sem,
            ).start()
            at += size
    copy(held, held, sem).wait()

    def one_pair(n, carry):
        coupling[n] = lax.dot_general(
            held[rows[2 * n]],
            held[rows[2 * n + 1]],
            (((1,), (1,)), ((), ())),
            preferred_element_type=jnp.float32,
        )
        return carry

    lax.fori_loop(0, coupling.shape[0], one_pair, 0, unroll=4)
    total = coupling[...] + before[...] + here[0] + there[...]
    result = -total / denominator[...]
    amplitude[...] = result
    parts = total * (2.0 * result - jnp.swapaxes(result, 1, 2))
    energy[...] = jnp.sum(jnp.sum(parts, axis=1), axis=1, keepdims=True)


def finish(rows, finals, near, straight, far, sizes):
    group = 2 * len(near)
    capacity, pno_count, width = straight[0].shape
    pair_count = rows.shape[0] // 2
    square = jax.ShapeDtypeStruct((pair_count, pno_count, pno_count), jnp.float32)
    return pl.pallas_call(
        functools.partial(finish_kernel, group, sizes),
        out_shape=(square, jax.ShapeDtypeStruct((pair_count, 1), jnp.float32)),
        in_specs=[SMEM] + [VMEM] * len(finals) + [ANY] * (len(near) + len(straight) + len(far)),
        out_specs=(VMEM, VMEM),
        scratch_shapes=[
            pltpu.VMEM(square.shape, jnp.float32),
            pltpu.VMEM((2 * group * capacity, pno_count, width), near[0].dtype),
            pltpu.SemaphoreType.DMA,
        ],
        compiler_params=pltpu.CompilerParams(vmem_limit_bytes=24 << 20),
        name="finish",
    )(rows, *finals, *near, *straight, *far)


def mixed(rows, offsets, near, far, others, spans, margin, tokens):
    inner = len(near)
    slots, pno_count, _ = near[0].shape
    pair_count = rows.shape[1] // 2
    width = sum(size for _, size in spans)
    return pl.pallas_call(
        functools.partial(mixed_kernel, inner, tuple(spans), margin),
        out_shape=jax.ShapeDtypeStruct((pair_count, pno_count, pno_count), jnp.float32),
        in_specs=[SMEM] * 2 + [ANY] * (len(near) + len(far) + len(others) + len(tokens)),
        out_specs=VMEM,
        scratch_shapes=[
            pltpu.VMEM((inner * slots + pair_count, pno_count, width), near[0].dtype),
            pltpu.SemaphoreType.DMA,
        ],
        compiler_params=pltpu.CompilerParams(vmem_limit_bytes=24 << 20),
    )(rows, offsets, *near, *far, *others, *tokens)


def slots_of(orbs):
    sequence = jnp.arange(orbs.shape[1], dtype=jnp.int32)
    same = orbs[:, :, None] == orbs[:, None, :]
    earlier = sequence[None, None, :] < sequence[None, :, None]
    return jnp.sum(jnp.where(same & earlier, 1, 0), axis=2).astype(jnp.int32)


def chunk_spans(fit_rows):
    sizes = (fit_rows // 2, fit_rows // 4, fit_rows // 8, fit_rows // 8)
    return [(sum(sizes[:c]), size) for c, size in enumerate(sizes)]


def on_device(raw_ints, fit_inverse, pair_orbs, pno_coef, pno_energy, occ_energy, fit_offset):
    orb_count = lax.axis_size("orb")
    region, me = lax.axis_index("aux"), lax.axis_index("orb")
    group = orb_count // 2
    inner = group // 2
    pair_count = pair_orbs.shape[0]
    pno_count, dom_count = pno_coef.shape[2:]
    side_count = 2 * pair_count
    capacity = max(2, 4 * pair_count // orb_count)
    fit_rows = fit_inverse.shape[1]
    margin = fit_rows // 4

    def across(array, mask):
        return lax.ppermute(array, "orb", [(i, i ^ mask) for i in range(orb_count)])

    own_orbs = pair_orbs.reshape(side_count)
    place = jnp.stack([region, me]).astype(jnp.int32)
    half = dom_count // 2

    def exchange(array, k):
        part = lax.all_to_all(
            array[:, :, :, k * half : (k + 1) * half],
            "aux",
            split_axis=0,
            concat_axis=2,
            tiled=True,
        )
        return part[0, 0]

    raw_parts = [exchange(raw_ints, 0)]
    packed = pack(
        own_orbs, place, pno_coef.reshape(side_count, pno_count, dom_count), group, capacity
    )
    later, packed = lax.optimization_barrier((raw_ints, packed))
    raw_parts.append(exchange(later, 1))
    blocks = [packed[0]]
    for m in range(1, group):
        blocks.append(across(packed[m], m))
    own_offset = fit_offset[region * orb_count + me]
    turned = jnp.roll(fit_inverse[0], own_offset, axis=0)
    mate_orbs = across(own_orbs, inner)
    orb_total = occ_energy.shape[0]

    def pick(values, chosen):
        selector = (region * orb_count + chosen)[:, None] == jnp.arange(orb_total, dtype=jnp.int32)
        return jnp.sum(jnp.where(selector, values[None, :], 0), axis=1)

    spans = chunk_spans(fit_rows)
    reverse = group + inner
    fitted, mirrored = [], [[None] * 2 for _ in spans]

    def mirror(c, k):
        begin, size = spans[c]
        mirrored[c][k] = across(fitted[k][begin : begin + size], reverse)

    for k in range(2):
        product = jnp.dot(turned, raw_parts[k], preferred_element_type=jnp.float32)
        fitted.append(product.astype(jnp.bfloat16))
        mirror(0, k)
    for c in range(1, len(spans)):
        mirror(c, 0)
        mirror(c, 1)

    energies, fitted[1] = lax.optimization_barrier((occ_energy, fitted[1]))
    occupied = pick(energies, own_orbs).reshape(pair_count, 2)
    denominator = (
        pno_energy[:, 0, :, None]
        + pno_energy[:, 1, None, :]
        - occupied[:, 0, None, None]
        - occupied[:, 1, None, None]
    )

    def hop(outs):
        return [outs[0]] + [across(outs[i], i) for i in range(1, inner)]

    def project_far(c, tokens):
        parts = project(blocks, 1, mirrored[c], tokens, c > 1)
        return hop(parts) if c < 2 else [parts[0]] + [across(parts[m], m) for m in range(1, group)]

    def pass_on(c, before, tokens):
        sent, here = relay(rows, offsets, before, near, far[c], spans[c], margin, tokens)
        return across(sent, inner), here

    near = project(blocks, 0, fitted, [denominator], False)
    last = spans[2][0]
    straight = [across(near[i][capacity:, :, last:], i + inner) for i in range(inner)]
    near = hop(near)
    far, others = [None] * 4, [None] * 2
    far[0] = project_far(0, [])
    mate_orbs, far[0][0] = lax.optimization_barrier((mate_orbs, far[0][0]))
    orbs = jnp.stack([own_orbs, mate_orbs])
    differs = orbs ^ me
    other_half = (differs & group) != 0
    line = jnp.where(other_half, inner, 0) + (differs & (inner - 1))
    home = jnp.arange(2, dtype=jnp.int32)[:, None]
    position = slots_of(orbs)
    there = ((differs & inner) != 0) != other_half
    rows = jnp.where(there, -1, line * 2 * capacity + home * capacity + position)
    rows_home = jnp.where(there, -1, line * capacity + position)
    place_of = (differs[0] ^ jnp.where(other_half[0], reverse, 0)) + jnp.where(
        other_half[0], group, 0
    )
    rows_all = place_of * capacity + position[0]
    offsets = pick(fit_offset, orbs.reshape(2 * side_count)).reshape(2, side_count)
    others[0], here = pass_on(0, jnp.zeros((8, 128), jnp.float32), [])
    far[1] = project_far(1, [here])
    far[2] = project_far(2, [far[1][0]])
    others[1], here = pass_on(1, here, [far[2][0]])
    there = across(here[1], inner)
    far[3] = project_far(3, [here])
    body = mixed(rows_home, offsets, near, far[0] + far[1], others, spans[:2], margin, [far[3][0]])
    amplitude, energy = finish(
        rows_all,
        [here, there, body, denominator],
        near,
        straight,
        far[2] + far[3],
        tuple(size for _, size in spans[2:]),
    )
    return (amplitude.reshape(pair_count, pno_count * pno_count), energy.reshape(pair_count))


def solution(mesh):
    return jax.shard_map(
        on_device,
        mesh=mesh,
        in_specs=(
            P(None, "orb", "aux", None),
            P(("aux", "orb"), None, None),
            P(("aux", "orb"), None),
            P(("aux", "orb"), None, None, None),
            P(("aux", "orb"), None, None),
            P(),
            P(),
        ),
        out_specs=(P(("aux", "orb"), None), P(("aux", "orb"))),
        check_vma=False,
    )
```

```python
import functools

import jax
import jax.numpy as jnp
from jax import lax
from jax.experimental import pallas as pl
from jax.experimental.pallas import tpu as pltpu
from jax.sharding import PartitionSpec as P

SMEM = pl.BlockSpec(memory_space=pltpu.SMEM)
VMEM = pl.BlockSpec(memory_space=pltpu.VMEM)
ANY = pl.BlockSpec(memory_space=pl.ANY)


def copy(source, target, sem):
    return pltpu.make_async_copy(source, target, sem)


def pack_kernel(group, capacity, orbs, place, coef, *refs):
    outs, (held, count, holder, load_sem, store_sem) = refs[:-5], refs[-5:]
    load = copy(coef, held, load_sem)
    load.start()

    def clear(i, carry):
        holder[i] = 0
        return carry

    def clear_count(i, carry):
        count[i] = 0
        return carry

    def assign(s, carry):
        orb = orbs[s]
        at = count[orb]
        holder[orb * capacity + at] = s
        count[orb] = at + 1
        return carry

    lax.fori_loop(0, 2 * group * capacity, clear, 0)
    lax.fori_loop(0, 2 * group, clear_count, 0)
    lax.fori_loop(0, held.shape[0], assign, 0)
    load.wait()
    for mask, out in enumerate(outs):
        for kind in range(2):
            orb = place[1] ^ mask ^ (kind * (group + group // 2))

            def send(k, carry, orb=orb, kind=kind, out=out, sem=store_sem.at[mask]):
                copy(held.at[holder[orb * capacity + k]], out.at[kind * capacity + k], sem).start()
                return carry

            lax.fori_loop(0, capacity, send, 0)
    for mask, out in enumerate(outs):
        copy(held.at[pl.ds(0, 2 * capacity)], out, store_sem.at[mask]).wait()


def pack(orbs, place, coef, group, capacity):
    side_count, pno_count, dom_count = coef.shape
    block = jax.ShapeDtypeStruct((2 * capacity, pno_count, dom_count), coef.dtype)
    return pl.pallas_call(
        functools.partial(pack_kernel, group, capacity),
        out_shape=(block,) * group,
        in_specs=[SMEM, SMEM, ANY],
        out_specs=(ANY,) * group,
        scratch_shapes=[
            pltpu.VMEM(coef.shape, coef.dtype),
            pltpu.SMEM((2 * group,), jnp.int32),
            pltpu.SMEM((2 * group * capacity,), jnp.int32),
            pltpu.SemaphoreType.DMA,
            pltpu.SemaphoreType.DMA((group,)),
        ],
        cost_estimate=pl.CostEstimate(
            flops=0, transcendentals=0, bytes_accessed=6 * side_count * pno_count * dom_count
        ),
        name="pack",
    )(orbs, place, coef)


def project_kernel(group, capacity, direct, *refs):
    inner = group // 2
    blocks, parts, outs = refs[:group], refs[group : group + 2], refs[group + 2 :]
    row_count, half = parts[0].shape
    pno_count = outs[0].shape[1]
    step = row_count if row_count <= 640 else 256

    def tile(t, carry):
        at = t * step if isinstance(t, int) else pl.multiple_of(t * step, step)
        rows = [part[pl.ds(at, step), :] for part in parts]
        for i in range(inner):
            for j in range(2):
                lines = blocks[i + j * inner][...].reshape(capacity * pno_count, 2 * half)
                product = sum(
                    lax.dot_general(
                        lines[:, k * half : (k + 1) * half],
                        rows[k],
                        (((1,), (1,)), ((), ())),
                        preferred_element_type=jnp.float32,
                    )
                    for k in range(2)
                )
                out, first = (outs[i + j * inner], 0) if direct else (outs[i], j * capacity)
                out[first : first + capacity, :, pl.ds(at, step)] = product.astype(
                    out.dtype
                ).reshape(capacity, pno_count, step)
        return carry

    if row_count == step:
        tile(0, 0)
    else:
        lax.fori_loop(0, row_count // step, tile, 0)


def project(blocks, kind, parts, tokens, direct):
    group = len(blocks)
    inner = group // 2
    slots, pno_count, dom_count = blocks[0].shape
    capacity = slots // 2
    row_count = parts[0].shape[0]
    count, lines = (group, capacity) if direct else (inner, slots)

    def kernel(*refs):
        project_kernel(group, capacity, direct, *refs[: group + 2], *refs[-count:])

    block = pl.BlockSpec((capacity, pno_count, dom_count), lambda i: (kind, 0, 0))
    part = pl.BlockSpec(parts[0].shape, lambda i: (0, 0))
    return pl.pallas_call(
        kernel,
        grid=(1,),
        out_shape=(jax.ShapeDtypeStruct((lines, pno_count, row_count), blocks[0].dtype),) * count,
        in_specs=[block] * group + [part] * 2 + [ANY] * len(tokens),
        out_specs=(pl.BlockSpec((lines, pno_count, row_count), lambda i: (0, 0, 0)),) * count,
        compiler_params=pltpu.CompilerParams(vmem_limit_bytes=32 << 20),
        cost_estimate=pl.CostEstimate(
            flops=2 * group * capacity * pno_count * dom_count * row_count,
            transcendentals=0,
            bytes_accessed=2 * group * capacity * pno_count * dom_count,
        ),
    )(*blocks, *parts, *tokens)


def gather_sides(near, far, spans, slots, held, sem):
    inner = len(near)
    low, width = spans[0][0], sum(size for _, size in spans)
    for i in range(inner):
        copy(
            near[i].at[pl.ds(0, slots), :, pl.ds(low, width)],
            held.at[pl.ds(i * slots, slots)],
            sem,
        ).start()
        for c, (begin, size) in enumerate(spans):
            copy(
                far[c * inner + i].at[pl.ds(0, slots)],
                held.at[pl.ds((inner + i) * slots, slots), :, pl.ds(begin - low, size)],
                sem,
            ).start()


def overlap(first, second, limits, low):
    if low < limits[2]:
        lane = lax.broadcasted_iota(jnp.int32, (1, second.shape[1]), 1) + low
        apart = (lane < limits[0]) != (lane < limits[1])
        second = second * jnp.where(apart, 0.0, 1.0).astype(second.dtype)
    return lax.dot_general(
        first, second, (((1,), (1,)), ((), ())), preferred_element_type=jnp.float32
    )


def relay_kernel(inner, spans, margin, rows, offsets, before, *refs):
    near, far = refs[:inner], refs[inner : 2 * inner]
    sent, coupling, held, sem = refs[-4:]
    low = spans[0][0]
    pair_count = sent.shape[0]
    gather_sides(near, far, spans, near[0].shape[0], held, sem)
    copy(held, held, sem).wait()

    def choose(n, carry):
        sent[n] = held[jnp.maximum(jnp.maximum(rows[1, 2 * n], rows[1, 2 * n + 1]), 0)]
        return carry

    lax.fori_loop(0, pair_count, choose, 0, unroll=4)
    for h in range(2):

        def one_pair(n, carry, h=h):
            first, second = rows[h, 2 * n], rows[h, 2 * n + 1]
            product = overlap(
                held[jnp.maximum(first, 0)],
                held[jnp.maximum(second, 0)],
                (offsets[h, 2 * n], offsets[h, 2 * n + 1], margin),
                low,
            )
            product = jnp.where((first >= 0) & (second >= 0), product, 0.0)
            coupling[h, n] = product if low == 0 else product + before[h, n]
            return carry

        lax.fori_loop(0, pair_count, one_pair, 0, unroll=4)


def relay(rows, offsets, before, near, far, span, margin, tokens):
    inner = len(near)
    slots, pno_count, _ = near[0].shape
    pair_count = rows.shape[1] // 2
    return pl.pallas_call(
        functools.partial(relay_kernel, inner, (span,), margin),
        out_shape=(
            jax.ShapeDtypeStruct((pair_count, pno_count, span[1]), near[0].dtype),
            jax.ShapeDtypeStruct((2, pair_count, pno_count, pno_count), jnp.float32),
        ),
        in_specs=[SMEM, SMEM, VMEM] + [ANY] * (len(near) + len(far) + len(tokens)),
        out_specs=(VMEM, VMEM),
        scratch_shapes=[
            pltpu.VMEM((2 * inner * slots, pno_count, span[1]), near[0].dtype),
            pltpu.SemaphoreType.DMA,
        ],
        compiler_params=pltpu.CompilerParams(vmem_limit_bytes=24 << 20),
    )(rows, offsets, before, *near, *far, *tokens)


def mixed_pairs(inner, spans, margin, rows, offsets, near, far, others, held, sem, write):
    low = spans[0][0]
    slots = near[0].shape[0] // 2
    pair_count = others[0].shape[0]
    at = 2 * inner * slots
    gather_sides(near, far, spans, slots, held, sem)
    for other, (begin, size) in zip(others, spans):
        copy(
            other, held.at[pl.ds(at, pair_count), :, pl.ds(begin - low, size)], sem
        ).start()
    copy(held, held, sem).wait()

    def one_pair(n, carry):
        first, second = rows[0, 2 * n], rows[0, 2 * n + 1]
        product = overlap(
            held[jnp.where(first >= 0, first, at + n)],
            held[jnp.where(second >= 0, second, at + n)],
            (offsets[0, 2 * n], offsets[0, 2 * n + 1], margin),
            low,
        )
        write(n, jnp.where((first >= 0) != (second >= 0), product, 0.0))
        return carry

    lax.fori_loop(0, pair_count, one_pair, 0, unroll=4)


def mixed_kernel(inner, spans, margin, rows, offsets, *refs):
    near, refs = refs[:inner], refs[inner:]
    far, refs = refs[: inner * len(spans)], refs[inner * len(spans) :]
    others = refs[: len(spans)]
    coupling, held, sem = refs[-3:]

    def write(n, product):
        coupling[n] = product

    mixed_pairs(inner, spans, margin, rows, offsets, near, far, others, held, sem, write)


def finish_kernel(group, sizes, rows, here, there, before, denominator, *refs):
    inner = group // 2
    near, straight, far = refs[:inner], refs[inner:group], refs[group : group + group * len(sizes)]
    amplitude, energy, coupling, held, sem = refs[-5:]
    capacity, _, width = straight[0].shape
    low = near[0].shape[2] - width
    for m in range(group):
        source = straight[m - inner]
        if m < inner:
            source = near[m].at[pl.ds(0, capacity), :, pl.ds(low, width)]
        copy(source, held.at[pl.ds(m * capacity, capacity)], sem).start()
        at = 0
        for c, size in enumerate(sizes):
            copy(
                far[c * group + m],
                held.at[pl.ds((group + m) * capacity, capacity), :, pl.ds(at, size)],
                sem,
            ).start()
            at += size
    copy(held, held, sem).wait()

    def one_pair(n, carry):
        coupling[n] = lax.dot_general(
            held[rows[2 * n]],
            held[rows[2 * n + 1]],
            (((1,), (1,)), ((), ())),
            preferred_element_type=jnp.float32,
        )
        return carry

    lax.fori_loop(0, coupling.shape[0], one_pair, 0, unroll=4)
    total = coupling[...] + before[...] + here[0] + there[...]
    result = -total / denominator[...]
    amplitude[...] = result
    parts = total * (2.0 * result - jnp.swapaxes(result, 1, 2))
    energy[...] = jnp.sum(jnp.sum(parts, axis=1), axis=1, keepdims=True)


def finish(rows, finals, near, straight, far, sizes):
    group = 2 * len(near)
    capacity, pno_count, width = straight[0].shape
    pair_count = rows.shape[0] // 2
    square = jax.ShapeDtypeStruct((pair_count, pno_count, pno_count), jnp.float32)
    return pl.pallas_call(
        functools.partial(finish_kernel, group, sizes),
        out_shape=(square, jax.ShapeDtypeStruct((pair_count, 1), jnp.float32)),
        in_specs=[SMEM] + [VMEM] * len(finals) + [ANY] * (len(near) + len(straight) + len(far)),
        out_specs=(VMEM, VMEM),
        scratch_shapes=[
            pltpu.VMEM(square.shape, jnp.float32),
            pltpu.VMEM((2 * group * capacity, pno_count, width), near[0].dtype),
            pltpu.SemaphoreType.DMA,
        ],
        compiler_params=pltpu.CompilerParams(vmem_limit_bytes=24 << 20),
        name="finish",
    )(rows, *finals, *near, *straight, *far)


def mixed(rows, offsets, near, far, others, spans, margin, tokens):
    inner = len(near)
    slots, pno_count, _ = near[0].shape
    pair_count = rows.shape[1] // 2
    width = sum(size for _, size in spans)
    return pl.pallas_call(
        functools.partial(mixed_kernel, inner, tuple(spans), margin),
        out_shape=jax.ShapeDtypeStruct((pair_count, pno_count, pno_count), jnp.float32),
        in_specs=[SMEM] * 2 + [ANY] * (len(near) + len(far) + len(others) + len(tokens)),
        out_specs=VMEM,
        scratch_shapes=[
            pltpu.VMEM((inner * slots + pair_count, pno_count, width), near[0].dtype),
            pltpu.SemaphoreType.DMA,
        ],
        compiler_params=pltpu.CompilerParams(vmem_limit_bytes=24 << 20),
    )(rows, offsets, *near, *far, *others, *tokens)


def slots_of(orbs):
    sequence = jnp.arange(orbs.shape[1], dtype=jnp.int32)
    same = orbs[:, :, None] == orbs[:, None, :]
    earlier = sequence[None, None, :] < sequence[None, :, None]
    return jnp.sum(jnp.where(same & earlier, 1, 0), axis=2).astype(jnp.int32)


def chunk_spans(fit_rows):
    sizes = (fit_rows // 2, fit_rows // 8, fit_rows // 4, fit_rows // 8)
    return [(sum(sizes[:c]), size) for c, size in enumerate(sizes)]


def on_device(raw_ints, fit_inverse, pair_orbs, pno_coef, pno_energy, occ_energy, fit_offset):
    orb_count = lax.axis_size("orb")
    region, me = lax.axis_index("aux"), lax.axis_index("orb")
    group = orb_count // 2
    inner = group // 2
    pair_count = pair_orbs.shape[0]
    pno_count, dom_count = pno_coef.shape[2:]
    side_count = 2 * pair_count
    capacity = max(2, 4 * pair_count // orb_count)
    fit_rows = fit_inverse.shape[1]
    margin = fit_rows // 4

    def across(array, mask):
        return lax.ppermute(array, "orb", [(i, i ^ mask) for i in range(orb_count)])

    own_orbs = pair_orbs.reshape(side_count)
    place = jnp.stack([region, me]).astype(jnp.int32)
    half = dom_count // 2

    def exchange(array, k):
        part = lax.all_to_all(
            array[:, :, :, k * half : (k + 1) * half],
            "aux",
            split_axis=0,
            concat_axis=2,
            tiled=True,
        )
        return part[0, 0]

    raw_parts = [exchange(raw_ints, 0)]
    packed = pack(
        own_orbs, place, pno_coef.reshape(side_count, pno_count, dom_count), group, capacity
    )
    later, packed = lax.optimization_barrier((raw_ints, packed))
    raw_parts.append(exchange(later, 1))
    blocks = [packed[0]]
    for m in range(1, group):
        blocks.append(across(packed[m], m))
    pairs = [(i, i ^ inner) for i in range(orb_count) if i // inner in (0, 3)]
    guard = lax.ppermute(packed[0][:2], "orb", pairs)
    own_offset = fit_offset[region * orb_count + me]
    turned = jnp.roll(fit_inverse[0], own_offset, axis=0)
    mate_orbs = across(own_orbs, inner)
    orb_total = occ_energy.shape[0]

    def pick(values, chosen):
        selector = (region * orb_count + chosen)[:, None] == jnp.arange(orb_total, dtype=jnp.int32)
        return jnp.sum(jnp.where(selector, values[None, :], 0), axis=1)

    spans = chunk_spans(fit_rows)
    reverse = group + inner
    fitted, mirrored = [], [[None] * 2 for _ in spans]

    def mirror(c, k):
        begin, size = spans[c]
        mirrored[c][k] = across(fitted[k][begin : begin + size], reverse)

    for k in range(2):
        product = jnp.dot(turned, raw_parts[k], preferred_element_type=jnp.float32)
        fitted.append(product.astype(jnp.bfloat16))
        mirror(0, k)
    for c in range(1, len(spans)):
        mirror(c, 0)
        mirror(c, 1)

    energies, fitted[1] = lax.optimization_barrier((occ_energy, fitted[1]))
    occupied = pick(energies, own_orbs).reshape(pair_count, 2)
    denominator = (
        pno_energy[:, 0, :, None]
        + pno_energy[:, 1, None, :]
        - occupied[:, 0, None, None]
        - occupied[:, 1, None, None]
    )

    def hop(outs):
        return [outs[0]] + [across(outs[i], i) for i in range(1, inner)]

    def project_far(c, tokens):
        parts = project(blocks, 1, mirrored[c], tokens, c > 1)
        return hop(parts) if c < 2 else [parts[0]] + [across(parts[m], m) for m in range(1, group)]

    def pass_on(c, before, tokens):
        sent, here = relay(rows, offsets, before, near, far[c], spans[c], margin, tokens)
        return across(sent, inner), here

    near = project(blocks, 0, fitted, [denominator, guard], False)
    last = spans[2][0]
    straight = [across(near[i][capacity:, :, last:], i + inner) for i in range(inner)]
    near = hop(near)
    far, others = [None] * 4, [None] * 2
    far[0] = project_far(0, [])
    mate_orbs, far[0][0] = lax.optimization_barrier((mate_orbs, far[0][0]))
    orbs = jnp.stack([own_orbs, mate_orbs])
    differs = orbs ^ me
    other_half = (differs & group) != 0
    line = jnp.where(other_half, inner, 0) + (differs & (inner - 1))
    home = jnp.arange(2, dtype=jnp.int32)[:, None]
    position = slots_of(orbs)
    there = ((differs & inner) != 0) != other_half
    rows = jnp.where(there, -1, line * 2 * capacity + home * capacity + position)
    rows_home = jnp.where(there, -1, line * capacity + position)
    place_of = (differs[0] ^ jnp.where(other_half[0], reverse, 0)) + jnp.where(
        other_half[0], group, 0
    )
    rows_all = place_of * capacity + position[0]
    offsets = pick(fit_offset, orbs.reshape(2 * side_count)).reshape(2, side_count)
    others[0], here = pass_on(0, jnp.zeros((8, 128), jnp.float32), [])
    far[1] = project_far(1, [here])
    far[2] = project_far(2, [far[1][0]])
    others[1], here = pass_on(1, here, [far[2][0]])
    there = across(here[1], inner)
    far[3] = project_far(3, [here])
    body = mixed(rows_home, offsets, near, far[0] + far[1], others, spans[:2], margin, [far[3][0]])
    amplitude, energy = finish(
        rows_all,
        [here, there, body, denominator],
        near,
        straight,
        far[2] + far[3],
        tuple(size for _, size in spans[2:]),
    )
    return (amplitude.reshape(pair_count, pno_count * pno_count), energy.reshape(pair_count))


def solution(mesh):
    return jax.shard_map(
        on_device,
        mesh=mesh,
        in_specs=(
            P(None, "orb", "aux", None),
            P(("aux", "orb"), None, None),
            P(("aux", "orb"), None),
            P(("aux", "orb"), None, None, None),
            P(("aux", "orb"), None, None),
            P(),
            P(),
        ),
        out_specs=(P(("aux", "orb"), None), P(("aux", "orb"))),
        check_vma=False,
    )
```

```python
import functools

import jax
import jax.numpy as jnp
from jax import lax
from jax.experimental import pallas as pl
from jax.experimental.pallas import tpu as pltpu
from jax.sharding import PartitionSpec as P

SMEM = pl.BlockSpec(memory_space=pltpu.SMEM)
VMEM = pl.BlockSpec(memory_space=pltpu.VMEM)
ANY = pl.BlockSpec(memory_space=pl.ANY)


def copy(source, target, sem):
    return pltpu.make_async_copy(source, target, sem)


def pack_kernel(group, capacity, masks, orbs, place, coef, *refs):
    outs, (held, count, holder, load_sem, store_sem) = refs[:-5], refs[-5:]
    load = copy(coef, held, load_sem)
    load.start()

    def clear(i, carry):
        holder[i] = 0
        return carry

    def clear_count(i, carry):
        count[i] = 0
        return carry

    def assign(s, carry):
        orb = orbs[s]
        at = count[orb]
        holder[orb * capacity + at] = s
        count[orb] = at + 1
        return carry

    lax.fori_loop(0, 2 * group * capacity, clear, 0)
    lax.fori_loop(0, 2 * group, clear_count, 0)
    lax.fori_loop(0, held.shape[0], assign, 0)
    load.wait()
    for at, (mask, out) in enumerate(zip(masks, outs)):
        for kind in range(2):
            orb = place[1] ^ mask ^ (kind * (group + group // 2))

            def send(k, carry, orb=orb, kind=kind, out=out, sem=store_sem.at[at]):
                copy(held.at[holder[orb * capacity + k]], out.at[kind * capacity + k], sem).start()
                return carry

            lax.fori_loop(0, capacity, send, 0)
    for at, out in enumerate(outs):
        copy(held.at[pl.ds(0, 2 * capacity)], out, store_sem.at[at]).wait()


def pack(orbs, place, coef, group, capacity, masks):
    side_count, pno_count, dom_count = coef.shape
    block = jax.ShapeDtypeStruct((2 * capacity, pno_count, dom_count), coef.dtype)
    return pl.pallas_call(
        functools.partial(pack_kernel, group, capacity, masks),
        out_shape=(block,) * len(masks),
        in_specs=[SMEM, SMEM, ANY],
        out_specs=(ANY,) * len(masks),
        scratch_shapes=[
            pltpu.VMEM(coef.shape, coef.dtype),
            pltpu.SMEM((2 * group,), jnp.int32),
            pltpu.SMEM((2 * group * capacity,), jnp.int32),
            pltpu.SemaphoreType.DMA,
            pltpu.SemaphoreType.DMA((len(masks),)),
        ],
        cost_estimate=pl.CostEstimate(
            flops=0, transcendentals=0, bytes_accessed=6 * side_count * pno_count * dom_count
        ),
    )(orbs, place, coef)


def project_kernel(group, capacity, direct, *refs):
    inner = group // 2
    blocks, parts, outs = refs[:group], refs[group : group + 2], refs[group + 2 :]
    row_count, half = parts[0].shape
    pno_count = outs[0].shape[1]
    step = row_count if row_count <= 640 else 256

    def tile(t, carry):
        at = t * step if isinstance(t, int) else pl.multiple_of(t * step, step)
        rows = [part[pl.ds(at, step), :] for part in parts]
        for i in range(inner):
            for j in range(2):
                lines = blocks[i + j * inner][...].reshape(capacity * pno_count, 2 * half)
                product = sum(
                    lax.dot_general(
                        lines[:, k * half : (k + 1) * half],
                        rows[k],
                        (((1,), (1,)), ((), ())),
                        preferred_element_type=jnp.float32,
                    )
                    for k in range(2)
                )
                out, first = (outs[i + j * inner], 0) if direct else (outs[i], j * capacity)
                out[first : first + capacity, :, pl.ds(at, step)] = product.astype(
                    out.dtype
                ).reshape(capacity, pno_count, step)
        return carry

    if row_count == step:
        tile(0, 0)
    else:
        lax.fori_loop(0, row_count // step, tile, 0)


def project(blocks, kind, parts, tokens, direct):
    group = len(blocks)
    inner = group // 2
    slots, pno_count, dom_count = blocks[0].shape
    capacity = slots // 2
    row_count = parts[0].shape[0]
    count, lines = (group, capacity) if direct else (inner, slots)

    def kernel(*refs):
        project_kernel(group, capacity, direct, *refs[: group + 2], *refs[-count:])

    block = pl.BlockSpec((capacity, pno_count, dom_count), lambda i: (kind, 0, 0))
    part = pl.BlockSpec(parts[0].shape, lambda i: (0, 0))
    return pl.pallas_call(
        kernel,
        grid=(1,),
        out_shape=(jax.ShapeDtypeStruct((lines, pno_count, row_count), blocks[0].dtype),) * count,
        in_specs=[block] * group + [part] * 2 + [ANY] * len(tokens),
        out_specs=(pl.BlockSpec((lines, pno_count, row_count), lambda i: (0, 0, 0)),) * count,
        compiler_params=pltpu.CompilerParams(vmem_limit_bytes=32 << 20),
        cost_estimate=pl.CostEstimate(
            flops=2 * group * capacity * pno_count * dom_count * row_count,
            transcendentals=0,
            bytes_accessed=2 * group * capacity * pno_count * dom_count,
        ),
    )(*blocks, *parts, *tokens)


def gather_sides(near, far, spans, slots, held, sem):
    inner = len(near)
    low, width = spans[0][0], sum(size for _, size in spans)
    for i in range(inner):
        copy(
            near[i].at[pl.ds(0, slots), :, pl.ds(low, width)],
            held.at[pl.ds(i * slots, slots)],
            sem,
        ).start()
        for c, (begin, size) in enumerate(spans):
            copy(
                far[c * inner + i].at[pl.ds(0, slots)],
                held.at[pl.ds((inner + i) * slots, slots), :, pl.ds(begin - low, size)],
                sem,
            ).start()


def overlap(first, second, limits, low):
    if low < limits[2]:
        lane = lax.broadcasted_iota(jnp.int32, (1, second.shape[1]), 1) + low
        apart = (lane < limits[0]) != (lane < limits[1])
        second = second * jnp.where(apart, 0.0, 1.0).astype(second.dtype)
    return lax.dot_general(
        first, second, (((1,), (1,)), ((), ())), preferred_element_type=jnp.float32
    )


def relay_kernel(inner, spans, margin, rows, offsets, before, *refs):
    near, far = refs[:inner], refs[inner : 2 * inner]
    sent, coupling, held, sem = refs[-4:]
    low = spans[0][0]
    pair_count = sent.shape[0]
    gather_sides(near, far, spans, near[0].shape[0], held, sem)
    copy(held, held, sem).wait()

    def choose(n, carry):
        sent[n] = held[jnp.maximum(jnp.maximum(rows[1, 2 * n], rows[1, 2 * n + 1]), 0)]
        return carry

    lax.fori_loop(0, pair_count, choose, 0, unroll=4)
    for h in range(2):

        def one_pair(n, carry, h=h):
            first, second = rows[h, 2 * n], rows[h, 2 * n + 1]
            product = overlap(
                held[jnp.maximum(first, 0)],
                held[jnp.maximum(second, 0)],
                (offsets[h, 2 * n], offsets[h, 2 * n + 1], margin),
                low,
            )
            product = jnp.where((first >= 0) & (second >= 0), product, 0.0)
            coupling[h, n] = product if low == 0 else product + before[h, n]
            return carry

        lax.fori_loop(0, pair_count, one_pair, 0, unroll=4)


def relay(rows, offsets, before, near, far, span, margin, tokens):
    inner = len(near)
    slots, pno_count, _ = near[0].shape
    pair_count = rows.shape[1] // 2
    return pl.pallas_call(
        functools.partial(relay_kernel, inner, (span,), margin),
        out_shape=(
            jax.ShapeDtypeStruct((pair_count, pno_count, span[1]), near[0].dtype),
            jax.ShapeDtypeStruct((2, pair_count, pno_count, pno_count), jnp.float32),
        ),
        in_specs=[SMEM, SMEM, VMEM] + [ANY] * (len(near) + len(far) + len(tokens)),
        out_specs=(VMEM, VMEM),
        scratch_shapes=[
            pltpu.VMEM((2 * inner * slots, pno_count, span[1]), near[0].dtype),
            pltpu.SemaphoreType.DMA,
        ],
        compiler_params=pltpu.CompilerParams(vmem_limit_bytes=24 << 20),
    )(rows, offsets, before, *near, *far, *tokens)


def mixed_pairs(inner, spans, margin, rows, offsets, near, far, others, held, sem, write):
    low = spans[0][0]
    slots = near[0].shape[0] // 2
    pair_count = others[0].shape[0]
    at = 2 * inner * slots
    gather_sides(near, far, spans, slots, held, sem)
    for other, (begin, size) in zip(others, spans):
        copy(
            other, held.at[pl.ds(at, pair_count), :, pl.ds(begin - low, size)], sem
        ).start()
    copy(held, held, sem).wait()

    def one_pair(n, carry):
        first, second = rows[0, 2 * n], rows[0, 2 * n + 1]
        product = overlap(
            held[jnp.where(first >= 0, first, at + n)],
            held[jnp.where(second >= 0, second, at + n)],
            (offsets[0, 2 * n], offsets[0, 2 * n + 1], margin),
            low,
        )
        write(n, jnp.where((first >= 0) != (second >= 0), product, 0.0))
        return carry

    lax.fori_loop(0, pair_count, one_pair, 0, unroll=4)


def mixed_kernel(inner, spans, margin, rows, offsets, *refs):
    near, refs = refs[:inner], refs[inner:]
    far, refs = refs[: inner * len(spans)], refs[inner * len(spans) :]
    others = refs[: len(spans)]
    coupling, held, sem = refs[-3:]

    def write(n, product):
        coupling[n] = product

    mixed_pairs(inner, spans, margin, rows, offsets, near, far, others, held, sem, write)


def finish_kernel(group, sizes, rows, here, there, before, denominator, *refs):
    inner = group // 2
    near, straight, far = refs[:inner], refs[inner:group], refs[group : group + group * len(sizes)]
    amplitude, energy, coupling, held, sem = refs[-5:]
    capacity, _, width = straight[0].shape
    low = near[0].shape[2] - width
    for m in range(group):
        source = straight[m - inner]
        if m < inner:
            source = near[m].at[pl.ds(0, capacity), :, pl.ds(low, width)]
        copy(source, held.at[pl.ds(m * capacity, capacity)], sem).start()
        at = 0
        for c, size in enumerate(sizes):
            copy(
                far[c * group + m],
                held.at[pl.ds((group + m) * capacity, capacity), :, pl.ds(at, size)],
                sem,
            ).start()
            at += size
    copy(held, held, sem).wait()

    def one_pair(n, carry):
        coupling[n] = lax.dot_general(
            held[rows[2 * n]],
            held[rows[2 * n + 1]],
            (((1,), (1,)), ((), ())),
            preferred_element_type=jnp.float32,
        )
        return carry

    lax.fori_loop(0, coupling.shape[0], one_pair, 0, unroll=4)
    total = coupling[...] + before[...] + here[0] + there[...]
    result = -total / denominator[...]
    count = result.shape[1]
    for p in range(count):
        amplitude[:, p * count : (p + 1) * count] = result[:, p, :]
    parts = total * (2.0 * result - jnp.swapaxes(result, 1, 2))
    energy[...] = jnp.sum(jnp.sum(parts, axis=1), axis=1)


def finish(rows, finals, near, straight, far, sizes):
    group = 2 * len(near)
    capacity, pno_count, width = straight[0].shape
    pair_count = rows.shape[0] // 2
    square = jax.ShapeDtypeStruct((pair_count, pno_count, pno_count), jnp.float32)
    return pl.pallas_call(
        functools.partial(finish_kernel, group, sizes),
        out_shape=(
            jax.ShapeDtypeStruct((pair_count, pno_count * pno_count), jnp.float32),
            jax.ShapeDtypeStruct((pair_count,), jnp.float32),
        ),
        in_specs=[SMEM] + [VMEM] * len(finals) + [ANY] * (len(near) + len(straight) + len(far)),
        out_specs=(VMEM, VMEM),
        scratch_shapes=[
            pltpu.VMEM(square.shape, jnp.float32),
            pltpu.VMEM((2 * group * capacity, pno_count, width), near[0].dtype),
            pltpu.SemaphoreType.DMA,
        ],
        compiler_params=pltpu.CompilerParams(vmem_limit_bytes=24 << 20),
        name="finish",
    )(rows, *finals, *near, *straight, *far)


def mixed(rows, offsets, near, far, others, spans, margin, tokens):
    inner = len(near)
    slots, pno_count, _ = near[0].shape
    pair_count = rows.shape[1] // 2
    width = sum(size for _, size in spans)
    return pl.pallas_call(
        functools.partial(mixed_kernel, inner, tuple(spans), margin),
        out_shape=jax.ShapeDtypeStruct((pair_count, pno_count, pno_count), jnp.float32),
        in_specs=[SMEM] * 2 + [ANY] * (len(near) + len(far) + len(others) + len(tokens)),
        out_specs=VMEM,
        scratch_shapes=[
            pltpu.VMEM((inner * slots + pair_count, pno_count, width), near[0].dtype),
            pltpu.SemaphoreType.DMA,
        ],
        compiler_params=pltpu.CompilerParams(vmem_limit_bytes=24 << 20),
    )(rows, offsets, *near, *far, *others, *tokens)


def slots_of(orbs):
    sequence = jnp.arange(orbs.shape[1], dtype=jnp.int32)
    same = orbs[:, :, None] == orbs[:, None, :]
    earlier = sequence[None, None, :] < sequence[None, :, None]
    return jnp.sum(jnp.where(same & earlier, 1, 0), axis=2).astype(jnp.int32)


def chunk_spans(fit_rows):
    sizes = (fit_rows // 2, fit_rows // 8, fit_rows // 4, fit_rows // 8)
    return [(sum(sizes[:c]), size) for c, size in enumerate(sizes)]


def on_device(raw_ints, fit_inverse, pair_orbs, pno_coef, pno_energy, occ_energy, fit_offset):
    orb_count = lax.axis_size("orb")
    region, me = lax.axis_index("aux"), lax.axis_index("orb")
    group = orb_count // 2
    inner = group // 2
    pair_count = pair_orbs.shape[0]
    pno_count, dom_count = pno_coef.shape[2:]
    side_count = 2 * pair_count
    capacity = max(2, 4 * pair_count // orb_count)
    fit_rows = fit_inverse.shape[1]
    margin = fit_rows // 4

    def across(array, mask):
        return lax.ppermute(array, "orb", [(i, i ^ mask) for i in range(orb_count)])

    own_orbs = pair_orbs.reshape(side_count)
    place = jnp.stack([region, me]).astype(jnp.int32)
    half = dom_count // 2

    def exchange(array, k):
        part = lax.all_to_all(
            array[:, :, :, k * half : (k + 1) * half],
            "aux",
            split_axis=0,
            concat_axis=2,
            tiled=True,
        )
        return part[0, 0]

    raw_parts = [exchange(raw_ints, 0)]
    coef = pno_coef.reshape(side_count, pno_count, dom_count)
    blocks = [None] * group
    packed = pack(own_orbs, place, coef, group, capacity, tuple(range(inner, group)))
    for m in range(inner, group):
        blocks[m] = across(packed[m - inner], m)
    pairs = [(i, i ^ inner) for i in range(orb_count) if i // inner in (0, 3)]
    guard = lax.ppermute(packed[0][:1], "orb", pairs)
    packed = pack(own_orbs, place, coef, group, capacity, tuple(range(inner)))
    blocks[0] = packed[0]
    for m in range(1, inner):
        blocks[m] = across(packed[m], m)
    later, blocks[0] = lax.optimization_barrier((raw_ints, blocks[0]))
    raw_parts.append(exchange(later, 1))
    own_offset = fit_offset[region * orb_count + me]
    turned = jnp.roll(fit_inverse[0], own_offset, axis=0)
    mate_orbs = across(own_orbs, inner)
    orb_total = occ_energy.shape[0]

    def pick(values, chosen):
        selector = (region * orb_count + chosen)[:, None] == jnp.arange(orb_total, dtype=jnp.int32)
        return jnp.sum(jnp.where(selector, values[None, :], 0), axis=1)

    spans = chunk_spans(fit_rows)
    reverse = group + inner
    fitted, mirrored = [], [[None] * 2 for _ in spans]

    def mirror(c, k):
        begin, size = spans[c]
        mirrored[c][k] = across(fitted[k][begin : begin + size], reverse)

    for k in range(2):
        product = jnp.dot(turned, raw_parts[k], preferred_element_type=jnp.float32)
        fitted.append(product.astype(jnp.bfloat16))
        mirror(0, k)
    for c in range(1, len(spans)):
        mirror(c, 0)
        mirror(c, 1)

    energies, levels, named, fitted[1] = lax.optimization_barrier(
        (occ_energy, pno_energy, own_orbs, fitted[1])
    )
    occupied = pick(energies, named).reshape(pair_count, 2)
    denominator = (
        levels[:, 0, :, None]
        + levels[:, 1, None, :]
        - occupied[:, 0, None, None]
        - occupied[:, 1, None, None]
    )

    def hop(outs):
        return [outs[0]] + [across(outs[i], i) for i in range(1, inner)]

    def project_far(c, tokens):
        parts = project(blocks, 1, mirrored[c], tokens, c > 1)
        return hop(parts) if c < 2 else [parts[0]] + [across(parts[m], m) for m in range(1, group)]

    def pass_on(c, before, tokens):
        sent, here = relay(rows, offsets, before, near, far[c], spans[c], margin, tokens)
        return across(sent, inner), here

    near = project(blocks, 0, fitted, [denominator, guard], False)
    last = spans[2][0]
    straight = [across(near[i][capacity:, :, last:], i + inner) for i in range(inner)]
    near = hop(near)
    far, others = [None] * 4, [None] * 2
    far[0] = project_far(0, [])
    mate_orbs, far[0][0] = lax.optimization_barrier((mate_orbs, far[0][0]))
    orbs = jnp.stack([own_orbs, mate_orbs])
    differs = orbs ^ me
    other_half = (differs & group) != 0
    line = jnp.where(other_half, inner, 0) + (differs & (inner - 1))
    home = jnp.arange(2, dtype=jnp.int32)[:, None]
    position = slots_of(orbs)
    there = ((differs & inner) != 0) != other_half
    rows = jnp.where(there, -1, line * 2 * capacity + home * capacity + position)
    rows_home = jnp.where(there, -1, line * capacity + position)
    place_of = (differs[0] ^ jnp.where(other_half[0], reverse, 0)) + jnp.where(
        other_half[0], group, 0
    )
    rows_all = place_of * capacity + position[0]
    offsets = pick(fit_offset, orbs.reshape(2 * side_count)).reshape(2, side_count)
    others[0], here = pass_on(0, jnp.zeros((8, 128), jnp.float32), [])
    far[1] = project_far(1, [here])
    far[2] = project_far(2, [far[1][0]])
    others[1], here = pass_on(1, here, [far[2][0]])
    there = across(here[1], inner)
    far[3] = project_far(3, [here])
    body = mixed(rows_home, offsets, near, far[0] + far[1], others, spans[:2], margin, [far[3][0]])
    amplitude, energy = finish(
        rows_all,
        [here, there, body, denominator],
        near,
        straight,
        far[2] + far[3],
        tuple(size for _, size in spans[2:]),
    )
    return amplitude, energy


def solution(mesh):
    return jax.shard_map(
        on_device,
        mesh=mesh,
        in_specs=(
            P(None, "orb", "aux", None),
            P(("aux", "orb"), None, None),
            P(("aux", "orb"), None),
            P(("aux", "orb"), None, None, None),
            P(("aux", "orb"), None, None),
            P(),
            P(),
        ),
        out_specs=(P(("aux", "orb"), None), P(("aux", "orb"))),
        check_vma=False,
    )
```

```python
import functools

import jax
import jax.numpy as jnp
from jax import lax
from jax.experimental import pallas as pl
from jax.experimental.pallas import tpu as pltpu
from jax.sharding import PartitionSpec as P

SMEM = pl.BlockSpec(memory_space=pltpu.SMEM)
VMEM = pl.BlockSpec(memory_space=pltpu.VMEM)
ANY = pl.BlockSpec(memory_space=pl.ANY)


def copy(source, target, sem):
    return pltpu.make_async_copy(source, target, sem)


def pack_kernel(group, capacity, masks, orbs, place, coef, *refs):
    outs, (held, count, holder, load_sem, store_sem) = refs[:-5], refs[-5:]
    load = copy(coef, held, load_sem)
    load.start()

    def clear(i, carry):
        holder[i] = 0
        return carry

    def clear_count(i, carry):
        count[i] = 0
        return carry

    def assign(s, carry):
        orb = orbs[s]
        at = count[orb]
        holder[orb * capacity + at] = s
        count[orb] = at + 1
        return carry

    lax.fori_loop(0, 2 * group * capacity, clear, 0)
    lax.fori_loop(0, 2 * group, clear_count, 0)
    lax.fori_loop(0, held.shape[0], assign, 0)
    load.wait()
    for at, (mask, out) in enumerate(zip(masks, outs)):
        for kind in range(2):
            orb = place[1] ^ mask ^ (kind * (group + group // 2))

            def send(k, carry, orb=orb, kind=kind, out=out, sem=store_sem.at[at]):
                copy(held.at[holder[orb * capacity + k]], out.at[kind * capacity + k], sem).start()
                return carry

            lax.fori_loop(0, capacity, send, 0)
    for at, out in enumerate(outs):
        copy(held.at[pl.ds(0, 2 * capacity)], out, store_sem.at[at]).wait()


def pack(orbs, place, coef, group, capacity, masks):
    side_count, pno_count, dom_count = coef.shape
    block = jax.ShapeDtypeStruct((2 * capacity, pno_count, dom_count), coef.dtype)
    return pl.pallas_call(
        functools.partial(pack_kernel, group, capacity, masks),
        out_shape=(block,) * len(masks),
        in_specs=[SMEM, SMEM, ANY],
        out_specs=(ANY,) * len(masks),
        scratch_shapes=[
            pltpu.VMEM(coef.shape, coef.dtype),
            pltpu.SMEM((2 * group,), jnp.int32),
            pltpu.SMEM((2 * group * capacity,), jnp.int32),
            pltpu.SemaphoreType.DMA,
            pltpu.SemaphoreType.DMA((len(masks),)),
        ],
        cost_estimate=pl.CostEstimate(
            flops=0, transcendentals=0, bytes_accessed=6 * side_count * pno_count * dom_count
        ),
    )(orbs, place, coef)


def project_kernel(group, capacity, direct, *refs):
    inner = group // 2
    blocks, parts, outs = refs[:group], refs[group : group + 2], refs[group + 2 :]
    row_count, half = parts[0].shape
    pno_count = outs[0].shape[1]
    step = row_count if row_count <= 640 else 256

    def tile(t, carry):
        at = t * step if isinstance(t, int) else pl.multiple_of(t * step, step)
        rows = [part[pl.ds(at, step), :] for part in parts]
        for i in range(inner):
            for j in range(2):
                lines = blocks[i + j * inner][...].reshape(capacity * pno_count, 2 * half)
                product = sum(
                    lax.dot_general(
                        lines[:, k * half : (k + 1) * half],
                        rows[k],
                        (((1,), (1,)), ((), ())),
                        preferred_element_type=jnp.float32,
                    )
                    for k in range(2)
                )
                out, first = (outs[i + j * inner], 0) if direct else (outs[i], j * capacity)
                out[first : first + capacity, :, pl.ds(at, step)] = product.astype(
                    out.dtype
                ).reshape(capacity, pno_count, step)
        return carry

    if row_count == step:
        tile(0, 0)
    else:
        lax.fori_loop(0, row_count // step, tile, 0)


def project(blocks, kind, parts, tokens, direct):
    group = len(blocks)
    inner = group // 2
    slots, pno_count, dom_count = blocks[0].shape
    capacity = slots // 2
    row_count = parts[0].shape[0]
    count, lines = (group, capacity) if direct else (inner, slots)

    def kernel(*refs):
        project_kernel(group, capacity, direct, *refs[: group + 2], *refs[-count:])

    block = pl.BlockSpec((capacity, pno_count, dom_count), lambda i: (kind, 0, 0))
    part = pl.BlockSpec(parts[0].shape, lambda i: (0, 0))
    return pl.pallas_call(
        kernel,
        grid=(1,),
        out_shape=(jax.ShapeDtypeStruct((lines, pno_count, row_count), blocks[0].dtype),) * count,
        in_specs=[block] * group + [part] * 2 + [ANY] * len(tokens),
        out_specs=(pl.BlockSpec((lines, pno_count, row_count), lambda i: (0, 0, 0)),) * count,
        compiler_params=pltpu.CompilerParams(vmem_limit_bytes=32 << 20),
        cost_estimate=pl.CostEstimate(
            flops=2 * group * capacity * pno_count * dom_count * row_count,
            transcendentals=0,
            bytes_accessed=2 * group * capacity * pno_count * dom_count,
        ),
    )(*blocks, *parts, *tokens)


def gather_sides(near, far, spans, slots, held, sem):
    inner = len(near)
    low, width = spans[0][0], sum(size for _, size in spans)
    for i in range(inner):
        copy(
            near[i].at[pl.ds(0, slots), :, pl.ds(low, width)],
            held.at[pl.ds(i * slots, slots)],
            sem,
        ).start()
        for c, (begin, size) in enumerate(spans):
            copy(
                far[c * inner + i].at[pl.ds(0, slots)],
                held.at[pl.ds((inner + i) * slots, slots), :, pl.ds(begin - low, size)],
                sem,
            ).start()


def overlap(first, second, limits, low):
    if low < limits[2]:
        lane = lax.broadcasted_iota(jnp.int32, (1, second.shape[1]), 1) + low
        apart = (lane < limits[0]) != (lane < limits[1])
        second = second * jnp.where(apart, 0.0, 1.0).astype(second.dtype)
    return lax.dot_general(
        first, second, (((1,), (1,)), ((), ())), preferred_element_type=jnp.float32
    )


def relay_kernel(inner, spans, margin, rows, offsets, before, *refs):
    near, far = refs[:inner], refs[inner : 2 * inner]
    sent, coupling, held, sem = refs[-4:]
    low = spans[0][0]
    pair_count = sent.shape[0]
    gather_sides(near, far, spans, near[0].shape[0], held, sem)
    copy(held, held, sem).wait()

    def choose(n, carry):
        sent[n] = held[jnp.maximum(jnp.maximum(rows[1, 2 * n], rows[1, 2 * n + 1]), 0)]
        return carry

    lax.fori_loop(0, pair_count, choose, 0, unroll=4)
    for h in range(2):

        def one_pair(n, carry, h=h):
            first, second = rows[h, 2 * n], rows[h, 2 * n + 1]
            product = overlap(
                held[jnp.maximum(first, 0)],
                held[jnp.maximum(second, 0)],
                (offsets[h, 2 * n], offsets[h, 2 * n + 1], margin),
                low,
            )
            product = jnp.where((first >= 0) & (second >= 0), product, 0.0)
            coupling[h, n] = product if low == 0 else product + before[h, n]
            return carry

        lax.fori_loop(0, pair_count, one_pair, 0, unroll=4)


def relay(rows, offsets, before, near, far, span, margin, tokens):
    inner = len(near)
    slots, pno_count, _ = near[0].shape
    pair_count = rows.shape[1] // 2
    return pl.pallas_call(
        functools.partial(relay_kernel, inner, (span,), margin),
        out_shape=(
            jax.ShapeDtypeStruct((pair_count, pno_count, span[1]), near[0].dtype),
            jax.ShapeDtypeStruct((2, pair_count, pno_count, pno_count), jnp.float32),
        ),
        in_specs=[SMEM, SMEM, VMEM] + [ANY] * (len(near) + len(far) + len(tokens)),
        out_specs=(VMEM, VMEM),
        scratch_shapes=[
            pltpu.VMEM((2 * inner * slots, pno_count, span[1]), near[0].dtype),
            pltpu.SemaphoreType.DMA,
        ],
        compiler_params=pltpu.CompilerParams(vmem_limit_bytes=24 << 20),
    )(rows, offsets, before, *near, *far, *tokens)


def mixed_pairs(inner, spans, margin, rows, offsets, near, far, others, held, sem, write):
    low = spans[0][0]
    slots = near[0].shape[0] // 2
    pair_count = others[0].shape[0]
    at = 2 * inner * slots
    gather_sides(near, far, spans, slots, held, sem)
    for other, (begin, size) in zip(others, spans):
        copy(
            other, held.at[pl.ds(at, pair_count), :, pl.ds(begin - low, size)], sem
        ).start()
    copy(held, held, sem).wait()

    def one_pair(n, carry):
        first, second = rows[0, 2 * n], rows[0, 2 * n + 1]
        product = overlap(
            held[jnp.where(first >= 0, first, at + n)],
            held[jnp.where(second >= 0, second, at + n)],
            (offsets[0, 2 * n], offsets[0, 2 * n + 1], margin),
            low,
        )
        write(n, jnp.where((first >= 0) != (second >= 0), product, 0.0))
        return carry

    lax.fori_loop(0, pair_count, one_pair, 0, unroll=4)


def mixed_kernel(inner, spans, margin, rows, offsets, *refs):
    near, refs = refs[:inner], refs[inner:]
    far, refs = refs[: inner * len(spans)], refs[inner * len(spans) :]
    others = refs[: len(spans)]
    coupling, held, sem = refs[-3:]

    def write(n, product):
        coupling[n] = product

    mixed_pairs(inner, spans, margin, rows, offsets, near, far, others, held, sem, write)


def finish_kernel(group, sizes, rows, here, there, before, denominator, *refs):
    inner = group // 2
    near, straight, far = refs[:inner], refs[inner:group], refs[group : group + group * len(sizes)]
    amplitude, energy, coupling, held, sem = refs[-5:]
    capacity, _, width = straight[0].shape
    low = near[0].shape[2] - width
    for m in range(group):
        source = straight[m - inner]
        if m < inner:
            source = near[m].at[pl.ds(0, capacity), :, pl.ds(low, width)]
        copy(source, held.at[pl.ds(m * capacity, capacity)], sem).start()
        at = 0
        for c, size in enumerate(sizes):
            copy(
                far[c * group + m],
                held.at[pl.ds((group + m) * capacity, capacity), :, pl.ds(at, size)],
                sem,
            ).start()
            at += size
    copy(held, held, sem).wait()

    def one_pair(n, carry):
        coupling[n] = lax.dot_general(
            held[rows[2 * n]],
            held[rows[2 * n + 1]],
            (((1,), (1,)), ((), ())),
            preferred_element_type=jnp.float32,
        )
        return carry

    lax.fori_loop(0, coupling.shape[0], one_pair, 0, unroll=4)
    total = coupling[...] + before[...] + here[0] + there[...]
    result = -total / denominator[...]
    count = result.shape[1]
    for p in range(count):
        amplitude[:, p * count : (p + 1) * count] = result[:, p, :]
    parts = total * (2.0 * result - jnp.swapaxes(result, 1, 2))
    energy[...] = jnp.sum(jnp.sum(parts, axis=1), axis=1)


def finish(rows, finals, near, straight, far, sizes):
    group = 2 * len(near)
    capacity, pno_count, width = straight[0].shape
    pair_count = rows.shape[0] // 2
    square = jax.ShapeDtypeStruct((pair_count, pno_count, pno_count), jnp.float32)
    return pl.pallas_call(
        functools.partial(finish_kernel, group, sizes),
        out_shape=(
            jax.ShapeDtypeStruct((pair_count, pno_count * pno_count), jnp.float32),
            jax.ShapeDtypeStruct((pair_count,), jnp.float32),
        ),
        in_specs=[SMEM] + [VMEM] * len(finals) + [ANY] * (len(near) + len(straight) + len(far)),
        out_specs=(VMEM, VMEM),
        scratch_shapes=[
            pltpu.VMEM(square.shape, jnp.float32),
            pltpu.VMEM((2 * group * capacity, pno_count, width), near[0].dtype),
            pltpu.SemaphoreType.DMA,
        ],
        compiler_params=pltpu.CompilerParams(vmem_limit_bytes=24 << 20),
        name="finish",
    )(rows, *finals, *near, *straight, *far)


def mixed(rows, offsets, near, far, others, spans, margin, tokens):
    inner = len(near)
    slots, pno_count, _ = near[0].shape
    pair_count = rows.shape[1] // 2
    width = sum(size for _, size in spans)
    return pl.pallas_call(
        functools.partial(mixed_kernel, inner, tuple(spans), margin),
        out_shape=jax.ShapeDtypeStruct((pair_count, pno_count, pno_count), jnp.float32),
        in_specs=[SMEM] * 2 + [ANY] * (len(near) + len(far) + len(others) + len(tokens)),
        out_specs=VMEM,
        scratch_shapes=[
            pltpu.VMEM((inner * slots + pair_count, pno_count, width), near[0].dtype),
            pltpu.SemaphoreType.DMA,
        ],
        compiler_params=pltpu.CompilerParams(vmem_limit_bytes=24 << 20),
    )(rows, offsets, *near, *far, *others, *tokens)


def slots_of(orbs):
    sequence = jnp.arange(orbs.shape[1], dtype=jnp.int32)
    same = orbs[:, :, None] == orbs[:, None, :]
    earlier = sequence[None, None, :] < sequence[None, :, None]
    return jnp.sum(jnp.where(same & earlier, 1, 0), axis=2).astype(jnp.int32)


def chunk_spans(fit_rows):
    sizes = (fit_rows // 2, fit_rows // 4, fit_rows // 8, fit_rows // 8)
    return [(sum(sizes[:c]), size) for c, size in enumerate(sizes)]


def on_device(raw_ints, fit_inverse, pair_orbs, pno_coef, pno_energy, occ_energy, fit_offset):
    orb_count = lax.axis_size("orb")
    region, me = lax.axis_index("aux"), lax.axis_index("orb")
    group = orb_count // 2
    inner = group // 2
    pair_count = pair_orbs.shape[0]
    pno_count, dom_count = pno_coef.shape[2:]
    side_count = 2 * pair_count
    capacity = max(2, 4 * pair_count // orb_count)
    fit_rows = fit_inverse.shape[1]
    margin = fit_rows // 4

    def across(array, mask):
        return lax.ppermute(array, "orb", [(i, i ^ mask) for i in range(orb_count)])

    own_orbs = pair_orbs.reshape(side_count)
    place = jnp.stack([region, me]).astype(jnp.int32)
    half = dom_count // 2

    def exchange(array, k):
        part = lax.all_to_all(
            array[:, :, :, k * half : (k + 1) * half],
            "aux",
            split_axis=0,
            concat_axis=2,
            tiled=True,
        )
        return part[0, 0]

    raw_parts = [exchange(raw_ints, 0)]
    coef = pno_coef.reshape(side_count, pno_count, dom_count)
    blocks = [None] * group
    packed = pack(own_orbs, place, coef, group, capacity, tuple(range(inner, group)))
    own = (region * orb_count + me).astype(jnp.uint32)
    own_offset = lax.dynamic_slice_in_dim(fit_offset, own, 1)[0]
    first_row = (fit_rows - own_offset).astype(jnp.uint32)
    later, *packed = lax.optimization_barrier((raw_ints, *packed))
    for m in range(inner, group):
        blocks[m] = across(packed[m - inner], m)
    pairs = [(i, i ^ inner) for i in range(orb_count) if i // inner in (0, 3)]
    guard = lax.ppermute(packed[0][:1], "orb", pairs)
    twice = jnp.concatenate([fit_inverse[0], fit_inverse[0]])
    turned = lax.dynamic_slice_in_dim(twice, first_row, fit_rows)
    raw_parts.append(exchange(later, 1))
    packed = pack(own_orbs, place, coef, group, capacity, tuple(range(inner)))
    blocks[0] = packed[0]
    for m in range(1, inner):
        blocks[m] = across(packed[m], m)
    raw_parts.append(exchange(later, 1))
    mate_orbs = across(own_orbs, inner)
    orb_total = occ_energy.shape[0]

    def pick(values, chosen):
        selector = (region * orb_count + chosen)[:, None] == jnp.arange(orb_total, dtype=jnp.int32)
        return jnp.sum(jnp.where(selector, values[None, :], 0), axis=1)

    spans = chunk_spans(fit_rows)
    reverse = group + inner
    fitted, mirrored = [], [[None] * 2 for _ in spans]

    def mirror(c, k):
        begin, size = spans[c]
        mirrored[c][k] = across(fitted[k][begin : begin + size], reverse)

    for k in range(2):
        product = jnp.dot(turned, raw_parts[k], preferred_element_type=jnp.float32)
        fitted.append(product.astype(jnp.bfloat16))
        mirror(0, k)
        mirror(1, k)
        mirror(2, k)
    for k in range(2):
        mirror(3, k)

    energies, levels, named, fitted[1] = lax.optimization_barrier(
        (occ_energy, pno_energy, own_orbs, fitted[1])
    )
    occupied = pick(energies, named).reshape(pair_count, 2)
    denominator = (
        levels[:, 0, :, None]
        + levels[:, 1, None, :]
        - occupied[:, 0, None, None]
        - occupied[:, 1, None, None]
    )

    def hop(outs):
        return [outs[0]] + [across(outs[i], i) for i in range(1, inner)]

    def project_far(c, tokens):
        parts = project(blocks, 1, mirrored[c], tokens, c > 1)
        return hop(parts) if c < 2 else [parts[0]] + [across(parts[m], m) for m in range(1, group)]

    def pass_on(c, before, tokens):
        sent, here = relay(rows, offsets, before, near, far[c], spans[c], margin, tokens)
        return across(sent, inner), here

    near = project(blocks, 0, fitted, [denominator, guard], False)
    last = spans[2][0]
    straight = [across(near[i][capacity:, :, last:], i + inner) for i in range(inner)]
    near = hop(near)
    far, others = [None] * 4, [None] * 2
    far[0] = project_far(0, [])
    mate_orbs, far[0][0] = lax.optimization_barrier((mate_orbs, far[0][0]))
    orbs = jnp.stack([own_orbs, mate_orbs])
    differs = orbs ^ me
    other_half = (differs & group) != 0
    line = jnp.where(other_half, inner, 0) + (differs & (inner - 1))
    home = jnp.arange(2, dtype=jnp.int32)[:, None]
    position = slots_of(orbs)
    there = ((differs & inner) != 0) != other_half
    rows = jnp.where(there, -1, line * 2 * capacity + home * capacity + position)
    rows_home = jnp.where(there, -1, line * capacity + position)
    place_of = (differs[0] ^ jnp.where(other_half[0], reverse, 0)) + jnp.where(
        other_half[0], group, 0
    )
    rows_all = place_of * capacity + position[0]
    offsets = pick(fit_offset, orbs.reshape(2 * side_count)).reshape(2, side_count)
    others[0], here = pass_on(0, jnp.zeros((8, 128), jnp.float32), [])
    far[1] = project_far(1, [here])
    others[1], here = pass_on(1, here, [])
    there = across(here[1], inner)
    far[2] = project_far(2, [here])
    far[3] = project_far(3, [far[2][0]])
    body = mixed(rows_home, offsets, near, far[0] + far[1], others, spans[:2], margin, [far[3][0]])
    amplitude, energy = finish(
        rows_all,
        [here, there, body, denominator],
        near,
        straight,
        far[2] + far[3],
        tuple(size for _, size in spans[2:]),
    )
    return amplitude, energy


def solution(mesh):
    return jax.shard_map(
        on_device,
        mesh=mesh,
        in_specs=(
            P(None, "orb", "aux", None),
            P(("aux", "orb"), None, None),
            P(("aux", "orb"), None),
            P(("aux", "orb"), None, None, None),
            P(("aux", "orb"), None, None),
            P(),
            P(),
        ),
        out_specs=(P(("aux", "orb"), None), P(("aux", "orb"))),
        check_vma=False,
    )
```

```python
import functools

import jax
import jax.numpy as jnp
from jax import lax
from jax.experimental import pallas as pl
from jax.experimental.pallas import tpu as pltpu
from jax.sharding import PartitionSpec as P

SMEM = pl.BlockSpec(memory_space=pltpu.SMEM)
VMEM = pl.BlockSpec(memory_space=pltpu.VMEM)
ANY = pl.BlockSpec(memory_space=pl.ANY)


def copy(source, target, sem):
    return pltpu.make_async_copy(source, target, sem)


def pack_kernel(group, capacity, masks, orbs, place, coef, *refs):
    outs, (held, count, holder, load_sem, store_sem) = refs[:-5], refs[-5:]
    load = copy(coef, held, load_sem)
    load.start()

    def clear(i, carry):
        holder[i] = 0
        return carry

    def clear_count(i, carry):
        count[i] = 0
        return carry

    def assign(s, carry):
        orb = orbs[s]
        at = count[orb]
        holder[orb * capacity + at] = s
        count[orb] = at + 1
        return carry

    lax.fori_loop(0, 2 * group * capacity, clear, 0)
    lax.fori_loop(0, 2 * group, clear_count, 0)
    lax.fori_loop(0, held.shape[0], assign, 0)
    load.wait()
    for at, (mask, out) in enumerate(zip(masks, outs)):
        for kind in range(2):
            orb = place[1] ^ mask ^ (kind * (group + group // 2))

            def send(k, carry, orb=orb, kind=kind, out=out, sem=store_sem.at[at]):
                copy(held.at[holder[orb * capacity + k]], out.at[kind * capacity + k], sem).start()
                return carry

            lax.fori_loop(0, capacity, send, 0)
    for at, out in enumerate(outs):
        copy(held.at[pl.ds(0, 2 * capacity)], out, store_sem.at[at]).wait()


def pack(orbs, place, coef, group, capacity, masks):
    side_count, pno_count, dom_count = coef.shape
    block = jax.ShapeDtypeStruct((2 * capacity, pno_count, dom_count), coef.dtype)
    return pl.pallas_call(
        functools.partial(pack_kernel, group, capacity, masks),
        out_shape=(block,) * len(masks),
        in_specs=[SMEM, SMEM, ANY],
        out_specs=(ANY,) * len(masks),
        scratch_shapes=[
            pltpu.VMEM(coef.shape, coef.dtype),
            pltpu.SMEM((2 * group,), jnp.int32),
            pltpu.SMEM((2 * group * capacity,), jnp.int32),
            pltpu.SemaphoreType.DMA,
            pltpu.SemaphoreType.DMA((len(masks),)),
        ],
        cost_estimate=pl.CostEstimate(
            flops=0, transcendentals=0, bytes_accessed=6 * side_count * pno_count * dom_count
        ),
    )(orbs, place, coef)


def project_kernel(group, capacity, direct, *refs):
    inner = group // 2
    blocks, parts, outs = refs[:group], refs[group : group + 2], refs[group + 2 :]
    row_count, cut = parts[0].shape
    dom_count = cut + parts[1].shape[1]
    columns = (slice(0, cut), slice(cut, dom_count))
    pno_count = outs[0].shape[1]
    step = row_count if row_count <= 640 else 256

    def tile(t, carry):
        at = t * step if isinstance(t, int) else pl.multiple_of(t * step, step)
        rows = [part[pl.ds(at, step), :] for part in parts]
        for i in range(inner):
            for j in range(2):
                lines = blocks[i + j * inner][...].reshape(capacity * pno_count, dom_count)
                product = sum(
                    lax.dot_general(
                        lines[:, columns[k]],
                        rows[k],
                        (((1,), (1,)), ((), ())),
                        preferred_element_type=jnp.float32,
                    )
                    for k in range(2)
                )
                out, first = (outs[i + j * inner], 0) if direct else (outs[i], j * capacity)
                out[first : first + capacity, :, pl.ds(at, step)] = product.astype(
                    out.dtype
                ).reshape(capacity, pno_count, step)
        return carry

    if row_count == step:
        tile(0, 0)
    else:
        lax.fori_loop(0, row_count // step, tile, 0)


def project(blocks, kind, parts, tokens, direct):
    group = len(blocks)
    inner = group // 2
    slots, pno_count, dom_count = blocks[0].shape
    capacity = slots // 2
    row_count = parts[0].shape[0]
    count, lines = (group, capacity) if direct else (inner, slots)

    def kernel(*refs):
        project_kernel(group, capacity, direct, *refs[: group + 2], *refs[-count:])

    block = pl.BlockSpec((capacity, pno_count, dom_count), lambda i: (kind, 0, 0))
    rows = [pl.BlockSpec(part.shape, lambda i: (0, 0)) for part in parts]
    return pl.pallas_call(
        kernel,
        grid=(1,),
        out_shape=(jax.ShapeDtypeStruct((lines, pno_count, row_count), blocks[0].dtype),) * count,
        in_specs=[block] * group + rows + [ANY] * len(tokens),
        out_specs=(pl.BlockSpec((lines, pno_count, row_count), lambda i: (0, 0, 0)),) * count,
        compiler_params=pltpu.CompilerParams(vmem_limit_bytes=32 << 20),
        cost_estimate=pl.CostEstimate(
            flops=2 * group * capacity * pno_count * dom_count * row_count,
            transcendentals=0,
            bytes_accessed=2 * group * capacity * pno_count * dom_count,
        ),
    )(*blocks, *parts, *tokens)


def gather_sides(near, far, spans, slots, held, sem):
    inner = len(near)
    low, width = spans[0][0], sum(size for _, size in spans)
    for i in range(inner):
        copy(
            near[i].at[pl.ds(0, slots), :, pl.ds(low, width)],
            held.at[pl.ds(i * slots, slots)],
            sem,
        ).start()
        for c, (begin, size) in enumerate(spans):
            copy(
                far[c * inner + i].at[pl.ds(0, slots)],
                held.at[pl.ds((inner + i) * slots, slots), :, pl.ds(begin - low, size)],
                sem,
            ).start()


def overlap(first, second, limits, low):
    if low < limits[2]:
        lane = lax.broadcasted_iota(jnp.int32, (1, second.shape[1]), 1) + low
        apart = (lane < limits[0]) != (lane < limits[1])
        second = second * jnp.where(apart, 0.0, 1.0).astype(second.dtype)
    return lax.dot_general(
        first, second, (((1,), (1,)), ((), ())), preferred_element_type=jnp.float32
    )


def relay_kernel(inner, spans, margin, rows, offsets, before, *refs):
    near, far = refs[:inner], refs[inner : 2 * inner]
    sent, coupling, held, sem = refs[-4:]
    low = spans[0][0]
    pair_count = sent.shape[0]
    gather_sides(near, far, spans, near[0].shape[0], held, sem)
    copy(held, held, sem).wait()

    def choose(n, carry):
        sent[n] = held[jnp.maximum(jnp.maximum(rows[1, 2 * n], rows[1, 2 * n + 1]), 0)]
        return carry

    lax.fori_loop(0, pair_count, choose, 0, unroll=4)
    for h in range(2):

        def one_pair(n, carry, h=h):
            first, second = rows[h, 2 * n], rows[h, 2 * n + 1]
            product = overlap(
                held[jnp.maximum(first, 0)],
                held[jnp.maximum(second, 0)],
                (offsets[h, 2 * n], offsets[h, 2 * n + 1], margin),
                low,
            )
            product = jnp.where((first >= 0) & (second >= 0), product, 0.0)
            coupling[h, n] = product if low == 0 else product + before[h, n]
            return carry

        lax.fori_loop(0, pair_count, one_pair, 0, unroll=4)


def relay(rows, offsets, before, near, far, span, margin, tokens):
    inner = len(near)
    slots, pno_count, _ = near[0].shape
    pair_count = rows.shape[1] // 2
    return pl.pallas_call(
        functools.partial(relay_kernel, inner, (span,), margin),
        out_shape=(
            jax.ShapeDtypeStruct((pair_count, pno_count, span[1]), near[0].dtype),
            jax.ShapeDtypeStruct((2, pair_count, pno_count, pno_count), jnp.float32),
        ),
        in_specs=[SMEM, SMEM, VMEM] + [ANY] * (len(near) + len(far) + len(tokens)),
        out_specs=(VMEM, VMEM),
        scratch_shapes=[
            pltpu.VMEM((2 * inner * slots, pno_count, span[1]), near[0].dtype),
            pltpu.SemaphoreType.DMA,
        ],
        compiler_params=pltpu.CompilerParams(vmem_limit_bytes=24 << 20),
    )(rows, offsets, before, *near, *far, *tokens)


def mixed_pairs(inner, spans, margin, rows, offsets, near, far, others, held, sem, write):
    low = spans[0][0]
    slots = near[0].shape[0] // 2
    pair_count = others[0].shape[0]
    at = 2 * inner * slots
    gather_sides(near, far, spans, slots, held, sem)
    for other, (begin, size) in zip(others, spans):
        copy(
            other, held.at[pl.ds(at, pair_count), :, pl.ds(begin - low, size)], sem
        ).start()
    copy(held, held, sem).wait()

    def one_pair(n, carry):
        first, second = rows[0, 2 * n], rows[0, 2 * n + 1]
        product = overlap(
            held[jnp.where(first >= 0, first, at + n)],
            held[jnp.where(second >= 0, second, at + n)],
            (offsets[0, 2 * n], offsets[0, 2 * n + 1], margin),
            low,
        )
        write(n, jnp.where((first >= 0) != (second >= 0), product, 0.0))
        return carry

    lax.fori_loop(0, pair_count, one_pair, 0, unroll=4)


def mixed_kernel(inner, spans, margin, rows, offsets, *refs):
    near, refs = refs[:inner], refs[inner:]
    far, refs = refs[: inner * len(spans)], refs[inner * len(spans) :]
    others = refs[: len(spans)]
    coupling, held, sem = refs[-3:]

    def write(n, product):
        coupling[n] = product

    mixed_pairs(inner, spans, margin, rows, offsets, near, far, others, held, sem, write)


def finish_kernel(group, sizes, rows, here, there, before, denominator, *refs):
    inner = group // 2
    near, straight, far = refs[:inner], refs[inner:group], refs[group : group + group * len(sizes)]
    amplitude, energy, coupling, held, sem = refs[-5:]
    capacity, _, width = straight[0].shape
    low = near[0].shape[2] - width
    for m in range(group):
        source = straight[m - inner]
        if m < inner:
            source = near[m].at[pl.ds(0, capacity), :, pl.ds(low, width)]
        copy(source, held.at[pl.ds(m * capacity, capacity)], sem).start()
        at = 0
        for c, size in enumerate(sizes):
            copy(
                far[c * group + m],
                held.at[pl.ds((group + m) * capacity, capacity), :, pl.ds(at, size)],
                sem,
            ).start()
            at += size
    copy(held, held, sem).wait()

    def one_pair(n, carry):
        coupling[n] = lax.dot_general(
            held[rows[2 * n]],
            held[rows[2 * n + 1]],
            (((1,), (1,)), ((), ())),
            preferred_element_type=jnp.float32,
        )
        return carry

    lax.fori_loop(0, coupling.shape[0], one_pair, 0, unroll=4)
    total = coupling[...] + before[...] + here[0] + there[...]
    result = -total / denominator[...]
    count = result.shape[1]
    for p in range(count):
        amplitude[:, p * count : (p + 1) * count] = result[:, p, :]
    parts = total * (2.0 * result - jnp.swapaxes(result, 1, 2))
    energy[...] = jnp.sum(jnp.sum(parts, axis=1), axis=1)


def finish(rows, finals, near, straight, far, sizes):
    group = 2 * len(near)
    capacity, pno_count, width = straight[0].shape
    pair_count = rows.shape[0] // 2
    square = jax.ShapeDtypeStruct((pair_count, pno_count, pno_count), jnp.float32)
    return pl.pallas_call(
        functools.partial(finish_kernel, group, sizes),
        out_shape=(
            jax.ShapeDtypeStruct((pair_count, pno_count * pno_count), jnp.float32),
            jax.ShapeDtypeStruct((pair_count,), jnp.float32),
        ),
        in_specs=[SMEM] + [VMEM] * len(finals) + [ANY] * (len(near) + len(straight) + len(far)),
        out_specs=(VMEM, VMEM),
        scratch_shapes=[
            pltpu.VMEM(square.shape, jnp.float32),
            pltpu.VMEM((2 * group * capacity, pno_count, width), near[0].dtype),
            pltpu.SemaphoreType.DMA,
        ],
        compiler_params=pltpu.CompilerParams(vmem_limit_bytes=24 << 20),
        name="finish",
    )(rows, *finals, *near, *straight, *far)


def mixed(rows, offsets, near, far, others, spans, margin, tokens):
    inner = len(near)
    slots, pno_count, _ = near[0].shape
    pair_count = rows.shape[1] // 2
    width = sum(size for _, size in spans)
    return pl.pallas_call(
        functools.partial(mixed_kernel, inner, tuple(spans), margin),
        out_shape=jax.ShapeDtypeStruct((pair_count, pno_count, pno_count), jnp.float32),
        in_specs=[SMEM] * 2 + [ANY] * (len(near) + len(far) + len(others) + len(tokens)),
        out_specs=VMEM,
        scratch_shapes=[
            pltpu.VMEM((inner * slots + pair_count, pno_count, width), near[0].dtype),
            pltpu.SemaphoreType.DMA,
        ],
        compiler_params=pltpu.CompilerParams(vmem_limit_bytes=24 << 20),
    )(rows, offsets, *near, *far, *others, *tokens)


def slots_of(orbs):
    sequence = jnp.arange(orbs.shape[1], dtype=jnp.int32)
    same = orbs[:, :, None] == orbs[:, None, :]
    earlier = sequence[None, None, :] < sequence[None, :, None]
    return jnp.sum(jnp.where(same & earlier, 1, 0), axis=2).astype(jnp.int32)


def chunk_spans(fit_rows):
    sizes = (fit_rows // 2, fit_rows // 4, fit_rows // 8, fit_rows // 8)
    return [(sum(sizes[:c]), size) for c, size in enumerate(sizes)]


def on_device(raw_ints, fit_inverse, pair_orbs, pno_coef, pno_energy, occ_energy, fit_offset):
    orb_count = lax.axis_size("orb")
    region, me = lax.axis_index("aux"), lax.axis_index("orb")
    group = orb_count // 2
    inner = group // 2
    pair_count = pair_orbs.shape[0]
    pno_count, dom_count = pno_coef.shape[2:]
    side_count = 2 * pair_count
    capacity = max(2, 4 * pair_count // orb_count)
    fit_rows = fit_inverse.shape[1]
    margin = fit_rows // 4

    def across(array, mask):
        return lax.ppermute(array, "orb", [(i, i ^ mask) for i in range(orb_count)])

    own_orbs = pair_orbs.reshape(side_count)
    place = jnp.stack([region, me]).astype(jnp.int32)
    cuts = (0, 7 * dom_count // 12 // 128 * 128, dom_count)

    def exchange(array, k):
        part = lax.all_to_all(
            array[:, :, :, cuts[k] : cuts[k + 1]],
            "aux",
            split_axis=0,
            concat_axis=2,
            tiled=True,
        )
        return part[0, 0]

    raw_parts = [exchange(raw_ints, 0)]
    coef = pno_coef.reshape(side_count, pno_count, dom_count)
    blocks = [None] * group
    packed = pack(own_orbs, place, coef, group, capacity, tuple(range(inner, group)))
    own = (region * orb_count + me).astype(jnp.uint32)
    own_offset = lax.dynamic_slice_in_dim(fit_offset, own, 1)[0]
    first_row = (fit_rows - own_offset).astype(jnp.uint32)
    later, *packed = lax.optimization_barrier((raw_ints, *packed))
    for m in range(inner, group):
        blocks[m] = across(packed[m - inner], m)
    pairs = [(i, i ^ inner) for i in range(orb_count) if i // inner in (0, 3)]
    guard = lax.ppermute(packed[0][:1], "orb", pairs)
    twice = jnp.concatenate([fit_inverse[0], fit_inverse[0]])
    turned = lax.dynamic_slice_in_dim(twice, first_row, fit_rows)
    raw_parts.append(exchange(later, 1))
    packed = pack(own_orbs, place, coef, group, capacity, tuple(range(inner)))
    blocks[0] = packed[0]
    for m in range(1, inner):
        blocks[m] = across(packed[m], m)
    raw_parts.append(exchange(later, 1))
    mate_orbs = across(own_orbs, inner)
    orb_total = occ_energy.shape[0]

    def pick(values, chosen):
        selector = (region * orb_count + chosen)[:, None] == jnp.arange(orb_total, dtype=jnp.int32)
        return jnp.sum(jnp.where(selector, values[None, :], 0), axis=1)

    spans = chunk_spans(fit_rows)
    reverse = group + inner
    fitted, mirrored = [], [[None] * 2 for _ in spans]

    def mirror(c, k):
        begin, size = spans[c]
        mirrored[c][k] = across(fitted[k][begin : begin + size], reverse)

    for k in range(2):
        product = jnp.dot(turned, raw_parts[k], preferred_element_type=jnp.float32)
        fitted.append(product.astype(jnp.bfloat16))
        mirror(0, k)
        mirror(1, k)
        mirror(2, k)
    for k in range(2):
        mirror(3, k)

    energies, levels, named, fitted[1] = lax.optimization_barrier(
        (occ_energy, pno_energy, own_orbs, fitted[1])
    )
    occupied = pick(energies, named).reshape(pair_count, 2)
    denominator = (
        levels[:, 0, :, None]
        + levels[:, 1, None, :]
        - occupied[:, 0, None, None]
        - occupied[:, 1, None, None]
    )

    def hop(outs):
        return [outs[0]] + [across(outs[i], i) for i in range(1, inner)]

    def project_far(c, tokens):
        parts = project(blocks, 1, mirrored[c], tokens, c > 1)
        return hop(parts) if c < 2 else [parts[0]] + [across(parts[m], m) for m in range(1, group)]

    def pass_on(c, before, tokens):
        sent, here = relay(rows, offsets, before, near, far[c], spans[c], margin, tokens)
        return across(sent, inner), here

    near = project(blocks, 0, fitted, [denominator, guard], False)
    last = spans[2][0]
    straight = [across(near[i][capacity:, :, last:], i + inner) for i in range(inner)]
    near = hop(near)
    far, others = [None] * 4, [None] * 2
    far[0] = project_far(0, [])
    mate_orbs, far[0][0] = lax.optimization_barrier((mate_orbs, far[0][0]))
    orbs = jnp.stack([own_orbs, mate_orbs])
    differs = orbs ^ me
    other_half = (differs & group) != 0
    line = jnp.where(other_half, inner, 0) + (differs & (inner - 1))
    home = jnp.arange(2, dtype=jnp.int32)[:, None]
    position = slots_of(orbs)
    there = ((differs & inner) != 0) != other_half
    rows = jnp.where(there, -1, line * 2 * capacity + home * capacity + position)
    rows_home = jnp.where(there, -1, line * capacity + position)
    place_of = (differs[0] ^ jnp.where(other_half[0], reverse, 0)) + jnp.where(
        other_half[0], group, 0
    )
    rows_all = place_of * capacity + position[0]
    offsets = pick(fit_offset, orbs.reshape(2 * side_count)).reshape(2, side_count)
    others[0], here = pass_on(0, jnp.zeros((8, 128), jnp.float32), [])
    far[1] = project_far(1, [here])
    others[1], here = pass_on(1, here, [])
    there = across(here[1], inner)
    far[2] = project_far(2, [here])
    far[3] = project_far(3, [far[2][0]])
    body = mixed(rows_home, offsets, near, far[0] + far[1], others, spans[:2], margin, [far[3][0]])
    amplitude, energy = finish(
        rows_all,
        [here, there, body, denominator],
        near,
        straight,
        far[2] + far[3],
        tuple(size for _, size in spans[2:]),
    )
    return amplitude, energy


def solution(mesh):
    return jax.shard_map(
        on_device,
        mesh=mesh,
        in_specs=(
            P(None, "orb", "aux", None),
            P(("aux", "orb"), None, None),
            P(("aux", "orb"), None),
            P(("aux", "orb"), None, None, None),
            P(("aux", "orb"), None, None),
            P(),
            P(),
        ),
        out_specs=(P(("aux", "orb"), None), P(("aux", "orb"))),
        check_vma=False,
    )
```

```python
import functools

import jax
import jax.numpy as jnp
from jax import lax
from jax.experimental import pallas as pl
from jax.experimental.pallas import tpu as pltpu
from jax.sharding import PartitionSpec as P

SMEM = pl.BlockSpec(memory_space=pltpu.SMEM)
VMEM = pl.BlockSpec(memory_space=pltpu.VMEM)
ANY = pl.BlockSpec(memory_space=pl.ANY)


def copy(source, target, sem):
    return pltpu.make_async_copy(source, target, sem)


def pack_kernel(group, capacity, masks, orbs, place, coef, *refs):
    outs, (held, count, holder, load_sem, store_sem) = refs[:-5], refs[-5:]
    load = copy(coef, held, load_sem)
    load.start()

    def clear(i, carry):
        holder[i] = 0
        return carry

    def clear_count(i, carry):
        count[i] = 0
        return carry

    def assign(s, carry):
        orb = orbs[s]
        at = count[orb]
        holder[orb * capacity + at] = s
        count[orb] = at + 1
        return carry

    lax.fori_loop(0, 2 * group * capacity, clear, 0)
    lax.fori_loop(0, 2 * group, clear_count, 0)
    lax.fori_loop(0, held.shape[0], assign, 0)
    load.wait()
    for at, (mask, out) in enumerate(zip(masks, outs)):
        for kind in range(2):
            orb = place[1] ^ mask ^ (kind * (group + group // 2))

            def send(k, carry, orb=orb, kind=kind, out=out, sem=store_sem.at[at]):
                copy(held.at[holder[orb * capacity + k]], out.at[kind * capacity + k], sem).start()
                return carry

            lax.fori_loop(0, capacity, send, 0)
    for at, out in enumerate(outs):
        copy(held.at[pl.ds(0, 2 * capacity)], out, store_sem.at[at]).wait()


def pack(orbs, place, coef, group, capacity, masks):
    side_count, pno_count, dom_count = coef.shape
    block = jax.ShapeDtypeStruct((2 * capacity, pno_count, dom_count), coef.dtype)
    return pl.pallas_call(
        functools.partial(pack_kernel, group, capacity, masks),
        out_shape=(block,) * len(masks),
        in_specs=[SMEM, SMEM, ANY],
        out_specs=(ANY,) * len(masks),
        scratch_shapes=[
            pltpu.VMEM(coef.shape, coef.dtype),
            pltpu.SMEM((2 * group,), jnp.int32),
            pltpu.SMEM((2 * group * capacity,), jnp.int32),
            pltpu.SemaphoreType.DMA,
            pltpu.SemaphoreType.DMA((len(masks),)),
        ],
        cost_estimate=pl.CostEstimate(
            flops=0, transcendentals=0, bytes_accessed=6 * side_count * pno_count * dom_count
        ),
    )(orbs, place, coef)


def project_kernel(group, capacity, direct, *refs):
    inner = group // 2
    blocks, parts, outs = refs[:group], refs[group : group + 2], refs[group + 2 :]
    row_count, half = parts[0].shape
    pno_count = outs[0].shape[1]
    step = row_count if row_count <= 640 else 256

    def tile(t, carry):
        at = t * step if isinstance(t, int) else pl.multiple_of(t * step, step)
        rows = [part[pl.ds(at, step), :] for part in parts]
        for i in range(inner):
            for j in range(2):
                lines = blocks[i + j * inner][...].reshape(capacity * pno_count, 2 * half)
                product = sum(
                    lax.dot_general(
                        lines[:, k * half : (k + 1) * half],
                        rows[k],
                        (((1,), (1,)), ((), ())),
                        preferred_element_type=jnp.float32,
                    )
                    for k in range(2)
                )
                out, first = (outs[i + j * inner], 0) if direct else (outs[i], j * capacity)
                out[first : first + capacity, :, pl.ds(at, step)] = product.astype(
                    out.dtype
                ).reshape(capacity, pno_count, step)
        return carry

    if row_count == step:
        tile(0, 0)
    else:
        lax.fori_loop(0, row_count // step, tile, 0)


def project(blocks, kind, parts, tokens, direct):
    group = len(blocks)
    inner = group // 2
    slots, pno_count, dom_count = blocks[0].shape
    capacity = slots // 2
    row_count = parts[0].shape[0]
    count, lines = (group, capacity) if direct else (inner, slots)

    def kernel(*refs):
        project_kernel(group, capacity, direct, *refs[: group + 2], *refs[-count:])

    block = pl.BlockSpec((capacity, pno_count, dom_count), lambda i: (kind, 0, 0))
    part = pl.BlockSpec(parts[0].shape, lambda i: (0, 0))
    return pl.pallas_call(
        kernel,
        grid=(1,),
        out_shape=(jax.ShapeDtypeStruct((lines, pno_count, row_count), blocks[0].dtype),) * count,
        in_specs=[block] * group + [part] * 2 + [ANY] * len(tokens),
        out_specs=(pl.BlockSpec((lines, pno_count, row_count), lambda i: (0, 0, 0)),) * count,
        compiler_params=pltpu.CompilerParams(vmem_limit_bytes=32 << 20),
        cost_estimate=pl.CostEstimate(
            flops=2 * group * capacity * pno_count * dom_count * row_count,
            transcendentals=0,
            bytes_accessed=2 * group * capacity * pno_count * dom_count,
        ),
    )(*blocks, *parts, *tokens)


def gather_sides(near, far, spans, slots, held, sem):
    inner = len(near)
    low, width = spans[0][0], sum(size for _, size in spans)
    for i in range(inner):
        copy(
            near[i].at[pl.ds(0, slots), :, pl.ds(low, width)],
            held.at[pl.ds(i * slots, slots)],
            sem,
        ).start()
        for c, (begin, size) in enumerate(spans):
            copy(
                far[c * inner + i].at[pl.ds(0, slots)],
                held.at[pl.ds((inner + i) * slots, slots), :, pl.ds(begin - low, size)],
                sem,
            ).start()


def overlap(first, second, limits, low):
    if low < limits[2]:
        lane = lax.broadcasted_iota(jnp.int32, (1, second.shape[1]), 1) + low
        apart = (lane < limits[0]) != (lane < limits[1])
        second = second * jnp.where(apart, 0.0, 1.0).astype(second.dtype)
    return lax.dot_general(
        first, second, (((1,), (1,)), ((), ())), preferred_element_type=jnp.float32
    )


def relay_kernel(inner, spans, margin, rows, offsets, before, *refs):
    near, far = refs[:inner], refs[inner : 2 * inner]
    sent, coupling, held, sem = refs[-4:]
    low = spans[0][0]
    pair_count = sent.shape[0]
    gather_sides(near, far, spans, near[0].shape[0], held, sem)
    copy(held, held, sem).wait()

    def choose(n, carry):
        sent[n] = held[jnp.maximum(jnp.maximum(rows[1, 2 * n], rows[1, 2 * n + 1]), 0)]
        return carry

    lax.fori_loop(0, pair_count, choose, 0, unroll=4)
    for h in range(2):

        def one_pair(n, carry, h=h):
            first, second = rows[h, 2 * n], rows[h, 2 * n + 1]
            product = overlap(
                held[jnp.maximum(first, 0)],
                held[jnp.maximum(second, 0)],
                (offsets[h, 2 * n], offsets[h, 2 * n + 1], margin),
                low,
            )
            product = jnp.where((first >= 0) & (second >= 0), product, 0.0)
            coupling[h, n] = product if low == 0 else product + before[h, n]
            return carry

        lax.fori_loop(0, pair_count, one_pair, 0, unroll=4)


def relay(rows, offsets, before, near, far, span, margin, tokens):
    inner = len(near)
    slots, pno_count, _ = near[0].shape
    pair_count = rows.shape[1] // 2
    return pl.pallas_call(
        functools.partial(relay_kernel, inner, (span,), margin),
        out_shape=(
            jax.ShapeDtypeStruct((pair_count, pno_count, span[1]), near[0].dtype),
            jax.ShapeDtypeStruct((2, pair_count, pno_count, pno_count), jnp.float32),
        ),
        in_specs=[SMEM, SMEM, VMEM] + [ANY] * (len(near) + len(far) + len(tokens)),
        out_specs=(VMEM, VMEM),
        scratch_shapes=[
            pltpu.VMEM((2 * inner * slots, pno_count, span[1]), near[0].dtype),
            pltpu.SemaphoreType.DMA,
        ],
        compiler_params=pltpu.CompilerParams(vmem_limit_bytes=24 << 20),
    )(rows, offsets, before, *near, *far, *tokens)


def mixed_pairs(inner, spans, margin, rows, offsets, near, far, others, held, sem, write):
    low = spans[0][0]
    slots = near[0].shape[0] // 2
    pair_count = others[0].shape[0]
    at = 2 * inner * slots
    gather_sides(near, far, spans, slots, held, sem)
    for other, (begin, size) in zip(others, spans):
        copy(
            other, held.at[pl.ds(at, pair_count), :, pl.ds(begin - low, size)], sem
        ).start()
    copy(held, held, sem).wait()

    def one_pair(n, carry):
        first, second = rows[0, 2 * n], rows[0, 2 * n + 1]
        product = overlap(
            held[jnp.where(first >= 0, first, at + n)],
            held[jnp.where(second >= 0, second, at + n)],
            (offsets[0, 2 * n], offsets[0, 2 * n + 1], margin),
            low,
        )
        write(n, jnp.where((first >= 0) != (second >= 0), product, 0.0))
        return carry

    lax.fori_loop(0, pair_count, one_pair, 0, unroll=4)


def mixed_kernel(inner, spans, margin, rows, offsets, *refs):
    near, refs = refs[:inner], refs[inner:]
    far, refs = refs[: inner * len(spans)], refs[inner * len(spans) :]
    others = refs[: len(spans)]
    coupling, held, sem = refs[-3:]

    def write(n, product):
        coupling[n] = product

    mixed_pairs(inner, spans, margin, rows, offsets, near, far, others, held, sem, write)


def finish_kernel(group, sizes, rows, here, there, before, denominator, *refs):
    inner = group // 2
    near, straight, far = refs[:inner], refs[inner:group], refs[group : group + group * len(sizes)]
    amplitude, energy, coupling, held, sem = refs[-5:]
    capacity, _, width = straight[0].shape
    low = near[0].shape[2] - width
    for m in range(group):
        source = straight[m - inner]
        if m < inner:
            source = near[m].at[pl.ds(0, capacity), :, pl.ds(low, width)]
        copy(source, held.at[pl.ds(m * capacity, capacity)], sem).start()
        at = 0
        for c, size in enumerate(sizes):
            copy(
                far[c * group + m],
                held.at[pl.ds((group + m) * capacity, capacity), :, pl.ds(at, size)],
                sem,
            ).start()
            at += size
    copy(held, held, sem).wait()

    def one_pair(n, carry):
        coupling[n] = lax.dot_general(
            held[rows[2 * n]],
            held[rows[2 * n + 1]],
            (((1,), (1,)), ((), ())),
            preferred_element_type=jnp.float32,
        )
        return carry

    lax.fori_loop(0, coupling.shape[0], one_pair, 0, unroll=4)
    total = coupling[...] + before[...] + here[0] + there[...]
    result = -total / denominator[...]
    count = result.shape[1]
    for p in range(count):
        amplitude[:, p * count : (p + 1) * count] = result[:, p, :]
    parts = total * (2.0 * result - jnp.swapaxes(result, 1, 2))
    energy[...] = jnp.sum(jnp.sum(parts, axis=1), axis=1)


def finish(rows, finals, near, straight, far, sizes):
    group = 2 * len(near)
    capacity, pno_count, width = straight[0].shape
    pair_count = rows.shape[0] // 2
    square = jax.ShapeDtypeStruct((pair_count, pno_count, pno_count), jnp.float32)
    return pl.pallas_call(
        functools.partial(finish_kernel, group, sizes),
        out_shape=(
            jax.ShapeDtypeStruct((pair_count, pno_count * pno_count), jnp.float32),
            jax.ShapeDtypeStruct((pair_count,), jnp.float32),
        ),
        in_specs=[SMEM] + [VMEM] * len(finals) + [ANY] * (len(near) + len(straight) + len(far)),
        out_specs=(VMEM, VMEM),
        scratch_shapes=[
            pltpu.VMEM(square.shape, jnp.float32),
            pltpu.VMEM((2 * group * capacity, pno_count, width), near[0].dtype),
            pltpu.SemaphoreType.DMA,
        ],
        compiler_params=pltpu.CompilerParams(vmem_limit_bytes=24 << 20),
        name="finish",
    )(rows, *finals, *near, *straight, *far)


def mixed(rows, offsets, near, far, others, spans, margin, tokens):
    inner = len(near)
    slots, pno_count, _ = near[0].shape
    pair_count = rows.shape[1] // 2
    width = sum(size for _, size in spans)
    return pl.pallas_call(
        functools.partial(mixed_kernel, inner, tuple(spans), margin),
        out_shape=jax.ShapeDtypeStruct((pair_count, pno_count, pno_count), jnp.float32),
        in_specs=[SMEM] * 2 + [ANY] * (len(near) + len(far) + len(others) + len(tokens)),
        out_specs=VMEM,
        scratch_shapes=[
            pltpu.VMEM((inner * slots + pair_count, pno_count, width), near[0].dtype),
            pltpu.SemaphoreType.DMA,
        ],
        compiler_params=pltpu.CompilerParams(vmem_limit_bytes=24 << 20),
    )(rows, offsets, *near, *far, *others, *tokens)


def slots_of(orbs):
    sequence = jnp.arange(orbs.shape[1], dtype=jnp.int32)
    same = orbs[:, :, None] == orbs[:, None, :]
    earlier = sequence[None, None, :] < sequence[None, :, None]
    return jnp.sum(jnp.where(same & earlier, 1, 0), axis=2).astype(jnp.int32)


def chunk_spans(fit_rows):
    sizes = (fit_rows // 2, fit_rows // 8, fit_rows // 4, fit_rows // 8)
    return [(sum(sizes[:c]), size) for c, size in enumerate(sizes)]


def on_device(raw_ints, fit_inverse, pair_orbs, pno_coef, pno_energy, occ_energy, fit_offset):
    orb_count = lax.axis_size("orb")
    region, me = lax.axis_index("aux"), lax.axis_index("orb")
    group = orb_count // 2
    inner = group // 2
    pair_count = pair_orbs.shape[0]
    pno_count, dom_count = pno_coef.shape[2:]
    side_count = 2 * pair_count
    capacity = max(2, 4 * pair_count // orb_count)
    fit_rows = fit_inverse.shape[1]
    margin = fit_rows // 4

    def across(array, mask):
        return lax.ppermute(array, "orb", [(i, i ^ mask) for i in range(orb_count)])

    own_orbs = pair_orbs.reshape(side_count)
    place = jnp.stack([region, me]).astype(jnp.int32)
    half = dom_count // 2

    def exchange(array, k):
        part = lax.all_to_all(
            array[:, :, :, k * half : (k + 1) * half],
            "aux",
            split_axis=0,
            concat_axis=2,
            tiled=True,
        )
        return part[0, 0]

    raw_parts = [exchange(raw_ints, 0)]
    coef = pno_coef.reshape(side_count, pno_count, dom_count)
    blocks = [None] * group
    packed = pack(own_orbs, place, coef, group, capacity, tuple(range(inner, group)))
    own = (region * orb_count + me).astype(jnp.uint32)
    own_offset = lax.dynamic_slice_in_dim(fit_offset, own, 1)[0]
    first_row = (fit_rows - own_offset).astype(jnp.uint32)
    later, *packed = lax.optimization_barrier((raw_ints, *packed))
    for m in range(inner, group):
        blocks[m] = across(packed[m - inner], m)
    pairs = [(i, i ^ inner) for i in range(orb_count) if i // inner in (0, 3)]
    guard = lax.ppermute(packed[0][:1], "orb", pairs)
    twice = jnp.concatenate([fit_inverse[0], fit_inverse[0]])
    turned = lax.dynamic_slice_in_dim(twice, first_row, fit_rows)
    raw_parts.append(exchange(later, 1))
    packed = pack(own_orbs, place, coef, group, capacity, tuple(range(inner)))
    blocks[0] = packed[0]
    for m in range(1, inner):
        blocks[m] = across(packed[m], m)
    raw_parts.append(exchange(later, 1))
    mate_orbs = across(own_orbs, inner)
    orb_total = occ_energy.shape[0]

    def pick(values, chosen):
        selector = (region * orb_count + chosen)[:, None] == jnp.arange(orb_total, dtype=jnp.int32)
        return jnp.sum(jnp.where(selector, values[None, :], 0), axis=1)

    spans = chunk_spans(fit_rows)
    reverse = group + inner
    fitted, mirrored = [], [[None] * 2 for _ in spans]

    def mirror(c, k):
        begin, size = spans[c]
        mirrored[c][k] = across(fitted[k][begin : begin + size], reverse)

    for k in range(2):
        product = jnp.dot(turned, raw_parts[k], preferred_element_type=jnp.float32)
        fitted.append(product.astype(jnp.bfloat16))
        mirror(0, k)
    fitted = list(lax.optimization_barrier(tuple(fitted)))
    for c in range(1, len(spans)):
        mirror(c, 0)
        mirror(c, 1)

    energies, levels, named, fitted[1] = lax.optimization_barrier(
        (occ_energy, pno_energy, own_orbs, fitted[1])
    )
    occupied = pick(energies, named).reshape(pair_count, 2)
    denominator = (
        levels[:, 0, :, None]
        + levels[:, 1, None, :]
        - occupied[:, 0, None, None]
        - occupied[:, 1, None, None]
    )

    def hop(outs):
        return [outs[0]] + [across(outs[i], i) for i in range(1, inner)]

    def project_far(c, tokens):
        parts = project(blocks, 1, mirrored[c], tokens, c > 1)
        return hop(parts) if c < 2 else [parts[0]] + [across(parts[m], m) for m in range(1, group)]

    def pass_on(c, before, tokens):
        sent, here = relay(rows, offsets, before, near, far[c], spans[c], margin, tokens)
        return across(sent, inner), here

    near = project(blocks, 0, fitted, [denominator, guard], False)
    last = spans[2][0]
    straight = [across(near[i][capacity:, :, last:], i + inner) for i in range(inner)]
    near = hop(near)
    far, others = [None] * 4, [None] * 2
    far[0] = project_far(0, [])
    mate_orbs, far[0][0] = lax.optimization_barrier((mate_orbs, far[0][0]))
    orbs = jnp.stack([own_orbs, mate_orbs])
    differs = orbs ^ me
    other_half = (differs & group) != 0
    line = jnp.where(other_half, inner, 0) + (differs & (inner - 1))
    home = jnp.arange(2, dtype=jnp.int32)[:, None]
    position = slots_of(orbs)
    there = ((differs & inner) != 0) != other_half
    rows = jnp.where(there, -1, line * 2 * capacity + home * capacity + position)
    rows_home = jnp.where(there, -1, line * capacity + position)
    place_of = (differs[0] ^ jnp.where(other_half[0], reverse, 0)) + jnp.where(
        other_half[0], group, 0
    )
    rows_all = place_of * capacity + position[0]
    offsets = pick(fit_offset, orbs.reshape(2 * side_count)).reshape(2, side_count)
    others[0], here = pass_on(0, jnp.zeros((8, 128), jnp.float32), [])
    far[1] = project_far(1, [here])
    others[1], here = pass_on(1, here, [])
    there = across(here[1], inner)
    far[2] = project_far(2, [here])
    far[3] = project_far(3, [far[2][0]])
    body = mixed(rows_home, offsets, near, far[0] + far[1], others, spans[:2], margin, [far[3][0]])
    amplitude, energy = finish(
        rows_all,
        [here, there, body, denominator],
        near,
        straight,
        far[2] + far[3],
        tuple(size for _, size in spans[2:]),
    )
    return amplitude, energy


def solution(mesh):
    return jax.shard_map(
        on_device,
        mesh=mesh,
        in_specs=(
            P(None, "orb", "aux", None),
            P(("aux", "orb"), None, None),
            P(("aux", "orb"), None),
            P(("aux", "orb"), None, None, None),
            P(("aux", "orb"), None, None),
            P(),
            P(),
        ),
        out_specs=(P(("aux", "orb"), None), P(("aux", "orb"))),
        check_vma=False,
    )
```
